32 devices in a mesh: dp: 8 (over z, x), shard: 4 (over y, core).
Axes of the slice: x: 2, y: 2, z: 4, core: 2. Of those that a mesh axis runs over, the one named last changes fastest.
Arguments:
- tokens: bfloat16 [8192, 2048], P('dp'), may hold values from -6 to 6
- block_ids: int32 [8, 1024], P('dp'), may hold values from 0 to 7, never falling along the last dimension, each value on 1 to 256 neighbouring positions
- cotangent: bfloat16 [8192, 2048], P('dp'), may hold values from -12 to 12
- gain_first: float32 [2048], P('dp'), may hold values from 0.3 to 2.5
- w_query: float32 [2048, 2048], P('dp', 'shard'), may hold values from -0.125 to 0.125
- w_key: float32 [2048, 512], P('dp', 'shard'), may hold values from -0.125 to 0.125
- w_value: float32 [2048, 512], P('dp', 'shard'), may hold values from -0.125 to 0.125
- w_output: float32 [2048, 2048], P('shard', 'dp'), may hold values from -2 to 2
- gain_second: float32 [2048], P('dp'), may hold values from 0.3 to 2.5
- w_gate: float32 [2048, 8192], P('dp', 'shard'), may hold values from -0.125 to 0.125
- w_up: float32 [2048, 8192], P('dp', 'shard'), may hold values from -0.125 to 0.125
- w_down: float32 [8192, 2048], P('shard', 'dp'), may hold values from -0.0625 to 0.0625
- moment_first: float32 [2048], P('dp'), may hold values from -6 to 6
- moment_query: float32 [2048, 2048], P('dp', 'shard'), may hold values from -4 to 4
- moment_key: float32 [2048, 512], P('dp', 'shard'), may hold values from -4 to 4
- moment_value: float32 [2048, 512], P('dp', 'shard'), may hold values from -4 to 4
- moment_output: float32 [2048, 2048], P('shard', 'dp'), may hold values from -4 to 4
- moment_second: float32 [2048], P('dp'), may hold values from -6 to 6
- moment_gate: float32 [2048, 8192], P('dp', 'shard'), may hold values from -4 to 4
- moment_up: float32 [2048, 8192], P('dp', 'shard'), may hold values from -4 to 4
- moment_down: float32 [8192, 2048], P('shard', 'dp'), may hold values from -4 to 4
- step: int32 [], replicated, may hold values from 1000 to 1999
- rate: float32 [], replicated, may hold values from 0.6 to 1.2
Outputs:
- output: bfloat16 [8192, 2048], P('dp')
- input_grad: float32 [8192, 2048], P('dp')
- global_norm: float32 [], replicated
- momentum_first: float32 [2048], P('dp')
- momentum_query: float32 [2048, 2048], P('dp', 'shard')
- momentum_key: float32 [2048, 512], P('dp', 'shard')
- momentum_value: float32 [2048, 512], P('dp', 'shard')
- momentum_output: float32 [2048, 2048], P('shard', 'dp')
- momentum_second: float32 [2048], P('dp')
- momentum_gate: float32 [2048, 8192], P('dp', 'shard')
- momentum_up: float32 [2048, 8192], P('dp', 'shard')
- momentum_down: float32 [8192, 2048], P('shard', 'dp')
- updated_first: float32 [2048], P('dp')
- updated_query: float32 [2048, 2048], P('dp', 'shard')
- updated_key: float32 [2048, 512], P('dp', 'shard')
- updated_value: float32 [2048, 512], P('dp', 'shard')
- updated_output: float32 [2048, 2048], P('shard', 'dp')
- updated_second: float32 [2048], P('dp')
- updated_gate: float32 [2048, 8192], P('dp', 'shard')
- updated_up: float32 [2048, 8192], P('dp', 'shard')
- updated_down: float32 [8192, 2048], P('shard', 'dp')
The draws below stay inside these ranges and needn't reach their ends.
Inputs may be any that keep to these rules, and one draw needn't show every extreme that they name: `block_ids`: along each row the block numbers never fall, every number 0 to 7 appears, and a block holds 1 to 256 positions.
All inputs are finite; a program needn't handle non-finite values.
Results may differ from the reference program's by a relative error of at most 0.02.
Values may be sent and summed in bfloat16 or wider, within the bound.
A program may use at most 256 MiB of HBM per device.

```python
import math
import jax
import jax.numpy as jnp
import numpy as np
from jax import lax

D = 2048
H = 32
KV = 8
HD = 64
FF = 8192
LEN = 1024
BMAX = 256
NBLK = 8
CLIP = 4096
WARMUP = 2000
NSEQ = 8
TOKENS = 8192


def feature_ramp(low_end, high_end):
    place = jnp.arange(D, dtype=jnp.float32) / jnp.float32(max(D - 1, 1))
    return low_end + (high_end - low_end) * place


def gain_draw(key):
    ramp = feature_ramp(0.6, 1.8)
    noise = 1.0 + 0.1 * jnp.clip(jax.random.normal(key, (D,), jnp.float32), -2.5, 2.5)
    return jnp.clip(ramp * noise, 0.3, 2.5)


def draw_gain_first(key, part):
    return gain_draw(jax.random.fold_in(key, 11))


def draw_gain_second(key, part):
    return gain_draw(jax.random.fold_in(key, 23))


def draw_cotangent(key, part):
    inner = jax.random.fold_in(key, 37)
    ramp = feature_ramp(0.6, 1.8)
    values = jnp.clip(jax.random.normal(inner, (TOKENS, D), jnp.float32), -6.0, 6.0)
    return jnp.clip(values * ramp[None, :], -12.0, 12.0).astype(jnp.bfloat16)


def steps_of(own_key, dims, pieces, least, largest):
    level = 1.0
    for position, blocks in pieces:
        steps = jax.random.uniform(jax.random.fold_in(jax.random.fold_in(own_key, 6), position), (blocks,), jnp.float32, least / len(pieces), largest / len(pieces))
        level = level * jnp.repeat(jnp.exp(steps), dims[position] // blocks).reshape((-1,) + (1,) * (len(dims) - 1 - position))
    return level


def profile(amount, total, limit, slope):
    weights = [(1 << 20) // math.isqrt(standing ** slope) + 1 for standing in range(2, amount + 1)]
    spare, given = total - limit - (amount - 1), [1] * (amount - 1)
    while spare > 0:
        free = [i for i in range(amount - 1) if given[i] < limit]
        pool, remaining = sum([weights[i] for i in free]), spare
        for i in free:
            addition = min(limit - given[i], max(1, remaining * weights[i] // pool), spare)
            given[i] = given[i] + addition
            spare = spare - addition
    return np.array([limit] + given)


def uneven_parts(stream_key, count, total, limit, skew):
    if count == 2:
        one = jax.random.randint(stream_key, (), max(1, total - limit), min(limit, total - 1) + 1)
        return jnp.stack([one, total - one])
    lengths = jnp.asarray(profile(count, total, limit, skew), jnp.int32)
    twos = (count - 1) // 2
    donor, sink = lengths[1:1 + 2 * twos:2], lengths[2:2 + 2 * twos:2]
    room = jnp.minimum(donor - 1, limit - sink)
    shifted = jax.random.randint(jax.random.fold_in(stream_key, 1), (twos,), 0, 1 << 20) % (room + 1)
    lengths = lengths.at[1:1 + 2 * twos:2].set(donor - shifted).at[2:2 + 2 * twos:2].set(sink + shifted)
    return lengths[jax.random.permutation(jax.random.fold_in(stream_key, 2), count)]


def scatter_about(own_key, dims, width, most, cuts=(), held_as=jnp.bfloat16):
    values = jax.random.normal(own_key, dims, jnp.float32) * width
    if len(cuts) > 0:
        values = steps_of(own_key, dims, cuts, -0.22, 0.18) * values
    return jnp.clip(values, min=-most, max=most).astype(held_as)


def setup_inputs(seed: int = 0) -> dict:
    streams_of = jax.random.split(jax.random.key(seed), 24)
    tokens = scatter_about(streams_of[0], (TOKENS, D), 1.0, 6.0, ((0, 8),))
    block_ids = jax.vmap(lambda own: jnp.searchsorted(jnp.cumsum(uneven_parts(own, NBLK, LEN, BMAX, 0)), jnp.arange(LEN), side="right"))(jax.random.split(streams_of[1], NSEQ)).reshape((NSEQ, LEN)).astype(jnp.int32)
    cotangent = draw_cotangent(jax.random.fold_in(streams_of[23], 71), 0)
    gain_first = draw_gain_first(jax.random.fold_in(streams_of[23], 71), 0)
    w_query = scatter_about(streams_of[4], (D, H * HD), D ** -0.5, 0.125, ((0, 8), (1, 4)), jnp.float32)
    w_key = scatter_about(streams_of[5], (D, KV * HD), D ** -0.5, 0.125, ((0, 8), (1, 4)), jnp.float32)
    w_value = scatter_about(streams_of[6], (D, KV * HD), D ** -0.5, 0.125, ((0, 8), (1, 4)), jnp.float32)
    w_output = scatter_about(streams_of[7], (H * HD, D), (max(4, H * HD // 256)) ** -0.5, 2.0, ((0, 4), (1, 8)), jnp.float32)
    gain_second = draw_gain_second(jax.random.fold_in(streams_of[23], 71), 0)
    w_gate = scatter_about(streams_of[9], (D, FF), D ** -0.5, 0.125, ((0, 8), (1, 4)), jnp.float32)
    w_up = scatter_about(streams_of[10], (D, FF), D ** -0.5, 0.125, ((0, 8), (1, 4)), jnp.float32)
    w_down = scatter_about(streams_of[11], (FF, D), FF ** -0.5, 0.0625, ((0, 4), (1, 8)), jnp.float32)
    moment_first = scatter_about(streams_of[12], (D,), 1.0, 6.0, ((0, 8),), jnp.float32)
    moment_query = scatter_about(streams_of[13], (D, H * HD), 0.5, 4.0, ((0, 8), (1, 4)), jnp.float32)
    moment_key = scatter_about(streams_of[14], (D, KV * HD), 0.5, 4.0, ((0, 8), (1, 4)), jnp.float32)
    moment_value = scatter_about(streams_of[15], (D, KV * HD), 0.5, 4.0, ((0, 8), (1, 4)), jnp.float32)
    moment_output = scatter_about(streams_of[16], (H * HD, D), 0.5, 4.0, ((0, 4), (1, 8)), jnp.float32)
    moment_second = scatter_about(streams_of[17], (D,), 1.0, 6.0, ((0, 8),), jnp.float32)
    moment_gate = scatter_about(streams_of[18], (D, FF), 0.5, 4.0, ((0, 8), (1, 4)), jnp.float32)
    moment_up = scatter_about(streams_of[19], (D, FF), 0.5, 4.0, ((0, 8), (1, 4)), jnp.float32)
    moment_down = scatter_about(streams_of[20], (FF, D), 0.5, 4.0, ((0, 4), (1, 8)), jnp.float32)
    step = jax.random.randint(streams_of[21], (), WARMUP // 2, WARMUP).astype(jnp.int32)
    rate = jnp.clip(jax.random.uniform(streams_of[22], (), jnp.float32, 0.6, 1.2), 0.6, 1.2)
    return {"tokens": tokens, "block_ids": block_ids, "cotangent": cotangent, "gain_first": gain_first, "w_query": w_query, "w_key": w_key, "w_value": w_value, "w_output": w_output, "gain_second": gain_second, "w_gate": w_gate, "w_up": w_up, "w_down": w_down, "moment_first": moment_first, "moment_query": moment_query, "moment_key": moment_key, "moment_value": moment_value, "moment_output": moment_output, "moment_second": moment_second, "moment_gate": moment_gate, "moment_up": moment_up, "moment_down": moment_down, "step": step, "rate": rate}


EPS = 1e-05
THETA = 10000000.0
NEGATIVE = -1e+30
HIGH = lax.Precision.HIGHEST

@jax.custom_vjp
def low(v):
    return lax.optimization_barrier(v.astype(jnp.bfloat16)).astype(jnp.float32)

@jax.custom_vjp
def low_back(v):
    return v

def low_keep(v):
    return (low(v), None)

def low_pass(kept, grad):
    return (grad,)

def back_keep(v):
    return (v, None)

def back_low(kept, grad):
    return (low(grad),)
low.defvjp(low_keep, low_pass)
low_back.defvjp(back_keep, back_low)

def mult(left, right):
    return jnp.dot(left, right, precision=HIGH, preferred_element_type=jnp.float32)

def rms_norm(values, gain):
    inverse = lax.rsqrt(lax.optimization_barrier(jnp.mean(values * values, axis=1, keepdims=True)) + EPS)
    return values * inverse * gain[None, :]

def angle_table(count):
    positions = (jnp.arange(count, dtype=jnp.int32) % LEN).astype(jnp.float32)
    powers = -2.0 * jnp.arange(HD // 2, dtype=jnp.float32) / HD
    angles = positions[:, None] * jnp.power(THETA, powers)[None, :]
    return (jnp.cos(angles)[:, None, :], jnp.sin(angles)[:, None, :])

def rotate(values, cosine, sine):
    half = values.shape[-1] // 2
    first = values[..., :half]
    second = values[..., half:]
    return jnp.concatenate([first * cosine - second * sine, second * cosine + first * sine], axis=-1)

def attend_one(parts):
    query, key, value, blocks = parts
    length = query.shape[0]
    group = H // KV
    grouped = query.reshape(length, KV, group, HD)
    scores = jnp.einsum('qkgd,jkd->kgqj', grouped, key, precision=HIGH, preferred_element_type=jnp.float32)
    scores = low_back(scores * (1.0 / jnp.sqrt(jnp.float32(HD))))
    allowed = blocks[None, :] <= blocks[:, None]
    scores = jnp.where(allowed[None, None], scores, NEGATIVE)
    weights = jnp.exp(scores - lax.optimization_barrier(jnp.max(scores, axis=3, keepdims=True)))
    probs = low(weights / lax.optimization_barrier(jnp.sum(weights, axis=3, keepdims=True)))
    mixed = jnp.einsum('kgqj,jkd->qkgd', probs, value, precision=HIGH, preferred_element_type=jnp.float32)
    return mixed.reshape(length, H * HD)

def layer(inputs, params, blocks):
    gain_one, query_weight, key_weight, value_weight, output_weight, gain_two, gate_weight, up_weight, down_weight = params
    count = inputs.shape[0]
    nseq = blocks.shape[0]
    cosine, sine = angle_table(count)
    normed = low(rms_norm(inputs, low(gain_one)))
    query = low(rotate(low_back(mult(normed, low(query_weight))).reshape(count, H, HD), cosine, sine))
    key = low(rotate(low_back(mult(normed, low(key_weight))).reshape(count, KV, HD), cosine, sine))
    value = low(low_back(mult(normed, low(value_weight)))).reshape(count, KV, HD)
    attended = lax.map(jax.checkpoint(attend_one), (query.reshape(nseq, LEN, H, HD), key.reshape(nseq, LEN, KV, HD), value.reshape(nseq, LEN, KV, HD), blocks))
    mixed = low(low_back(attended.reshape(count, H * HD)))
    hidden = inputs + low_back(mult(mixed, low(output_weight)))
    normed_two = low(rms_norm(hidden, low(gain_two)))
    gate = low_back(mult(normed_two, low(gate_weight)))
    up = low_back(mult(normed_two, low(up_weight)))
    activated = low(gate * jax.nn.sigmoid(gate) * up)
    return hidden + low_back(mult(activated, low(down_weight)))

def reference(tokens, block_ids, cotangent, gain_first, w_query, w_key, w_value, w_output, gain_second, w_gate, w_up, w_down, moment_first, moment_query, moment_key, moment_value, moment_output, moment_second, moment_gate, moment_up, moment_down, step, rate):
    masters = (gain_first, w_query, w_key, w_value, w_output, gain_second, w_gate, w_up, w_down)
    moments = (moment_first, moment_query, moment_key, moment_value, moment_output, moment_second, moment_gate, moment_up, moment_down)

    def layer_of(inputs, *params):
        return layer(inputs, params, block_ids)
    result, pull = jax.vjp(layer_of, tokens.astype(jnp.float32), *masters)
    grads = pull(cotangent.astype(jnp.float32))
    input_grad = grads[0]
    gradients = grads[1:]
    squares = jnp.zeros((), jnp.float32)
    for gradient in gradients:
        squares = squares + jnp.sum(gradient * gradient)
    global_norm = jnp.sqrt(squares)
    factor = jnp.minimum(1.0, CLIP / global_norm)
    rate_now = rate * jnp.minimum(1.0, (step.astype(jnp.float32) + 1.0) / WARMUP)
    momenta = [0.5 * moment + 0.5 * (factor * gradient) for moment, gradient in zip(moments, gradients)]
    updated = [master - rate_now * momentum for master, momentum in zip(masters, momenta)]
    return (result.astype(jnp.bfloat16), input_grad, global_norm, momenta[0], momenta[1], momenta[2], momenta[3], momenta[4], momenta[5], momenta[6], momenta[7], momenta[8], updated[0], updated[1], updated[2], updated[3], updated[4], updated[5], updated[6], updated[7], updated[8])
```

```python
import math

import jax
import jax.numpy as jnp
from jax import lax
from jax.sharding import PartitionSpec as P

H = 32
KV = 8
HD = 64
CLIP = 4096
WARMUP = 2000

EPS = 1e-05
THETA = 10000000.0
NEGATIVE = -1e30
CHUNKS = 2

BF = jnp.bfloat16
F32 = jnp.float32


def inverse_rms(values):
    return lax.rsqrt(jnp.mean(values * values, axis=-1, keepdims=True) + EPS)


def norm_back(values, inverse, gain, grad_normed):
    scaled = grad_normed * gain
    gain_grad = jnp.sum(grad_normed * values * inverse, axis=0)
    grad_values = inverse * scaled - values * inverse**3 * jnp.mean(
        scaled * values, axis=-1, keepdims=True
    )
    return (gain_grad, grad_values)


def angle_table(length):
    positions = jnp.arange(length, dtype=jnp.int32).astype(F32)
    powers = -2.0 * jnp.arange(HD // 2, dtype=F32) / HD
    angles = positions[:, None] * jnp.power(THETA, powers)[None, :]
    return (jnp.cos(angles)[None, :, None, :], jnp.sin(angles)[None, :, None, :])


def rotate(values, cosine, sine):
    half = values.shape[-1] // 2
    first = values[..., :half]
    second = values[..., half:]
    return jnp.concatenate(
        [first * cosine - second * sine, second * cosine + first * sine], axis=-1
    )


def unrotate(grads, cosine, sine):
    half = grads.shape[-1] // 2
    first = grads[..., :half]
    second = grads[..., half:]
    return jnp.concatenate(
        [first * cosine + second * sine, second * cosine - first * sine], axis=-1
    )


def item_scores(query, key, blocks, scale):
    scores = jnp.einsum("qgd,jd->gqj", query, key, preferred_element_type=F32) * scale
    allowed = blocks[None, :] <= blocks[:, None]
    return jnp.where(allowed[None], scores, NEGATIVE)


def attend_forward(scale):

    def run(parts):
        query, key, value, blocks = parts
        scores = item_scores(query, key, blocks, scale)
        peak = jnp.max(scores, axis=2, keepdims=True)
        weights = jnp.exp(scores - peak)
        total = jnp.sum(weights, axis=2, keepdims=True)
        probs = (weights / total).astype(BF)
        mixed = jnp.einsum("gqj,jd->qgd", probs, value, preferred_element_type=F32)
        return (mixed.astype(BF), peak, total)

    return run


def attend_backward(scale):

    def run(parts):
        query, key, value, blocks, peak, total, grad_mixed = parts
        scores = item_scores(query, key, blocks, scale)
        probs = jnp.exp(scores - peak) / total
        probs_low = probs.astype(BF)
        grad_value = jnp.einsum("gqj,qgd->jd", probs_low, grad_mixed, preferred_element_type=F32)
        grad_probs = jnp.einsum("qgd,jd->gqj", grad_mixed, value, preferred_element_type=F32)
        grad_scores = (
            probs * (grad_probs - jnp.sum(probs * grad_probs, axis=2, keepdims=True))
        ).astype(BF)
        grad_query = (
            jnp.einsum("gqj,jd->qgd", grad_scores, key, preferred_element_type=F32) * scale
        )
        grad_key = jnp.einsum("gqj,qgd->jd", grad_scores, query, preferred_element_type=F32) * scale
        return (grad_query, grad_key, grad_value)

    return run


def build(dps, shards):
    total = dps * shards
    axes = ("dp", "shard")
    zgroups = [[i for i in range(dps) if i % 2 == p] for p in (0, 1)]

    def swap(values, dx, ds):
        pairs = [
            (i, ((i // shards) ^ dx) * shards + ((i % shards) ^ ds)) for i in range(total)
        ]
        return lax.ppermute(values, axes, pairs)

    def gather(piece):
        return lax.all_gather(piece, "dp", axis=0, tiled=True, axis_index_groups=zgroups)

    def scatter(whole):
        return lax.psum_scatter(
            whole, "dp", scatter_dimension=0, tiled=True, axis_index_groups=zgroups
        )

    def sum_to_owner(partial):
        even = partial[:, 0::2]
        odd = partial[:, 1::2].astype(BF)
        paired = even.astype(F32) + swap(odd, 0, 1).astype(F32)
        low = paired.astype(BF)
        from_y = swap(low[0, 1], 0, 2)
        from_x = swap(low[1, 0], 1, 0)
        from_d = swap(low[1, 1], 1, 2)
        return paired[0, 0] + from_y.astype(F32) + from_x.astype(F32) + from_d.astype(F32)

    def spread(own):
        from_y = swap(own, 0, 2)
        from_x = swap(own, 1, 0)
        from_d = swap(own, 1, 2)
        mine = jnp.stack([own, from_y, from_x, from_d])
        theirs = swap(mine, 0, 1)
        return jnp.stack([mine, theirs], axis=1).reshape((2, shards) + own.shape)

    def on_device(
        tokens,
        block_ids,
        cotangent,
        gain_first,
        w_query,
        w_key,
        w_value,
        w_output,
        gain_second,
        w_gate,
        w_up,
        w_down,
        moment_first,
        moment_query,
        moment_key,
        moment_value,
        moment_output,
        moment_second,
        moment_gate,
        moment_up,
        moment_down,
        step,
        rate,
    ):
        length = block_ids.shape[1]
        width = tokens.shape[1]
        scale = 1.0 / math.sqrt(HD)
        group = H // KV
        dp = lax.axis_index("dp")
        me = lax.axis_index("shard")
        x = lax.rem(dp, 2)
        core = lax.rem(me, 2)
        quarter = length // shards
        rows = w_query.shape[0]

        def half(values, which):
            size = values.shape[1] // 2
            return lax.dynamic_slice_in_dim(values, which * size, size, axis=1)

        def ordered(mine, theirs, axis=0):
            first = jnp.where(x == 0, mine, theirs)
            second = jnp.where(x == 0, theirs, mine)
            return jnp.concatenate([first, second], axis=axis)

        low_q = w_query.astype(BF)
        low_k = w_key.astype(BF)
        low_v = w_value.astype(BF)
        low_o = w_output.astype(BF).T
        low_g = w_gate.astype(BF)
        low_u = w_up.astype(BF)
        low_d = w_down.astype(BF).T

        def attn_half(which):
            return jnp.concatenate([half(low_q, which), half(low_k, which), half(low_v, which)], axis=1)

        cols = low_q.shape[1] // 2 + low_k.shape[1]
        gains = jnp.stack([gain_first, gain_second]).astype(BF)
        gains = jnp.pad(gains, ((0, 14), (0, cols - rows)))
        sent = swap(jnp.concatenate([attn_half(1 - x), gains], axis=0), 1, 0)
        piece = jnp.concatenate(
            [ordered(attn_half(x), sent[:rows]), ordered(gains, sent[rows:])], axis=0
        )
        groups = dps // 2
        packed = gather(piece).reshape(groups, 2 * rows + 32, cols)
        qkv_weight = packed[:, : 2 * rows].reshape(width, cols)
        tails = packed[:, 2 * rows :].reshape(groups, 2, 16, cols)
        gain_one = tails[:, :, 0, :rows].reshape(width).astype(F32)
        gain_two = tails[:, :, 1, :rows].reshape(width).astype(F32)

        out_weight = gather(ordered(half(low_o, x), swap(half(low_o, 1 - x), 1, 0)))
        size = low_g.shape[1] // 2 // CHUNKS

        def ffn_part(which, j):
            return jnp.concatenate(
                [half(low, which)[:, j * size : (j + 1) * size] for low in (low_g, low_u, low_d)],
                axis=1,
            )

        ffn_weights = []
        for j in range(CHUNKS):
            ffn_weights.append(gather(ordered(ffn_part(x, j), swap(ffn_part(1 - x, j), 1, 0))))

        start = core * (length // 2)
        got = swap(lax.dynamic_slice_in_dim(tokens, start, length // 2, axis=0), 1, 0)
        got_other = swap(got, 0, 1)
        other_tokens = jnp.where(
            core == 0,
            jnp.concatenate([got, got_other], axis=0),
            jnp.concatenate([got_other, got], axis=0),
        )
        both = jnp.stack([tokens, other_tokens])
        blocks = jnp.concatenate([block_ids, swap(block_ids, 1, 0)], axis=0)

        def to_relative(values):
            parts = [
                lax.dynamic_slice_in_dim(values, (me ^ ds) * quarter, quarter, axis=1)
                for ds in range(shards)
            ]
            return jnp.stack(parts, axis=1)

        def to_natural(values):
            parts = [
                lax.dynamic_index_in_dim(values, me ^ q, axis=1, keepdims=False)
                for q in range(shards)
            ]
            return jnp.concatenate(parts, axis=1)

        cot_own = to_relative(cotangent[None])[0]
        cot_got = swap(cot_own[0::2], 1, 0)
        cot_core = swap(cot_got, 0, 1)
        cot_other = jnp.stack([cot_got, cot_core], axis=1).reshape(cot_own.shape)
        cot_rel = jnp.stack([cot_own, cot_other]).reshape(2 * length, width)

        inputs = both.astype(F32)
        inverse_first = inverse_rms(inputs)
        normed = (inputs * inverse_first * gain_one).astype(BF).reshape(2 * length, width)
        cosine, sine = angle_table(length)
        lin = jnp.dot(normed, qkv_weight, preferred_element_type=F32)
        lin = lin.reshape(2, length, cols // HD, HD)
        query = rotate(lin[:, :, :group], cosine, sine).astype(BF)
        key = rotate(lin[:, :, group : group + 1], cosine, sine).astype(BF)[:, :, 0]
        value = lin[:, :, group + 1].astype(BF)
        mixed, peak, total_w = lax.map(attend_forward(scale), (query, key, value, blocks))
        mixed_rel = to_relative(mixed.reshape(2, length, group * HD)).reshape(2 * length, group * HD)
        partial = jnp.einsum("tk,dk->td", mixed_rel, out_weight, preferred_element_type=F32)
        summed = sum_to_owner(partial.astype(BF).reshape(2, shards, quarter, width))
        tokens_own = lax.dynamic_slice_in_dim(tokens, me * quarter, quarter, axis=0).astype(F32)
        hidden = tokens_own + summed
        inverse_second = inverse_rms(hidden)
        normed_two_own = (hidden * inverse_second * gain_two).astype(BF)
        normed_two = spread(normed_two_own).reshape(2 * length, width)

        grads_ffn = []
        partial_two = None
        result = None
        for j in range(CHUNKS):
            weight = ffn_weights[j]
            w_gu, w_dt = weight[:, : 2 * size], weight[:, 2 * size :]
            gate_up = jnp.dot(normed_two, w_gu, preferred_element_type=F32)
            gate, up = gate_up[:, :size], gate_up[:, size:]
            grad_act = jnp.dot(cot_rel, w_dt, preferred_element_type=F32)
            sig = jax.nn.sigmoid(gate)
            activated = (gate * sig * up).astype(BF)
            grad_gate_in = (grad_act * up * sig * (1.0 + gate * (1.0 - sig))).astype(BF)
            grad_up_in = (grad_act * gate * sig).astype(BF)
            grad_gu = jnp.concatenate([grad_gate_in, grad_up_in], axis=1)
            part = jnp.einsum("tf,cf->tc", grad_gu, w_gu, preferred_element_type=F32)
            partial_two = part if partial_two is None else partial_two + part
            part = jnp.einsum("tf,cf->tc", activated, w_dt, preferred_element_type=F32)
            result = part if result is None else result + part
            d_gu = jnp.einsum("tc,tf->cf", normed_two, grad_gu, preferred_element_type=F32)
            d_dt = jnp.einsum("tc,tf->cf", cot_rel, activated, preferred_element_type=F32)
            grads_ffn.append(scatter(jnp.concatenate([d_gu.astype(BF), d_dt.astype(BF)], axis=1)))

        shape = (2, shards, quarter, width)
        grad_normed_two = sum_to_owner(partial_two.astype(BF).reshape(shape))
        cot_mine = cot_own[0].astype(F32)
        gain_grad_two, grad_through = norm_back(hidden, inverse_second, gain_two, grad_normed_two)
        grad_hidden = cot_mine + grad_through
        grad_hidden_rel = spread(grad_hidden.astype(BF)).reshape(2 * length, width)

        def to_sequence(own):
            from_y = swap(own, 0, 2)
            mine = jnp.stack([own, from_y])
            theirs = swap(mine, 0, 1)
            rel = jnp.stack([mine, theirs], axis=1).reshape((1, shards) + own.shape)
            return to_natural(rel)[0]

        output_own = (hidden + sum_to_owner(result.astype(BF).reshape(shape))).astype(BF)
        output = to_sequence(output_own)

        d_out = jnp.einsum("td,tk->dk", grad_hidden_rel, mixed_rel, preferred_element_type=F32)
        grad_out = scatter(d_out.astype(BF))
        grad_mixed = jnp.dot(grad_hidden_rel, out_weight, preferred_element_type=F32).astype(BF)
        grad_mixed = to_natural(grad_mixed.reshape(2, shards, quarter, group * HD))
        grad_query, grad_key, grad_value = lax.map(
            attend_backward(scale),
            (
                query,
                key,
                value,
                blocks,
                peak,
                total_w,
                grad_mixed.reshape(2, length, group, HD),
            ),
        )
        grad_qkv = jnp.concatenate(
            [
                unrotate(grad_query, cosine, sine).astype(BF),
                unrotate(grad_key[:, :, None], cosine, sine).astype(BF),
                grad_value[:, :, None].astype(BF),
            ],
            axis=2,
        ).reshape(2, length, cols)
        d_qkv = jnp.einsum(
            "tc,tk->ck", normed, grad_qkv.reshape(2 * length, cols), preferred_element_type=F32
        )
        grad_qkv_w = scatter(d_qkv.astype(BF))
        partial_one = jnp.einsum(
            "tk,ck->tc",
            to_relative(grad_qkv).reshape(2 * length, cols),
            qkv_weight,
            preferred_element_type=F32,
        )
        grad_normed = sum_to_owner(partial_one.astype(BF).reshape(shape))
        inverse_own = inverse_rms(tokens_own)
        gain_grad_one, grad_inner = norm_back(tokens_own, inverse_own, gain_one, grad_normed)
        input_grad = to_sequence((grad_hidden + grad_inner).astype(BF)).astype(F32)

        def owned_halves(piece):
            keep = lax.dynamic_slice_in_dim(piece, x * rows, rows, axis=0)
            send = lax.dynamic_slice_in_dim(piece, (1 - x) * rows, rows, axis=0)
            return keep, swap(send, 1, 0)

        def joined(mine, theirs):
            return ordered(mine, theirs, axis=1).astype(F32)

        mine, theirs = owned_halves(grad_qkv_w)
        qc = group * HD
        own_q = joined(mine[:, :qc], theirs[:, :qc])
        own_k = joined(mine[:, qc : qc + HD], theirs[:, qc : qc + HD])
        own_v = joined(mine[:, qc + HD :], theirs[:, qc + HD :])
        mine, theirs = owned_halves(grad_out)
        own_o = joined(mine, theirs).T
        pairs = [owned_halves(piece) for piece in grads_ffn]
        own_gud = []
        for part in range(3):
            cut = slice(part * size, (part + 1) * size)
            own_gud.append(
                joined(
                    jnp.concatenate([m[:, cut] for m, t in pairs], axis=1),
                    jnp.concatenate([t[:, cut] for m, t in pairs], axis=1),
                )
            )
        own_g, own_u, own_d = own_gud[0], own_gud[1], own_gud[2].T
        gain_grads = lax.psum(jnp.stack([gain_grad_one, gain_grad_two]), axes)
        gain_grads = lax.dynamic_slice_in_dim(gain_grads, dp * rows, rows, axis=1)
        owned = (gain_grads[0], own_q, own_k, own_v, own_o, gain_grads[1], own_g, own_u, own_d)

        first_shard = (me == 0).astype(F32)
        squares = first_shard * (jnp.sum(owned[0] * owned[0]) + jnp.sum(owned[5] * owned[5]))
        for position in (1, 2, 3, 4, 6, 7, 8):
            squares = squares + jnp.sum(owned[position] * owned[position])
        global_norm = jnp.sqrt(lax.psum(squares, axes))
        factor = jnp.minimum(1.0, CLIP / global_norm)
        rate_now = rate * jnp.minimum(1.0, (step.astype(F32) + 1.0) / WARMUP)
        masters = (gain_first, w_query, w_key, w_value, w_output, gain_second, w_gate, w_up, w_down)
        moments = (
            moment_first,
            moment_query,
            moment_key,
            moment_value,
            moment_output,
            moment_second,
            moment_gate,
            moment_up,
            moment_down,
        )
        momenta = [
            0.5 * moment + 0.5 * (factor * gradient) for moment, gradient in zip(moments, owned)
        ]
        updated = [master - rate_now * momentum for master, momentum in zip(masters, momenta)]
        return (output, input_grad, global_norm, *momenta, *updated)

    return on_device


def solution(mesh):
    rows, both, back = P("dp"), P("dp", "shard"), P("shard", "dp")
    tokens = P("dp", None)
    params = (rows, both, both, both, back, rows, both, both, back)
    in_specs = (tokens, tokens, tokens, *params, *params, P(), P())
    out_specs = (tokens, tokens, P(), *params, *params)
    return jax.shard_map(
        build(mesh.shape["dp"], mesh.shape["shard"]),
        mesh=mesh,
        in_specs=in_specs,
        out_specs=out_specs,
        check_vma=False,
    )
```

```python
import functools

import jax
import jax.numpy as jnp
from jax import lax
from jax.experimental import pallas as pl
from jax.experimental.pallas import tpu as pltpu
from jax.sharding import PartitionSpec as P

H = 32
KV = 8
CLIP = 4096
WARMUP = 2000
THETA = 10000000.0
CHUNKS = 2
MESH = pl.DeviceIdType.MESH


BF = jnp.bfloat16
F32 = jnp.float32
HD = 64
EPS = 1e-05
NEGATIVE = -1e30
VMEM = 48 << 20

def dot(a, b, ca, cb):
    return lax.dot_general(a, b, (((ca,), (cb,)), ((), ())), preferred_element_type=F32)

def swap_halves(v):
    n = v.shape[1]
    lane = lax.broadcasted_iota(jnp.int32, v.shape, 1)
    return jnp.where(lane % HD < HD // 2, pltpu.roll(v, n - HD // 2, 1), pltpu.roll(v, HD // 2, 1))

def qkv_body(tok_ref, gain_ref, w_ref, cos_ref, sin_ref, normed_ref, q_ref, k_ref, v_ref):
    x = tok_ref[...].astype(F32)
    inv = lax.rsqrt(jnp.mean(x * x, axis=1, keepdims=True) + EPS)
    normed = (x * inv * gain_ref[...]).astype(BF)
    normed_ref[...] = normed
    lin = dot(normed, w_ref[...], 1, 0)
    heads = q_ref.shape[0]
    qc = heads * HD
    rot = lin * cos_ref[...] + swap_halves(lin) * sin_ref[...]
    for h in range(heads):
        q_ref[h] = (rot[:, h * HD : (h + 1) * HD]).astype(BF)
    k_ref[...] = rot[:, qc : qc + HD].astype(BF)
    v_ref[...] = rot[:, qc + HD :].astype(BF)

def qkv(tokens, gain, weight, cos, sin, heads, tile=256):
    count, width = tokens.shape
    cols = weight.shape[1]
    length = cos.shape[0]
    per = length // tile
    full = lambda i: (0, 0)
    row = lambda i: (i, 0)
    return pl.pallas_call(
        qkv_body,
        grid=(count // tile,),
        in_specs=[
            pl.BlockSpec((tile, width), row),
            pl.BlockSpec((1, width), full),
            pl.BlockSpec((width, cols), full),
            pl.BlockSpec((tile, cols), lambda i: (i % per, 0)),
            pl.BlockSpec((tile, cols), lambda i: (i % per, 0)),
        ],
        out_specs=[
            pl.BlockSpec((tile, width), row),
            pl.BlockSpec((heads, tile, HD), lambda i: (0, i, 0)),
            pl.BlockSpec((tile, HD), row),
            pl.BlockSpec((tile, HD), row),
        ],
        out_shape=[
            jax.ShapeDtypeStruct((count, width), BF),
            jax.ShapeDtypeStruct((heads, count, HD), BF),
            jax.ShapeDtypeStruct((count, HD), BF),
            jax.ShapeDtypeStruct((count, HD), BF),
        ],
        compiler_params=pltpu.CompilerParams(vmem_limit_bytes=VMEM),
        cost_estimate=pl.CostEstimate(flops=2 * count * width * cols, bytes_accessed=4 * count * width, transcendentals=0),
        name="qkv_rope",
    )(tokens, gain, weight, cos, sin)

def fwd_body(limits, q_ref, k_ref, v_ref, brow_ref, bcol_ref, o_ref, lse_ref):
    heads, tile, _ = q_ref.shape
    i = pl.program_id(1)
    def run(keys):
        k = k_ref[:keys]
        v = v_ref[:keys]
        allowed = brow_ref[0][:, :keys] <= bcol_ref[...]
        outs = []
        lses = []
        for h in range(heads):
            s = dot(q_ref[h] * BF(0.125), k, 1, 1)
            s = jnp.where(allowed, s, NEGATIVE)
            m = jnp.max(s, axis=1, keepdims=True)
            p = jnp.exp(s - m)
            l = jnp.sum(p, axis=1, keepdims=True)
            o = dot(p.astype(BF), v, 1, 0) / l
            outs.append(o.astype(BF))
            lses.append(m + jnp.log(l))
        o_ref[...] = jnp.concatenate(outs, axis=1)
        lse_ref[...] = jnp.concatenate(lses, axis=1)
    for n, keys in enumerate(limits):
        @pl.when(i == n)
        def _(keys=keys):
            run(keys)

def attend(q, k, v, brow, bcol, length, tile=256, most=256):
    heads, count, _ = q.shape
    seqs = count // length
    per = length // tile
    limits = tuple(min(length, (n + 1) * tile + most) for n in range(per))
    return pl.pallas_call(
        functools.partial(fwd_body, limits),
        grid=(seqs, per),
        in_specs=[
            pl.BlockSpec((heads, tile, HD), lambda b, i: (0, b * per + i, 0)),
            pl.BlockSpec((length, HD), lambda b, i: (b, 0)),
            pl.BlockSpec((length, HD), lambda b, i: (b, 0)),
            pl.BlockSpec((1, 1, length), lambda b, i: (b, 0, 0)),
            pl.BlockSpec((tile, 1), lambda b, i: (b * per + i, 0)),
        ],
        out_specs=[
            pl.BlockSpec((tile, heads * HD), lambda b, i: (b * per + i, 0)),
            pl.BlockSpec((tile, heads), lambda b, i: (b * per + i, 0)),
        ],
        out_shape=[
            jax.ShapeDtypeStruct((count, heads * HD), BF),
            jax.ShapeDtypeStruct((count, heads), F32),
        ],
        compiler_params=pltpu.CompilerParams(vmem_limit_bytes=VMEM),
        cost_estimate=pl.CostEstimate(flops=4 * heads * count * length * HD * 4, bytes_accessed=count * 2048, transcendentals=heads * count * length),
        name="attend",
    )(q, k, v, brow, bcol)

def bwd_body(limits, q_ref, k_ref, v_ref, brow_ref, bcol_ref, lse_ref, do_ref, cos_ref, sin_ref, kcos_ref, ksin_ref, dq_ref, dkv_ref, dk_acc, dv_acc):
    heads, tile, _ = q_ref.shape
    i = pl.program_id(1)
    @pl.when(i == 0)
    def _():
        dk_acc[...] = jnp.zeros_like(dk_acc)
        dv_acc[...] = jnp.zeros_like(dv_acc)
    def run(keys):
        k = k_ref[:keys]
        v = v_ref[:keys]
        allowed = brow_ref[0][:, :keys] <= bcol_ref[...]
        dqs = []
        dk = jnp.zeros((HD, keys), F32)
        dv = jnp.zeros((HD, keys), F32)
        for h in range(heads):
            q = q_ref[h] * BF(0.125)
            do = do_ref[:, h * HD : (h + 1) * HD]
            s = dot(q, k, 1, 1)
            s = jnp.where(allowed, s, NEGATIVE)
            p = jnp.exp(s - lse_ref[:, h : h + 1])
            dp = dot(do, v, 1, 1)
            pdp = p * dp
            delta = jnp.sum(pdp, axis=1, keepdims=True)
            ds = (pdp - p * delta).astype(BF)
            dqs.append(dot(ds, k, 1, 0) * 0.125)
            dk = dk + dot(q, ds, 0, 0)
            dv = dv + dot(do, p.astype(BF), 0, 0)
        dk_acc[:, :keys] += dk
        dv_acc[:, :keys] += dv
        dq = jnp.concatenate(dqs, axis=1)
        dq_ref[...] = (dq * cos_ref[...] - swap_halves(dq) * sin_ref[...]).astype(BF)
    for n, keys in enumerate(limits):
        @pl.when(i == n)
        def _(keys=keys):
            run(keys)
    @pl.when(i == len(limits) - 1)
    def _():
        both = jnp.concatenate([dk_acc[...], dv_acc[...]], axis=0).T
        dkv_ref[...] = (both * kcos_ref[...] - swap_halves(both) * ksin_ref[...]).astype(BF)

def attend_back(q, k, v, brow, bcol, lse, do, cos, sin, length, tile=256, most=256):
    heads, count, _ = q.shape
    seqs = count // length
    per = length // tile
    qc = heads * HD
    limits = tuple(min(length, (n + 1) * tile + most) for n in range(per))
    rowm = lambda b, i: (b * per + i, 0)
    return pl.pallas_call(
        functools.partial(bwd_body, limits),
        grid=(seqs, per),
        in_specs=[
            pl.BlockSpec((heads, tile, HD), lambda b, i: (0, b * per + i, 0)),
            pl.BlockSpec((length, HD), lambda b, i: (b, 0)),
            pl.BlockSpec((length, HD), lambda b, i: (b, 0)),
            pl.BlockSpec((1, 1, length), lambda b, i: (b, 0, 0)),
            pl.BlockSpec((tile, 1), rowm),
            pl.BlockSpec((tile, heads), rowm),
            pl.BlockSpec((tile, qc), rowm),
            pl.BlockSpec((tile, qc), lambda b, i: (i, 0)),
            pl.BlockSpec((tile, qc), lambda b, i: (i, 0)),
            pl.BlockSpec((length, 2 * HD), lambda b, i: (0, qc // (2 * HD))),
            pl.BlockSpec((length, 2 * HD), lambda b, i: (0, qc // (2 * HD))),
        ],
        out_specs=[
            pl.BlockSpec((tile, qc), rowm),
            pl.BlockSpec((length, 2 * HD), lambda b, i: (b, 0)),
        ],
        out_shape=[
            jax.ShapeDtypeStruct((count, qc), BF),
            jax.ShapeDtypeStruct((count, 2 * HD), BF),
        ],
        scratch_shapes=[pltpu.VMEM((HD, length), F32), pltpu.VMEM((HD, length), F32)],
        compiler_params=pltpu.CompilerParams(vmem_limit_bytes=VMEM),
        cost_estimate=pl.CostEstimate(flops=10 * heads * count * length * HD * 4, bytes_accessed=count * 4096, transcendentals=heads * count * length),
        name="attend_back",
    )(q, k, v, brow, bcol, lse, do, cos, sin, cos, sin)

def rope_tables(length, heads):
    positions = jnp.arange(length, dtype=jnp.int32).astype(F32)
    powers = -2.0 * jnp.arange(HD // 2, dtype=F32) / HD
    angles = positions[:, None] * jnp.power(THETA, powers)[None, :]
    c = jnp.cos(angles); s = jnp.sin(angles)
    cos = jnp.concatenate([jnp.tile(jnp.concatenate([c, c], axis=1), (1, heads + 1)), jnp.ones((length, HD), F32)], axis=1)
    sin = jnp.concatenate([jnp.tile(jnp.concatenate([-s, s], axis=1), (1, heads + 1)), jnp.zeros((length, HD), F32)], axis=1)
    return cos, sin

def up_body(first, last, n2_ref, cot_ref, w_ref, *rest):
    if first:
        act_ref, dgu_ref, part_ref = rest
    else:
        prev_ref, act_ref, dgu_ref, part_ref = rest
    size = act_ref.shape[1]
    gu = dot(n2_ref[...], w_ref[:, : 2 * size], 1, 0)
    da = dot(cot_ref[...], w_ref[:, 2 * size :], 1, 0)
    gate, up = gu[:, :size], gu[:, size:]
    sig = 1.0 / (1.0 + jnp.exp(-gate))
    gs = gate * sig
    act_ref[...] = (gs * up).astype(BF)
    dg = (da * up * sig * (1.0 + gate * (1.0 - sig))).astype(BF)
    du = (da * gs).astype(BF)
    dgu = jnp.concatenate([dg, du], axis=1)
    dgu_ref[...] = dgu
    part = dot(dgu, w_ref[:, : 2 * size], 1, 1)
    if not first:
        part = part + prev_ref[...]
    part_ref[...] = part.astype(part_ref.dtype)

def up_back(n2, cot, weight, prev, last, tile=256):
    count, width = n2.shape
    size = weight.shape[1] // 3
    row = lambda i: (i, 0)
    full = lambda i: (0, 0)
    ins = [n2, cot, weight] + ([] if prev is None else [prev])
    specs = [pl.BlockSpec((tile, width), row), pl.BlockSpec((tile, width), row), pl.BlockSpec((width, 3 * size), full, pipeline_mode=pl.Buffered(1))]
    if prev is not None:
        specs.append(pl.BlockSpec((tile, width), row))
    return pl.pallas_call(
        functools.partial(up_body, prev is None, last),
        grid=(count // tile,),
        in_specs=specs,
        out_specs=[pl.BlockSpec((tile, size), row), pl.BlockSpec((tile, 2 * size), row), pl.BlockSpec((tile, width), row)],
        out_shape=[jax.ShapeDtypeStruct((count, size), BF), jax.ShapeDtypeStruct((count, 2 * size), BF), jax.ShapeDtypeStruct((count, width), BF if last else F32)],
        compiler_params=pltpu.CompilerParams(vmem_limit_bytes=VMEM),
        cost_estimate=pl.CostEstimate(flops=2 * count * width * size * 5, bytes_accessed=12 * count * width, transcendentals=count * size),
        name="swiglu_part",
    )(*ins)

def grad_body(n2_ref, cot_ref, dgu_ref, act_ref, o_ref):
    size = act_ref.shape[1]
    o_ref[:, : 2 * size] = dot(n2_ref[...], dgu_ref[...], 0, 0).astype(BF)
    o_ref[:, 2 * size :] = dot(cot_ref[...], act_ref[...], 0, 0).astype(BF)

def ffn_grads(n2, cot, dgu, act, tile=256):
    count, width = n2.shape
    size = act.shape[1]
    col = lambda i: (0, i)
    full = lambda i: (0, 0)
    return pl.pallas_call(
        grad_body,
        grid=(width // tile,),
        in_specs=[pl.BlockSpec((count, tile), col), pl.BlockSpec((count, tile), col), pl.BlockSpec((count, 2 * size), full, pipeline_mode=pl.Buffered(1)), pl.BlockSpec((count, size), full, pipeline_mode=pl.Buffered(1))],
        out_specs=pl.BlockSpec((tile, 3 * size), lambda i: (i, 0)),
        out_shape=jax.ShapeDtypeStruct((width, 3 * size), BF),
        compiler_params=pltpu.CompilerParams(vmem_limit_bytes=VMEM),
        cost_estimate=pl.CostEstimate(flops=2 * count * width * size * 3, bytes_accessed=8 * count * width, transcendentals=0),
        name="swiglu_grads",
    )(n2, cot, dgu, act)

def out_body(*refs):
    count = len(refs) // 2
    total = dot(refs[0][...], refs[count][...], 1, 1)
    for j in range(1, count):
        total = total + dot(refs[j][...], refs[count + j][...], 1, 1)
    refs[-1][...] = total.astype(BF)


def down(acts, weights, tile=256):
    count, size = acts[0].shape
    width = weights[0].shape[0]
    row = lambda i: (i, 0)
    return pl.pallas_call(
        out_body,
        grid=(count // tile,),
        in_specs=[pl.BlockSpec((tile, size), row) for _ in acts]
        + [
            pl.BlockSpec((width, size), lambda i: (0, 2), pipeline_mode=pl.Buffered(1))
            for _ in weights
        ],
        out_specs=pl.BlockSpec((tile, width), row),
        out_shape=jax.ShapeDtypeStruct((count, width), BF),
        compiler_params=pltpu.CompilerParams(vmem_limit_bytes=VMEM),
        cost_estimate=pl.CostEstimate(
            flops=2 * count * width * size * len(acts),
            bytes_accessed=8 * count * width,
            transcendentals=0,
        ),
        name="swiglu_down",
    )(*acts, *weights)


def sum_body(dps, shards, x_ref, o_ref, slots, send, recv):
    total = dps * shards
    me = lax.axis_index("dp") * shards + lax.axis_index("shard")
    barrier = pltpu.get_barrier_semaphore()

    def device(p):
        target = lax.rem(me + p, total)
        return (target // shards, lax.rem(target, shards))

    def greet(p, carry):
        pl.semaphore_signal(barrier, inc=1, device_id=device(p), device_id_type=MESH)
        return carry

    lax.fori_loop(1, total, greet, 0)
    slots[me] = x_ref[...]
    pl.semaphore_wait(barrier, total - 1)

    def copy(p):
        return pltpu.make_async_remote_copy(
            src_ref=x_ref,
            dst_ref=slots.at[me],
            send_sem=send.at[p],
            recv_sem=recv.at[p],
            device_id=device(p),
            device_id_type=MESH,
        )

    def start(p, carry):
        copy(p).start()
        return carry

    def finish(p, carry):
        copy(p).wait()
        return carry

    lax.fori_loop(1, total, start, 0)
    lax.fori_loop(1, total, finish, 0)
    o_ref[...] = lax.fori_loop(
        0, total, lambda i, acc: acc + slots[i], jnp.zeros(x_ref.shape, F32)
    )


def sum_all(values, dps, shards, number):
    total = dps * shards
    return pl.pallas_call(
        functools.partial(sum_body, dps, shards),
        in_specs=[pl.BlockSpec(memory_space=pltpu.VMEM)],
        out_specs=pl.BlockSpec(memory_space=pltpu.VMEM),
        out_shape=jax.ShapeDtypeStruct(values.shape, F32),
        scratch_shapes=[
            pltpu.VMEM((total,) + values.shape, F32),
            pltpu.SemaphoreType.DMA((total,)),
            pltpu.SemaphoreType.DMA((total,)),
        ],
        compiler_params=pltpu.CompilerParams(collective_id=number, has_side_effects=True),
        name="sum_all",
    )(values)


def after(value, *others):
    return lax.optimization_barrier((value,) + others)[0]


def inverse_rms(values):
    return lax.rsqrt(jnp.mean(values * values, axis=-1, keepdims=True) + EPS)


def norm_back(values, inverse, gain, grad_normed):
    scaled = grad_normed * gain
    gain_grad = jnp.sum(grad_normed * values * inverse, axis=0)
    grad_values = inverse * scaled - values * inverse**3 * jnp.mean(
        scaled * values, axis=-1, keepdims=True
    )
    return (gain_grad, grad_values)


def build(dps, shards):
    total = dps * shards
    axes = ("dp", "shard")
    zgroups = [[i for i in range(dps) if i % 2 == p] for p in (0, 1)]

    def swap(values, dx, ds):
        pairs = [
            (i, ((i // shards) ^ dx) * shards + ((i % shards) ^ ds)) for i in range(total)
        ]
        return lax.ppermute(values, axes, pairs)

    def gather(piece):
        return lax.all_gather(piece, "dp", axis=0, tiled=True, axis_index_groups=zgroups)

    def scatter(whole):
        return lax.psum_scatter(
            whole, "dp", scatter_dimension=0, tiled=True, axis_index_groups=zgroups
        )

    def sum_to_owner(partial):
        even = partial[:, 0::2]
        odd = partial[:, 1::2].astype(BF)
        paired = even.astype(F32) + swap(odd, 0, 1).astype(F32)
        low = paired.astype(BF)
        from_y = swap(low[0, 1], 0, 2)
        from_x = swap(low[1, 0], 1, 0)
        from_d = swap(low[1, 1], 1, 2)
        return paired[0, 0] + from_y.astype(F32) + from_x.astype(F32) + from_d.astype(F32)

    def spread(own):
        from_y = swap(own, 0, 2)
        from_x = swap(own, 1, 0)
        from_d = swap(own, 1, 2)
        mine = jnp.stack([own, from_y, from_x, from_d])
        theirs = swap(mine, 0, 1)
        return jnp.stack([mine, theirs], axis=1).reshape((2, shards) + own.shape)

    def on_device(
        tokens,
        block_ids,
        cotangent,
        gain_first,
        w_query,
        w_key,
        w_value,
        w_output,
        gain_second,
        w_gate,
        w_up,
        w_down,
        moment_first,
        moment_query,
        moment_key,
        moment_value,
        moment_output,
        moment_second,
        moment_gate,
        moment_up,
        moment_down,
        step,
        rate,
    ):
        length = block_ids.shape[1]
        width = tokens.shape[1]
        group = H // KV
        dp = lax.axis_index("dp")
        me = lax.axis_index("shard")
        x = lax.rem(dp, 2)
        quarter = length // shards
        rows = w_query.shape[0]

        def half(values, which):
            size = values.shape[1] // 2
            return lax.dynamic_slice_in_dim(values, which * size, size, axis=1)

        def ordered(mine, theirs, axis=0):
            first = jnp.where(x == 0, mine, theirs)
            second = jnp.where(x == 0, theirs, mine)
            return jnp.concatenate([first, second], axis=axis)

        low_q = w_query.astype(BF)
        low_k = w_key.astype(BF)
        low_v = w_value.astype(BF)
        low_o = w_output.astype(BF).T
        low_g = w_gate.astype(BF)
        low_u = w_up.astype(BF)
        low_d = w_down.astype(BF).T

        def attn_half(which):
            return jnp.concatenate([half(low_q, which), half(low_k, which), half(low_v, which)], axis=1)

        cols = low_q.shape[1] // 2 + low_k.shape[1]
        gains = jnp.stack([gain_first, gain_second]).astype(BF)
        gains = jnp.pad(gains, ((0, 14), (0, cols - rows)))
        sent = swap(jnp.concatenate([attn_half(1 - x), gains], axis=0), 1, 0)
        piece = jnp.concatenate(
            [ordered(attn_half(x), sent[:rows]), ordered(gains, sent[rows:])], axis=0
        )
        groups = dps // 2
        packed = gather(piece).reshape(groups, 2 * rows + 32, cols)
        qkv_weight = packed[:, : 2 * rows].reshape(width, cols)
        tails = packed[:, 2 * rows :].reshape(groups, 2, 16, cols)
        gain_one = tails[:, :, 0, :rows].reshape(1, width).astype(F32)
        gain_two = tails[:, :, 1, :rows].reshape(1, width).astype(F32)

        tokens_mine = lax.dynamic_slice_in_dim(tokens, me * quarter, quarter, axis=0)
        tokens_x = swap(after(tokens_mine, sent), 1, 0)
        out_x = swap(after(half(low_o, 1 - x), sent), 1, 0)
        out_weight = gather(ordered(half(low_o, x), out_x))
        size = low_g.shape[1] // 2 // CHUNKS

        def ffn_part(which, j):
            return jnp.concatenate(
                [half(low, which)[:, j * size : (j + 1) * size] for low in (low_g, low_u, low_d)],
                axis=1,
            )

        ffn_weights = []
        previous = (tokens_x, out_x)
        for j in range(CHUNKS):
            ffn_x = swap(after(ffn_part(1 - x, j), *previous), 1, 0)
            previous = (ffn_x,)
            ffn_weights.append(gather(ordered(ffn_part(x, j), ffn_x)))

        def natural_index(values):
            return jnp.concatenate(
                [
                    lax.dynamic_index_in_dim(values, me ^ q, axis=0, keepdims=False)
                    for q in range(shards)
                ],
                axis=0,
            )

        def rest_of(from_x):
            from_xy = swap(from_x, 0, 2)
            pair = jnp.stack([from_x, from_xy])
            return jnp.stack([pair, swap(pair, 0, 1)], axis=1).reshape((shards,) + from_x.shape)

        both = jnp.concatenate([tokens, natural_index(rest_of(tokens_x))], axis=0)
        blocks = jnp.concatenate([block_ids, swap(block_ids, 1, 0)], axis=0)
        block_rows = blocks[:, None, :]
        block_cols = blocks.reshape(2 * length, 1)

        def to_relative(values):
            values = values.reshape(2, length, values.shape[-1])
            parts = [
                lax.dynamic_slice_in_dim(values, (me ^ ds) * quarter, quarter, axis=1)
                for ds in range(shards)
            ]
            return jnp.stack(parts, axis=1)

        def to_natural(values):
            parts = [
                lax.dynamic_index_in_dim(values, me ^ q, axis=1, keepdims=False)
                for q in range(shards)
            ]
            return jnp.concatenate(parts, axis=1)

        cot_own = jnp.stack(
            [
                lax.dynamic_slice_in_dim(cotangent, (me ^ ds) * quarter, quarter, axis=0)
                for ds in range(shards)
            ]
        )
        cot_x = swap(after(cot_own[0], *previous), 1, 0)
        cot_rel = jnp.concatenate([cot_own, rest_of(cot_x)], axis=0).reshape(2 * length, width)

        cosine, sine = rope_tables(length, group)
        normed, query, key, value = qkv(both, gain_one, qkv_weight, cosine, sine, group)
        mixed, lse = attend(query, key, value, block_rows, block_cols, length)
        mixed_rel = to_relative(mixed).reshape(2 * length, group * HD)
        partial = jnp.einsum("tk,dk->td", mixed_rel, out_weight, preferred_element_type=F32)
        summed = sum_to_owner(partial.astype(BF).reshape(2, shards, quarter, width))
        tokens_own = lax.dynamic_slice_in_dim(tokens, me * quarter, quarter, axis=0).astype(F32)
        hidden = tokens_own + summed
        inverse_second = inverse_rms(hidden)
        normed_two_own = (hidden * inverse_second * gain_two).astype(BF)
        normed_two = spread(normed_two_own).reshape(2 * length, width)

        shape = (2, shards, quarter, width)
        grads_ffn = []
        acts = []
        partial_two = None
        for j in range(CHUNKS):
            last = j == CHUNKS - 1
            act, grad_gu, partial_two = up_back(
                normed_two, cot_rel, ffn_weights[j], partial_two, last
            )
            acts.append(act)
            grads_ffn.append(scatter(ffn_grads(normed_two, cot_rel, grad_gu, act)))
        grad_normed_two = sum_to_owner(partial_two.reshape(shape))
        cot_mine = cot_own[0].astype(F32)
        gain_grad_two, grad_through = norm_back(hidden, inverse_second, gain_two, grad_normed_two)
        grad_hidden = cot_mine + grad_through
        grad_hidden_rel = spread(grad_hidden.astype(BF)).reshape(2 * length, width)

        def to_sequence(own):
            from_y = swap(own, 0, 2)
            mine = jnp.stack([own, from_y])
            theirs = swap(mine, 0, 1)
            rel = jnp.stack([mine, theirs], axis=1).reshape((1, shards) + own.shape)
            return to_natural(rel)[0]

        result = after(down(acts, ffn_weights), grad_hidden_rel)
        output_own = (hidden + sum_to_owner(result.reshape(shape))).astype(BF)
        output = to_sequence(output_own)

        d_out = jnp.einsum("td,tk->dk", grad_hidden_rel, mixed_rel, preferred_element_type=F32)
        grad_out = scatter(d_out.astype(BF))
        grad_mixed = jnp.dot(grad_hidden_rel, out_weight, preferred_element_type=F32).astype(BF)
        grad_mixed = to_natural(grad_mixed.reshape(2, shards, quarter, group * HD))
        grad_q, grad_kv = attend_back(
            query,
            key,
            value,
            block_rows,
            block_cols,
            lse,
            grad_mixed.reshape(2 * length, group * HD),
            cosine,
            sine,
            length,
        )
        grad_qkv = jnp.concatenate([grad_q, grad_kv], axis=1)
        d_qkv = jnp.einsum(
            "tc,tk->ck", normed, grad_qkv, preferred_element_type=F32
        ).astype(BF)
        grad_qkv_w = scatter(d_qkv)
        partial_one = jnp.einsum(
            "tk,ck->tc",
            after(to_relative(grad_qkv).reshape(2 * length, cols), d_qkv),
            qkv_weight,
            preferred_element_type=F32,
        )
        grad_normed = sum_to_owner(partial_one.astype(BF).reshape(shape))
        inverse_own = inverse_rms(tokens_own)
        gain_grad_one, grad_inner = norm_back(tokens_own, inverse_own, gain_one, grad_normed)
        input_grad = to_sequence((grad_hidden + grad_inner).astype(BF)).astype(F32)

        def owned_halves(piece):
            keep = lax.dynamic_slice_in_dim(piece, x * rows, rows, axis=0)
            send = lax.dynamic_slice_in_dim(piece, (1 - x) * rows, rows, axis=0)
            return keep, swap(send, 1, 0)

        def joined(mine, theirs):
            return ordered(mine, theirs, axis=1).astype(F32)

        mine, theirs = owned_halves(grad_qkv_w)
        qc = group * HD
        own_q = joined(mine[:, :qc], theirs[:, :qc])
        own_k = joined(mine[:, qc : qc + HD], theirs[:, qc : qc + HD])
        own_v = joined(mine[:, qc + HD :], theirs[:, qc + HD :])
        mine, theirs = owned_halves(grad_out)
        own_o = joined(mine, theirs).T
        pairs = [owned_halves(piece) for piece in grads_ffn]
        own_gud = []
        for part in range(3):
            cut = slice(part * size, (part + 1) * size)
            own_gud.append(
                joined(
                    jnp.concatenate([m[:, cut] for m, t in pairs], axis=1),
                    jnp.concatenate([t[:, cut] for m, t in pairs], axis=1),
                )
            )
        own_g, own_u, own_d = own_gud[0], own_gud[1], own_gud[2].T
        gain_grads = sum_all(
            jnp.stack([gain_grad_one, gain_grad_two]).reshape(-1, 128), dps, shards, 1
        ).reshape(2, width)
        gain_grads = lax.dynamic_slice_in_dim(gain_grads, dp * rows, rows, axis=1)
        owned = (gain_grads[0], own_q, own_k, own_v, own_o, gain_grads[1], own_g, own_u, own_d)

        first_shard = (me == 0).astype(F32)
        squares = first_shard * (jnp.sum(owned[0] * owned[0]) + jnp.sum(owned[5] * owned[5]))
        for position in (1, 2, 3, 4, 6, 7, 8):
            squares = squares + jnp.sum(owned[position] * owned[position])
        squares = sum_all(jnp.broadcast_to(squares, (8, 128)), dps, shards, 2)
        global_norm = jnp.sqrt(squares[0, 0])
        factor = jnp.minimum(1.0, CLIP / global_norm)
        rate_now = rate * jnp.minimum(1.0, (step.astype(F32) + 1.0) / WARMUP)
        masters = (gain_first, w_query, w_key, w_value, w_output, gain_second, w_gate, w_up, w_down)
        moments = (
            moment_first,
            moment_query,
            moment_key,
            moment_value,
            moment_output,
            moment_second,
            moment_gate,
            moment_up,
            moment_down,
        )
        momenta = [
            0.5 * moment + 0.5 * (factor * gradient) for moment, gradient in zip(moments, owned)
        ]
        updated = [master - rate_now * momentum for master, momentum in zip(masters, momenta)]
        return (output, input_grad, global_norm, *momenta, *updated)

    return on_device


def solution(mesh):
    rows, both, back = P("dp"), P("dp", "shard"), P("shard", "dp")
    tokens = P("dp", None)
    params = (rows, both, both, both, back, rows, both, both, back)
    in_specs = (tokens, tokens, tokens, *params, *params, P(), P())
    out_specs = (tokens, tokens, P(), *params, *params)
    return jax.shard_map(
        build(mesh.shape["dp"], mesh.shape["shard"]),
        mesh=mesh,
        in_specs=in_specs,
        out_specs=out_specs,
        check_vma=False,
    )
```

```python
import functools

import jax
import jax.numpy as jnp
from jax import lax
from jax.experimental import pallas as pl
from jax.experimental.pallas import tpu as pltpu
from jax.sharding import PartitionSpec as P

H = 32
KV = 8
CLIP = 4096
WARMUP = 2000
THETA = 10000000.0
CHUNKS = 2
MESH = pl.DeviceIdType.MESH


BF = jnp.bfloat16
F32 = jnp.float32
HD = 64
EPS = 1e-05
NEGATIVE = -1e30
VMEM = 48 << 20

def dot(a, b, ca, cb):
    return lax.dot_general(a, b, (((ca,), (cb,)), ((), ())), preferred_element_type=F32)

def swap_halves(v):
    n = v.shape[1]
    lane = lax.broadcasted_iota(jnp.int32, v.shape, 1)
    return jnp.where(lane % HD < HD // 2, pltpu.roll(v, n - HD // 2, 1), pltpu.roll(v, HD // 2, 1))

def qkv_body(tok_ref, gain_ref, w_ref, cos_ref, sin_ref, normed_ref, q_ref, k_ref, v_ref):
    x = tok_ref[...].astype(F32)
    inv = lax.rsqrt(jnp.mean(x * x, axis=1, keepdims=True) + EPS)
    normed = (x * inv * gain_ref[...]).astype(BF)
    normed_ref[...] = normed
    lin = dot(normed, w_ref[...], 1, 0)
    heads = q_ref.shape[0]
    qc = heads * HD
    rot = lin * cos_ref[...] + swap_halves(lin) * sin_ref[...]
    for h in range(heads):
        q_ref[h] = (rot[:, h * HD : (h + 1) * HD]).astype(BF)
    k_ref[...] = rot[:, qc : qc + HD].astype(BF)
    v_ref[...] = rot[:, qc + HD :].astype(BF)

def qkv(tokens, gain, weight, cos, sin, heads, tile=256):
    count, width = tokens.shape
    cols = weight.shape[1]
    length = cos.shape[0]
    per = length // tile
    full = lambda i: (0, 0)
    row = lambda i: (i, 0)
    return pl.pallas_call(
        qkv_body,
        grid=(count // tile,),
        in_specs=[
            pl.BlockSpec((tile, width), row),
            pl.BlockSpec((1, width), full),
            pl.BlockSpec((width, cols), full),
            pl.BlockSpec((tile, cols), lambda i: (i % per, 0)),
            pl.BlockSpec((tile, cols), lambda i: (i % per, 0)),
        ],
        out_specs=[
            pl.BlockSpec((tile, width), row),
            pl.BlockSpec((heads, tile, HD), lambda i: (0, i, 0)),
            pl.BlockSpec((tile, HD), row),
            pl.BlockSpec((tile, HD), row),
        ],
        out_shape=[
            jax.ShapeDtypeStruct((count, width), BF),
            jax.ShapeDtypeStruct((heads, count, HD), BF),
            jax.ShapeDtypeStruct((count, HD), BF),
            jax.ShapeDtypeStruct((count, HD), BF),
        ],
        compiler_params=pltpu.CompilerParams(vmem_limit_bytes=VMEM),
        cost_estimate=pl.CostEstimate(flops=2 * count * width * cols, bytes_accessed=4 * count * width, transcendentals=0),
        name="qkv_rope",
    )(tokens, gain, weight, cos, sin)

def fwd_body(limits, q_ref, k_ref, v_ref, brow_ref, bcol_ref, o_ref, lse_ref):
    heads, tile, _ = q_ref.shape
    i = pl.program_id(1)
    def run(keys):
        k = k_ref[:keys]
        v = v_ref[:keys]
        allowed = brow_ref[0][:, :keys] <= bcol_ref[...]
        outs = []
        lses = []
        for h in range(heads):
            s = dot(q_ref[h] * BF(0.125), k, 1, 1)
            s = jnp.where(allowed, s, NEGATIVE)
            m = jnp.max(s, axis=1, keepdims=True)
            p = jnp.exp(s - m)
            l = jnp.sum(p, axis=1, keepdims=True)
            o = dot(p.astype(BF), v, 1, 0) / l
            outs.append(o.astype(BF))
            lses.append(m + jnp.log(l))
        o_ref[...] = jnp.concatenate(outs, axis=1)
        lse_ref[...] = jnp.concatenate(lses, axis=1)
    for n, keys in enumerate(limits):
        @pl.when(i == n)
        def _(keys=keys):
            run(keys)

def attend(q, k, v, brow, bcol, length, tile=256, most=256):
    heads, count, _ = q.shape
    seqs = count // length
    per = length // tile
    limits = tuple(min(length, (n + 1) * tile + most) for n in range(per))
    return pl.pallas_call(
        functools.partial(fwd_body, limits),
        grid=(seqs, per),
        in_specs=[
            pl.BlockSpec((heads, tile, HD), lambda b, i: (0, b * per + i, 0)),
            pl.BlockSpec((length, HD), lambda b, i: (b, 0)),
            pl.BlockSpec((length, HD), lambda b, i: (b, 0)),
            pl.BlockSpec((1, 1, length), lambda b, i: (b, 0, 0)),
            pl.BlockSpec((tile, 1), lambda b, i: (b * per + i, 0)),
        ],
        out_specs=[
            pl.BlockSpec((tile, heads * HD), lambda b, i: (b * per + i, 0)),
            pl.BlockSpec((tile, heads), lambda b, i: (b * per + i, 0)),
        ],
        out_shape=[
            jax.ShapeDtypeStruct((count, heads * HD), BF),
            jax.ShapeDtypeStruct((count, heads), F32),
        ],
        compiler_params=pltpu.CompilerParams(vmem_limit_bytes=VMEM),
        cost_estimate=pl.CostEstimate(flops=4 * heads * count * length * HD * 4, bytes_accessed=count * 2048, transcendentals=heads * count * length),
        name="attend",
    )(q, k, v, brow, bcol)

def bwd_body(limits, q_ref, k_ref, v_ref, brow_ref, bcol_ref, lse_ref, do_ref, cos_ref, sin_ref, kcos_ref, ksin_ref, dq_ref, dkv_ref, dk_acc, dv_acc):
    heads, tile, _ = q_ref.shape
    i = pl.program_id(1)
    @pl.when(i == 0)
    def _():
        dk_acc[...] = jnp.zeros_like(dk_acc)
        dv_acc[...] = jnp.zeros_like(dv_acc)
    def run(keys):
        k = k_ref[:keys]
        v = v_ref[:keys]
        allowed = brow_ref[0][:, :keys] <= bcol_ref[...]
        dqs = []
        dk = jnp.zeros((HD, keys), F32)
        dv = jnp.zeros((HD, keys), F32)
        for h in range(heads):
            q = q_ref[h] * BF(0.125)
            do = do_ref[:, h * HD : (h + 1) * HD]
            s = dot(q, k, 1, 1)
            s = jnp.where(allowed, s, NEGATIVE)
            p = jnp.exp(s - lse_ref[:, h : h + 1])
            dp = dot(do, v, 1, 1)
            pdp = p * dp
            delta = jnp.sum(pdp, axis=1, keepdims=True)
            ds = (pdp - p * delta).astype(BF)
            dqs.append(dot(ds, k, 1, 0) * 0.125)
            dk = dk + dot(q, ds, 0, 0)
            dv = dv + dot(do, p.astype(BF), 0, 0)
        dk_acc[:, :keys] += dk
        dv_acc[:, :keys] += dv
        dq = jnp.concatenate(dqs, axis=1)
        dq_ref[...] = (dq * cos_ref[...] - swap_halves(dq) * sin_ref[...]).astype(BF)
    for n, keys in enumerate(limits):
        @pl.when(i == n)
        def _(keys=keys):
            run(keys)
    @pl.when(i == len(limits) - 1)
    def _():
        both = jnp.concatenate([dk_acc[...], dv_acc[...]], axis=0).T
        dkv_ref[...] = (both * kcos_ref[...] - swap_halves(both) * ksin_ref[...]).astype(BF)

def attend_back(q, k, v, brow, bcol, lse, do, cos, sin, length, tile=256, most=256):
    heads, count, _ = q.shape
    seqs = count // length
    per = length // tile
    qc = heads * HD
    limits = tuple(min(length, (n + 1) * tile + most) for n in range(per))
    rowm = lambda b, i: (b * per + i, 0)
    return pl.pallas_call(
        functools.partial(bwd_body, limits),
        grid=(seqs, per),
        in_specs=[
            pl.BlockSpec((heads, tile, HD), lambda b, i: (0, b * per + i, 0)),
            pl.BlockSpec((length, HD), lambda b, i: (b, 0)),
            pl.BlockSpec((length, HD), lambda b, i: (b, 0)),
            pl.BlockSpec((1, 1, length), lambda b, i: (b, 0, 0)),
            pl.BlockSpec((tile, 1), rowm),
            pl.BlockSpec((tile, heads), rowm),
            pl.BlockSpec((tile, qc), rowm),
            pl.BlockSpec((tile, qc), lambda b, i: (i, 0)),
            pl.BlockSpec((tile, qc), lambda b, i: (i, 0)),
            pl.BlockSpec((length, 2 * HD), lambda b, i: (0, qc // (2 * HD))),
            pl.BlockSpec((length, 2 * HD), lambda b, i: (0, qc // (2 * HD))),
        ],
        out_specs=[
            pl.BlockSpec((tile, qc), rowm),
            pl.BlockSpec((length, 2 * HD), lambda b, i: (b, 0)),
        ],
        out_shape=[
            jax.ShapeDtypeStruct((count, qc), BF),
            jax.ShapeDtypeStruct((count, 2 * HD), BF),
        ],
        scratch_shapes=[pltpu.VMEM((HD, length), F32), pltpu.VMEM((HD, length), F32)],
        compiler_params=pltpu.CompilerParams(vmem_limit_bytes=VMEM),
        cost_estimate=pl.CostEstimate(flops=10 * heads * count * length * HD * 4, bytes_accessed=count * 4096, transcendentals=heads * count * length),
        name="attend_back",
    )(q, k, v, brow, bcol, lse, do, cos, sin, cos, sin)

def rope_tables(length, heads):
    positions = jnp.arange(length, dtype=jnp.int32).astype(F32)
    powers = -2.0 * jnp.arange(HD // 2, dtype=F32) / HD
    angles = positions[:, None] * jnp.power(THETA, powers)[None, :]
    c = jnp.cos(angles); s = jnp.sin(angles)
    cos = jnp.concatenate([jnp.tile(jnp.concatenate([c, c], axis=1), (1, heads + 1)), jnp.ones((length, HD), F32)], axis=1)
    sin = jnp.concatenate([jnp.tile(jnp.concatenate([-s, s], axis=1), (1, heads + 1)), jnp.zeros((length, HD), F32)], axis=1)
    return cos, sin

def up_body(first, last, n2_ref, cot_ref, w_ref, *rest):
    if first:
        act_ref, dgu_ref, part_ref = rest
    else:
        prev_ref, act_ref, dgu_ref, part_ref = rest
    size = act_ref.shape[1]
    gu = dot(n2_ref[...], w_ref[:, : 2 * size], 1, 0)
    da = dot(cot_ref[...], w_ref[:, 2 * size :], 1, 0)
    gate, up = gu[:, :size], gu[:, size:]
    sig = 1.0 / (1.0 + jnp.exp(-gate))
    gs = gate * sig
    act_ref[...] = (gs * up).astype(BF)
    dg = (da * up * sig * (1.0 + gate * (1.0 - sig))).astype(BF)
    du = (da * gs).astype(BF)
    dgu = jnp.concatenate([dg, du], axis=1)
    dgu_ref[...] = dgu
    part = dot(dgu, w_ref[:, : 2 * size], 1, 1)
    if not first:
        part = part + prev_ref[...]
    part_ref[...] = part.astype(part_ref.dtype)

def up_back(n2, cot, weight, prev, last, tile=256):
    count, width = n2.shape
    size = weight.shape[1] // 3
    row = lambda i: (i, 0)
    full = lambda i: (0, 0)
    ins = [n2, cot, weight] + ([] if prev is None else [prev])
    specs = [pl.BlockSpec((tile, width), row), pl.BlockSpec((tile, width), row), pl.BlockSpec((width, 3 * size), full, pipeline_mode=pl.Buffered(1))]
    if prev is not None:
        specs.append(pl.BlockSpec((tile, width), row))
    return pl.pallas_call(
        functools.partial(up_body, prev is None, last),
        grid=(count // tile,),
        in_specs=specs,
        out_specs=[pl.BlockSpec((tile, size), row), pl.BlockSpec((tile, 2 * size), row), pl.BlockSpec((tile, width), row)],
        out_shape=[jax.ShapeDtypeStruct((count, size), BF), jax.ShapeDtypeStruct((count, 2 * size), BF), jax.ShapeDtypeStruct((count, width), BF if last else F32)],
        compiler_params=pltpu.CompilerParams(vmem_limit_bytes=VMEM),
        cost_estimate=pl.CostEstimate(flops=2 * count * width * size * 5, bytes_accessed=12 * count * width, transcendentals=count * size),
        name="swiglu_part",
    )(*ins)

def grad_body(n2a, n2b, cota, cotb, dgua, dgub, acta, actb, o_ref):
    size = acta.shape[1]
    gu = dot(n2a[...], dgua[...], 0, 0) + dot(n2b[...], dgub[...], 0, 0)
    o_ref[:, : 2 * size] = gu.astype(BF)
    dt = dot(cota[...], acta[...], 0, 0) + dot(cotb[...], actb[...], 0, 0)
    o_ref[:, 2 * size :] = dt.astype(BF)


def ffn_grads(n2, cot, dgu, act, tile=256):
    count, width = n2[0].shape
    size = act[0].shape[1]
    col = lambda i: (0, i)
    full = lambda i: (0, 0)
    return pl.pallas_call(
        grad_body,
        grid=(width // tile,),
        in_specs=[pl.BlockSpec((count, tile), col)] * 4
        + [pl.BlockSpec((count, 2 * size), full, pipeline_mode=pl.Buffered(1))] * 2
        + [pl.BlockSpec((count, size), full, pipeline_mode=pl.Buffered(1))] * 2,
        out_specs=pl.BlockSpec((tile, 3 * size), lambda i: (i, 0)),
        out_shape=jax.ShapeDtypeStruct((width, 3 * size), BF),
        compiler_params=pltpu.CompilerParams(vmem_limit_bytes=VMEM),
        cost_estimate=pl.CostEstimate(
            flops=4 * count * width * size * 3,
            bytes_accessed=16 * count * width,
            transcendentals=0,
        ),
        name="swiglu_grads",
    )(*n2, *cot, *dgu, *act)


def out_body(*refs):
    count = len(refs) // 2
    total = dot(refs[0][...], refs[count][...], 1, 1)
    for j in range(1, count):
        total = total + dot(refs[j][...], refs[count + j][...], 1, 1)
    refs[-1][...] = total.astype(BF)


def down(acts, weights, tile=256):
    count, size = acts[0].shape
    width = weights[0].shape[0]
    row = lambda i: (i, 0)
    return pl.pallas_call(
        out_body,
        grid=(count // tile,),
        in_specs=[pl.BlockSpec((tile, size), row) for _ in acts]
        + [
            pl.BlockSpec((width, size), lambda i: (0, 2), pipeline_mode=pl.Buffered(1))
            for _ in weights
        ],
        out_specs=pl.BlockSpec((tile, width), row),
        out_shape=jax.ShapeDtypeStruct((count, width), BF),
        compiler_params=pltpu.CompilerParams(vmem_limit_bytes=VMEM),
        cost_estimate=pl.CostEstimate(
            flops=2 * count * width * size * len(acts),
            bytes_accessed=8 * count * width,
            transcendentals=0,
        ),
        name="swiglu_down",
    )(*acts, *weights)


def sum_body(dps, shards, x_ref, o_ref, slots, send, recv):
    total = dps * shards
    me = lax.axis_index("dp") * shards + lax.axis_index("shard")
    barrier = pltpu.get_barrier_semaphore()

    def device(p):
        target = lax.rem(me + p, total)
        return (target // shards, lax.rem(target, shards))

    def greet(p, carry):
        pl.semaphore_signal(barrier, inc=1, device_id=device(p), device_id_type=MESH)
        return carry

    lax.fori_loop(1, total, greet, 0)
    slots[me] = x_ref[...]
    pl.semaphore_wait(barrier, total - 1)

    def copy(p):
        return pltpu.make_async_remote_copy(
            src_ref=x_ref,
            dst_ref=slots.at[me],
            send_sem=send.at[p],
            recv_sem=recv.at[p],
            device_id=device(p),
            device_id_type=MESH,
        )

    def start(p, carry):
        copy(p).start()
        return carry

    def finish(p, carry):
        copy(p).wait()
        return carry

    lax.fori_loop(1, total, start, 0)
    lax.fori_loop(1, total, finish, 0)
    o_ref[...] = lax.fori_loop(
        0, total, lambda i, acc: acc + slots[i], jnp.zeros(x_ref.shape, F32)
    )


def sum_all(values, dps, shards, number):
    total = dps * shards
    return pl.pallas_call(
        functools.partial(sum_body, dps, shards),
        in_specs=[pl.BlockSpec(memory_space=pltpu.VMEM)],
        out_specs=pl.BlockSpec(memory_space=pltpu.VMEM),
        out_shape=jax.ShapeDtypeStruct(values.shape, F32),
        scratch_shapes=[
            pltpu.VMEM((total,) + values.shape, F32),
            pltpu.SemaphoreType.DMA((total,)),
            pltpu.SemaphoreType.DMA((total,)),
        ],
        compiler_params=pltpu.CompilerParams(collective_id=number, has_side_effects=True),
        name="sum_all",
    )(values)


def after(*values):
    return lax.optimization_barrier(values)


def inverse_rms(values):
    return lax.rsqrt(jnp.mean(values * values, axis=-1, keepdims=True) + EPS)


def norm_back(values, inverse, gain, grad_normed):
    scaled = grad_normed * gain
    gain_grad = jnp.sum(grad_normed * values * inverse, axis=0)
    grad_values = inverse * scaled - values * inverse**3 * jnp.mean(
        scaled * values, axis=-1, keepdims=True
    )
    return (gain_grad, grad_values)


def build(dps, shards):
    total = dps * shards
    axes = ("dp", "shard")
    zgroups = [[i for i in range(dps) if i % 2 == p] for p in (0, 1)]

    def swap(values, dx, ds):
        pairs = [
            (i, ((i // shards) ^ dx) * shards + ((i % shards) ^ ds)) for i in range(total)
        ]
        return lax.ppermute(values, axes, pairs)

    def gather(piece):
        return lax.all_gather(piece, "dp", axis=0, tiled=True, axis_index_groups=zgroups)

    def scatter(whole):
        return lax.psum_scatter(
            whole, "dp", scatter_dimension=0, tiled=True, axis_index_groups=zgroups
        )


    def sum_to_owner(even, odd, between=None):
        got = swap(odd, 0, 1)

        def pair(k):
            return even[k].astype(F32) + got[k].astype(F32)

        from_d = swap(pair(3).astype(BF), 1, 2)
        from_y = swap(pair(1).astype(BF), 0, 2)
        from_x = swap(pair(2).astype(BF), 1, 0)
        filler = None
        if between is not None:
            filler = between(got)
            from_d, from_y, from_x, filler = after(from_d, from_y, from_x, filler)
        result = pair(0) + from_y.astype(F32) + from_x.astype(F32) + from_d.astype(F32)
        return result if between is None else (result, filler)

    def spread(own, between=None):
        from_d = swap(own, 1, 2)
        from_y = swap(own, 0, 2)
        from_x = swap(own, 1, 0)
        if between is not None:
            filler = between(own)
            from_d, from_y, from_x, filler = after(from_d, from_y, from_x, filler)
            mine = jnp.stack([own, from_y, from_x, from_d])
            return mine, swap(mine, 0, 1), filler
        mine = jnp.stack([own, from_y, from_x, from_d])
        return mine, swap(mine, 0, 1)

    def on_device(
        tokens,
        block_ids,
        cotangent,
        gain_first,
        w_query,
        w_key,
        w_value,
        w_output,
        gain_second,
        w_gate,
        w_up,
        w_down,
        moment_first,
        moment_query,
        moment_key,
        moment_value,
        moment_output,
        moment_second,
        moment_gate,
        moment_up,
        moment_down,
        step,
        rate,
    ):
        length = block_ids.shape[1]
        width = tokens.shape[1]
        group = H // KV
        dp = lax.axis_index("dp")
        me = lax.axis_index("shard")
        x = lax.rem(dp, 2)
        quarter = length // shards
        rows = w_query.shape[0]

        def half(values, which):
            size = values.shape[1] // 2
            return lax.dynamic_slice_in_dim(values, which * size, size, axis=1)

        def ordered(mine, theirs, axis=0):
            first = jnp.where(x == 0, mine, theirs)
            second = jnp.where(x == 0, theirs, mine)
            return jnp.concatenate([first, second], axis=axis)

        def natural(parts):
            stacked = jnp.stack(parts)
            return jnp.concatenate(
                [
                    lax.dynamic_index_in_dim(stacked, me ^ q, axis=0, keepdims=False)
                    for q in range(shards)
                ],
                axis=0,
            )

        def cut(values, ds):
            return lax.dynamic_slice_in_dim(values, (me ^ ds) * quarter, quarter, axis=0)

        def halves(own, other):
            return [
                jnp.stack([cut(own, dc), cut(own, dc + 2), cut(other, dc), cut(other, dc + 2)])
                for dc in (0, 1)
            ]

        def streams(mine, theirs):
            return [
                natural([mine[k], theirs[k], mine[k + 1], theirs[k + 1]]) for k in (0, 2)
            ]

        def flat(values):
            return values.reshape(-1, values.shape[-1])

        low_q = w_query.astype(BF)
        low_k = w_key.astype(BF)
        low_v = w_value.astype(BF)

        def attn_half(which):
            return jnp.concatenate(
                [half(low_q, which), half(low_k, which), half(low_v, which)], axis=1
            )

        cols = low_q.shape[1] // 2 + low_k.shape[1]
        gains = jnp.stack([gain_first, gain_second]).astype(BF)
        gains = jnp.pad(gains, ((0, 14), (0, cols - rows)))
        sent = swap(jnp.concatenate([attn_half(1 - x), gains], axis=0), 1, 0)
        piece = jnp.concatenate(
            [ordered(attn_half(x), sent[:rows]), ordered(gains, sent[rows:])], axis=0
        )
        groups = dps // 2
        packed = gather(piece).reshape(groups, 2 * rows + 32, cols)
        qkv_weight = packed[:, : 2 * rows].reshape(width, cols)
        tails = packed[:, 2 * rows :].reshape(groups, 2, 16, cols)
        gain_one = tails[:, :, 0, :rows].reshape(1, width).astype(F32)
        gain_two = tails[:, :, 1, :rows].reshape(1, width).astype(F32)

        low_o, w_g, w_u, w_d = after((w_output, w_gate, w_up, w_down), sent)[0]
        low_o = low_o.astype(BF).T
        low_g = w_g.astype(BF)
        low_u = w_u.astype(BF)
        low_d = w_d.astype(BF).T
        tokens_x = swap(after(cut(tokens, 0), sent)[0], 1, 0)
        blocks_x = swap(block_ids, 1, 0)
        out_x = swap(half(low_o, 1 - x), 1, 0)
        size = low_g.shape[1] // 2 // CHUNKS

        def ffn_part(which, j):
            return jnp.concatenate(
                [half(low, which)[:, j * size : (j + 1) * size] for low in (low_g, low_u, low_d)],
                axis=1,
            )

        def rest_of(from_x):
            from_xy = swap(from_x, 0, 2)
            other = swap(jnp.stack([from_x, from_xy]), 0, 1)
            return [from_x, other[0], from_xy, other[1]]

        out_weight = gather(ordered(half(low_o, x), out_x))
        send_first, _, _ = after(ffn_part(1 - x, 0), tokens_x, out_x)
        first_x = swap(send_first, 1, 0)
        ffn_weights = [gather(ordered(ffn_part(x, 0), first_x))]
        cot_x = swap(after(cut(cotangent, 0), first_x)[0], 1, 0)
        second_x = swap(after(ffn_part(1 - x, 1), cot_x)[0], 1, 0)
        ffn_weights.append(gather(ordered(ffn_part(x, 1), second_x)))

        cosine, sine = rope_tables(length, group)

        def forward(own_tokens, own_blocks):
            normed, query, key, value = qkv(own_tokens, gain_one, qkv_weight, cosine, sine, group)
            block_rows = own_blocks[:, None, :]
            block_cols = own_blocks.reshape(length, 1)
            mixed, lse = attend(query, key, value, block_rows, block_cols, length)
            return normed, mixed, (query, key, value, block_rows, block_cols, lse)

        normed_own, mixed_own, saved_own = forward(tokens, block_ids)
        other_tokens = natural(rest_of(tokens_x))
        other_tokens, _, _ = after(other_tokens, cot_x, mixed_own)
        normed_other, mixed_other, saved_other = forward(other_tokens, blocks_x)
        cot_rest = rest_of(cot_x)
        mixed_own, mixed_other, cot_rest, second_x = after(
            mixed_own, mixed_other, cot_rest, second_x
        )
        cot_mine = flat(jnp.stack([cut(cotangent, 0), cut(cotangent, 2), cot_rest[0], cot_rest[2]]))
        cot_theirs = flat(
            jnp.stack([cut(cotangent, 1), cut(cotangent, 3), cot_rest[1], cot_rest[3]])
        )
        mixed_mine, mixed_theirs = halves(mixed_own, mixed_other)

        def project(values, weight):
            partial = jnp.einsum("atk,dk->atd", values, weight, preferred_element_type=F32)
            return partial.astype(BF)

        summed = sum_to_owner(project(mixed_mine, out_weight), project(mixed_theirs, out_weight))
        tokens_own = cut(tokens, 0).astype(F32)
        hidden = tokens_own + summed
        inverse_second = inverse_rms(hidden)
        mine, theirs = spread((hidden * inverse_second * gain_two).astype(BF))
        two_mine, two_theirs = flat(mine), flat(theirs)

        shape = (4, quarter, width)
        acts_mine = []
        acts_theirs = []
        part_mine = part_theirs = None
        first_grads = None
        for j in range(CHUNKS):
            last = j == CHUNKS - 1
            weight = ffn_weights[j]
            theirs_in = two_theirs
            if first_grads is not None:
                theirs_in, first_grads = after(two_theirs, first_grads)
            act_theirs, gu_theirs, part_theirs = up_back(
                theirs_in, cot_theirs, weight, part_theirs, last
            )
            mine_in = two_mine
            if last:
                mine_in, part_theirs = after(two_mine, part_theirs)
            act_mine, gu_mine, part_mine = up_back(mine_in, cot_mine, weight, part_mine, last)
            acts_mine.append(act_mine)
            acts_theirs.append(act_theirs)

            def part_grads(token=None):
                gu = gu_mine if token is None else after(gu_mine, token)[0]
                return ffn_grads(
                    (two_mine, two_theirs),
                    (cot_mine, cot_theirs),
                    (gu, gu_theirs),
                    (act_mine, act_theirs),
                )

            if not last:
                first_grads = part_grads()
        grad_normed_two, last_grads = sum_to_owner(
            part_mine.reshape(shape), part_theirs.reshape(shape), part_grads
        )
        first_piece = scatter(first_grads)
        last_piece = scatter(last_grads)
        gain_grad_two, grad_through = norm_back(hidden, inverse_second, gain_two, grad_normed_two)
        grad_hidden = cut(cotangent, 0).astype(F32) + grad_through

        def outputs(token):
            return tuple(
                down([after(a, token)[0] for a in acts], ffn_weights)
                for acts in (acts_mine, acts_theirs)
            )

        gh_mine, gh_theirs, (out_mine, out_theirs) = spread(grad_hidden.astype(BF), outputs)

        def to_sequence(own):
            pair = jnp.stack([own, swap(own, 0, 2)])
            other = swap(pair, 0, 1)
            return natural([pair[0], other[0], pair[1], other[1]])

        grad_mixed_mine = project(gh_mine, out_weight.T)
        grad_mixed_theirs = project(gh_theirs, out_weight.T)
        grad_mixed = streams(grad_mixed_mine, grad_mixed_theirs)
        grad_mixed, first_piece = after(grad_mixed, first_piece)
        backs = [
            attend_back(*saved, grad_mixed[k], cosine, sine, length)
            for k, saved in enumerate((saved_own, saved_other))
        ]
        grad_qkv = [jnp.concatenate(pair, axis=1) for pair in backs]
        d_out = jnp.einsum("atd,atk->dk", gh_mine, mixed_mine, preferred_element_type=F32)
        d_out = d_out + jnp.einsum(
            "atd,atk->dk", gh_theirs, mixed_theirs, preferred_element_type=F32
        )
        grad_out = scatter(d_out.astype(BF))
        d_qkv = jnp.einsum("tc,tk->ck", normed_own, grad_qkv[0], preferred_element_type=F32)
        d_qkv = d_qkv + jnp.einsum(
            "tc,tk->ck", normed_other, grad_qkv[1], preferred_element_type=F32
        )
        d_qkv = d_qkv.astype(BF)
        grad_qkv_w = scatter(d_qkv)
        gq_mine, gq_theirs = halves(*grad_qkv)
        gq_mine, gq_theirs, _ = after(gq_mine, gq_theirs, d_qkv)
        grad_normed, last_piece = sum_to_owner(
            project(gq_mine, qkv_weight), project(gq_theirs, qkv_weight), lambda token: last_piece
        )

        out_theirs, _ = after(out_theirs, gh_theirs)
        output_own = hidden + sum_to_owner(out_mine.reshape(shape), out_theirs.reshape(shape))
        output = to_sequence(output_own.astype(BF))

        inverse_own = inverse_rms(tokens_own)
        gain_grad_one, grad_inner = norm_back(tokens_own, inverse_own, gain_one, grad_normed)
        input_grad = to_sequence((grad_hidden + grad_inner).astype(BF)).astype(F32)

        def owned_halves(piece):
            keep = lax.dynamic_slice_in_dim(piece, x * rows, rows, axis=0)
            send = lax.dynamic_slice_in_dim(piece, (1 - x) * rows, rows, axis=0)
            return keep, swap(send, 1, 0)

        def joined(mine, theirs):
            return ordered(mine, theirs, axis=1).astype(F32)

        first_piece, _ = after(first_piece, d_qkv)
        pairs = [owned_halves(first_piece), owned_halves(last_piece)]
        grad_out, pairs = after(grad_out, pairs)
        mine, theirs = owned_halves(grad_out)
        grad_qkv_w, theirs = after(grad_qkv_w, theirs)
        own_o = joined(mine, theirs).T
        own_gud = []
        for part in range(3):
            span = slice(part * size, (part + 1) * size)
            own_gud.append(
                joined(
                    jnp.concatenate([m[:, span] for m, t in pairs], axis=1),
                    jnp.concatenate([t[:, span] for m, t in pairs], axis=1),
                )
            )
        own_g, own_u, own_d = own_gud[0], own_gud[1], own_gud[2].T
        gain_grads = jnp.stack([gain_grad_one, gain_grad_two]).reshape(-1, 128)
        gain_grads, output = after(gain_grads, output)
        gain_grads = sum_all(gain_grads, dps, shards, 1).reshape(2, width)
        gain_grads = lax.dynamic_slice_in_dim(gain_grads, dp * rows, rows, axis=1)
        mine, theirs = owned_halves(grad_qkv_w)
        qc = group * HD
        own_q = joined(mine[:, :qc], theirs[:, :qc])
        own_k = joined(mine[:, qc : qc + HD], theirs[:, qc : qc + HD])
        own_v = joined(mine[:, qc + HD :], theirs[:, qc + HD :])
        owned = (gain_grads[0], own_q, own_k, own_v, own_o, gain_grads[1], own_g, own_u, own_d)

        first_shard = (me == 0).astype(F32)
        squares = first_shard * (jnp.sum(owned[0] * owned[0]) + jnp.sum(owned[5] * owned[5]))
        for position in (1, 2, 3, 4, 6, 7, 8):
            squares = squares + jnp.sum(owned[position] * owned[position])
        squares = jnp.broadcast_to(squares, (8, 128))
        squares, input_grad = after(squares, input_grad)
        squares = sum_all(squares, dps, shards, 2)
        global_norm = jnp.sqrt(squares[0, 0])
        factor = jnp.minimum(1.0, CLIP / global_norm)
        rate_now = rate * jnp.minimum(1.0, (step.astype(F32) + 1.0) / WARMUP)
        masters = (gain_first, w_query, w_key, w_value, w_output, gain_second, w_gate, w_up, w_down)
        moments = (
            moment_first,
            moment_query,
            moment_key,
            moment_value,
            moment_output,
            moment_second,
            moment_gate,
            moment_up,
            moment_down,
        )
        momenta = [
            0.5 * moment + 0.5 * (factor * gradient) for moment, gradient in zip(moments, owned)
        ]
        updated = [master - rate_now * momentum for master, momentum in zip(masters, momenta)]
        return (output, input_grad, global_norm, *momenta, *updated)

    return on_device


def solution(mesh):
    rows, both, back = P("dp"), P("dp", "shard"), P("shard", "dp")
    tokens = P("dp", None)
    params = (rows, both, both, both, back, rows, both, both, back)
    in_specs = (tokens, tokens, tokens, *params, *params, P(), P())
    out_specs = (tokens, tokens, P(), *params, *params)
    return jax.shard_map(
        build(mesh.shape["dp"], mesh.shape["shard"]),
        mesh=mesh,
        in_specs=in_specs,
        out_specs=out_specs,
        check_vma=False,
    )
```

```python
import functools

import jax
import jax.numpy as jnp
from jax import lax
from jax.experimental import pallas as pl
from jax.experimental.pallas import tpu as pltpu
from jax.sharding import PartitionSpec as P

H = 32
KV = 8
CLIP = 4096
WARMUP = 2000
THETA = 10000000.0
CHUNKS = 2
MESH = pl.DeviceIdType.MESH


BF = jnp.bfloat16
F32 = jnp.float32
HD = 64
EPS = 1e-05
NEGATIVE = -1e30
VMEM = 48 << 20

def dot(a, b, ca, cb):
    return lax.dot_general(a, b, (((ca,), (cb,)), ((), ())), preferred_element_type=F32)

def swap_halves(v):
    n = v.shape[1]
    lane = lax.broadcasted_iota(jnp.int32, v.shape, 1)
    return jnp.where(lane % HD < HD // 2, pltpu.roll(v, n - HD // 2, 1), pltpu.roll(v, HD // 2, 1))

def qkv_body(tok_ref, gain_ref, w_ref, cos_ref, sin_ref, normed_ref, q_ref, k_ref, v_ref):
    x = tok_ref[...].astype(F32)
    inv = lax.rsqrt(jnp.mean(x * x, axis=1, keepdims=True) + EPS)
    normed = (x * inv * gain_ref[...]).astype(BF)
    normed_ref[...] = normed
    lin = dot(normed, w_ref[...], 1, 0)
    heads = q_ref.shape[0]
    qc = heads * HD
    rot = lin * cos_ref[...] + swap_halves(lin) * sin_ref[...]
    for h in range(heads):
        q_ref[h] = (rot[:, h * HD : (h + 1) * HD]).astype(BF)
    k_ref[...] = rot[:, qc : qc + HD].astype(BF)
    v_ref[...] = rot[:, qc + HD :].astype(BF)

def qkv(tokens, gain, weight, cos, sin, heads, tile=256):
    count, width = tokens.shape
    cols = weight.shape[1]
    length = cos.shape[0]
    per = length // tile
    full = lambda i: (0, 0)
    row = lambda i: (i, 0)
    return pl.pallas_call(
        qkv_body,
        grid=(count // tile,),
        in_specs=[
            pl.BlockSpec((tile, width), row),
            pl.BlockSpec((1, width), full),
            pl.BlockSpec((width, cols), full),
            pl.BlockSpec((tile, cols), lambda i: (i % per, 0)),
            pl.BlockSpec((tile, cols), lambda i: (i % per, 0)),
        ],
        out_specs=[
            pl.BlockSpec((tile, width), row),
            pl.BlockSpec((heads, tile, HD), lambda i: (0, i, 0)),
            pl.BlockSpec((tile, HD), row),
            pl.BlockSpec((tile, HD), row),
        ],
        out_shape=[
            jax.ShapeDtypeStruct((count, width), BF),
            jax.ShapeDtypeStruct((heads, count, HD), BF),
            jax.ShapeDtypeStruct((count, HD), BF),
            jax.ShapeDtypeStruct((count, HD), BF),
        ],
        compiler_params=pltpu.CompilerParams(vmem_limit_bytes=VMEM),
        cost_estimate=pl.CostEstimate(flops=2 * count * width * cols, bytes_accessed=4 * count * width, transcendentals=0),
        name="qkv_rope",
    )(tokens, gain, weight, cos, sin)

def fwd_body(limits, q_ref, k_ref, v_ref, brow_ref, bcol_ref, o_ref, lse_ref):
    heads, tile, _ = q_ref.shape
    i = pl.program_id(1)
    def run(keys):
        k = k_ref[:keys]
        v = v_ref[:keys]
        allowed = brow_ref[0][:, :keys] <= bcol_ref[...]
        outs = []
        lses = []
        for h in range(heads):
            s = dot(q_ref[h] * BF(0.125), k, 1, 1)
            s = jnp.where(allowed, s, NEGATIVE)
            m = jnp.max(s, axis=1, keepdims=True)
            p = jnp.exp(s - m)
            l = jnp.sum(p, axis=1, keepdims=True)
            o = dot(p.astype(BF), v, 1, 0) / l
            outs.append(o.astype(BF))
            lses.append(m + jnp.log(l))
        o_ref[...] = jnp.concatenate(outs, axis=1)
        lse_ref[...] = jnp.concatenate(lses, axis=1)
    for n, keys in enumerate(limits):
        @pl.when(i == n)
        def _(keys=keys):
            run(keys)

def attend(q, k, v, brow, bcol, length, tile=256, most=256):
    heads, count, _ = q.shape
    seqs = count // length
    per = length // tile
    limits = tuple(min(length, (n + 1) * tile + most) for n in range(per))
    return pl.pallas_call(
        functools.partial(fwd_body, limits),
        grid=(seqs, per),
        in_specs=[
            pl.BlockSpec((heads, tile, HD), lambda b, i: (0, b * per + i, 0)),
            pl.BlockSpec((length, HD), lambda b, i: (b, 0)),
            pl.BlockSpec((length, HD), lambda b, i: (b, 0)),
            pl.BlockSpec((1, 1, length), lambda b, i: (b, 0, 0)),
            pl.BlockSpec((tile, 1), lambda b, i: (b * per + i, 0)),
        ],
        out_specs=[
            pl.BlockSpec((tile, heads * HD), lambda b, i: (b * per + i, 0)),
            pl.BlockSpec((tile, heads), lambda b, i: (b * per + i, 0)),
        ],
        out_shape=[
            jax.ShapeDtypeStruct((count, heads * HD), BF),
            jax.ShapeDtypeStruct((count, heads), F32),
        ],
        compiler_params=pltpu.CompilerParams(vmem_limit_bytes=VMEM),
        cost_estimate=pl.CostEstimate(flops=4 * heads * count * length * HD * 4, bytes_accessed=count * 2048, transcendentals=heads * count * length),
        name="attend",
    )(q, k, v, brow, bcol)

def bwd_body(
    limits,
    q_ref,
    k_ref,
    v_ref,
    brow_ref,
    bcol_ref,
    lse_ref,
    do_ref,
    cos_ref,
    sin_ref,
    kcos_ref,
    ksin_ref,
    even,
    odd,
    hidden_ref,
    piece,
    dq_ref,
    dkv_ref,
    out_ref,
    theirs,
    dk_acc,
    dv_acc,
    *scratch
):
    heads, tile, _ = q_ref.shape
    i = pl.program_id(1)
    turn = pl.program_id(0) * pl.num_programs(1) + i
    targets = neighbours()
    job = Job(even, odd, scratch[:8], targets)
    swapped = trade(piece, theirs, scratch[8])
    blocks = range(PARTS)

    @pl.when(turn == 0)
    def _():
        meet(targets)
        job.start()
        for s in blocks:
            job.first(s)

    @pl.when(turn == 1)
    def _():
        swapped.start()

    for s in blocks:

        @pl.when(turn == 2 + s)
        def _(s=s):
            job.second(s)

    @pl.when(turn == 6)
    def _():
        for s in blocks:
            job.own[job.span(s)] = (hidden_ref[job.span(s)] + job.total(s)).astype(BF)
            job.line_start(s, out_ref)

    @pl.when(i == 0)
    def _():
        dk_acc[...] = jnp.zeros_like(dk_acc)
        dv_acc[...] = jnp.zeros_like(dv_acc)
    def run(keys):
        k = k_ref[:keys]
        v = v_ref[:keys]
        allowed = brow_ref[0][:, :keys] <= bcol_ref[...]
        dqs = []
        dk = jnp.zeros((HD, keys), F32)
        dv = jnp.zeros((HD, keys), F32)
        for h in range(heads):
            q = q_ref[h] * BF(0.125)
            do = do_ref[:, h * HD : (h + 1) * HD]
            s = dot(q, k, 1, 1)
            s = jnp.where(allowed, s, NEGATIVE)
            p = jnp.exp(s - lse_ref[:, h : h + 1])
            dp = dot(do, v, 1, 1)
            pdp = p * dp
            delta = jnp.sum(pdp, axis=1, keepdims=True)
            ds = (pdp - p * delta).astype(BF)
            dqs.append(dot(ds, k, 1, 0) * 0.125)
            dk = dk + dot(q, ds, 0, 0)
            dv = dv + dot(do, p.astype(BF), 0, 0)
        dk_acc[:, :keys] += dk
        dv_acc[:, :keys] += dv
        dq = jnp.concatenate(dqs, axis=1)
        dq_ref[...] = (dq * cos_ref[...] - swap_halves(dq) * sin_ref[...]).astype(BF)
    for n, keys in enumerate(limits):
        @pl.when(i == n)
        def _(keys=keys):
            run(keys)

    @pl.when(turn == 7)
    def _():
        for s in blocks:
            job.line_core(s, out_ref)
        job.line_end(out_ref)
        swapped.wait()

    @pl.when(i == len(limits) - 1)
    def _():
        both = jnp.concatenate([dk_acc[...], dv_acc[...]], axis=0).T
        dkv_ref[...] = (both * kcos_ref[...] - swap_halves(both) * ksin_ref[...]).astype(BF)

def attend_back(
    q, k, v, brow, bcol, lse, do, cos, sin, length, even, odd, hidden, piece, tile=256, most=256
):
    heads, count, _ = q.shape
    seqs = count // length
    per = length // tile
    qc = heads * HD
    limits = tuple(min(length, (n + 1) * tile + most) for n in range(per))
    rowm = lambda b, i: (b * per + i, 0)
    return pl.pallas_call(
        functools.partial(bwd_body, limits),
        grid=(seqs, per),
        in_specs=[
            pl.BlockSpec((heads, tile, HD), lambda b, i: (0, b * per + i, 0)),
            pl.BlockSpec((length, HD), lambda b, i: (b, 0)),
            pl.BlockSpec((length, HD), lambda b, i: (b, 0)),
            pl.BlockSpec((1, 1, length), lambda b, i: (b, 0, 0)),
            pl.BlockSpec((tile, 1), rowm),
            pl.BlockSpec((tile, heads), rowm),
            pl.BlockSpec((tile, qc), rowm),
            pl.BlockSpec((tile, qc), lambda b, i: (i, 0)),
            pl.BlockSpec((tile, qc), lambda b, i: (i, 0)),
            pl.BlockSpec((length, 2 * HD), lambda b, i: (0, qc // (2 * HD))),
            pl.BlockSpec((length, 2 * HD), lambda b, i: (0, qc // (2 * HD))),
            IN_VMEM,
            ANY,
            IN_VMEM,
            ANY,
        ],
        out_specs=[
            pl.BlockSpec((tile, qc), rowm),
            pl.BlockSpec((length, 2 * HD), lambda b, i: (b, 0)),
            ANY,
            ANY,
        ],
        out_shape=[
            jax.ShapeDtypeStruct((count, qc), BF),
            jax.ShapeDtypeStruct((count, 2 * HD), BF),
            jax.ShapeDtypeStruct((length, even.shape[2]), BF),
            jax.ShapeDtypeStruct((piece.shape[0] // 2, piece.shape[1]), BF),
        ],
        scratch_shapes=[pltpu.VMEM((HD, length), F32), pltpu.VMEM((HD, length), F32)]
        + Job.scratch(even.shape[1], even.shape[2])
        + [pltpu.SemaphoreType.DMA((2, 1))],
        compiler_params=pltpu.CompilerParams(
            collective_id=7, has_side_effects=True, vmem_limit_bytes=VMEM
        ),
        cost_estimate=pl.CostEstimate(flops=10 * heads * count * length * HD * 4, bytes_accessed=count * 4096, transcendentals=heads * count * length),
        name="attend_back",
    )(q, k, v, brow, bcol, lse, do, cos, sin, cos, sin, even, odd, hidden, piece)

def rope_tables(length, heads):
    positions = jnp.arange(length, dtype=jnp.int32).astype(F32)
    powers = -2.0 * jnp.arange(HD // 2, dtype=F32) / HD
    angles = positions[:, None] * jnp.power(THETA, powers)[None, :]
    c = jnp.cos(angles); s = jnp.sin(angles)
    cos = jnp.concatenate([jnp.tile(jnp.concatenate([c, c], axis=1), (1, heads + 1)), jnp.ones((length, HD), F32)], axis=1)
    sin = jnp.concatenate([jnp.tile(jnp.concatenate([-s, s], axis=1), (1, heads + 1)), jnp.zeros((length, HD), F32)], axis=1)
    return cos, sin

def up_body(first, last, n2_ref, cot_ref, w_ref, *rest):
    if first:
        act_ref, dgu_ref, part_ref = rest
    else:
        prev_ref, act_ref, dgu_ref, part_ref = rest
    size = act_ref.shape[1]
    gu = dot(n2_ref[...], w_ref[:, : 2 * size], 1, 0)
    da = dot(cot_ref[...], w_ref[:, 2 * size :], 1, 0)
    gate, up = gu[:, :size], gu[:, size:]
    sig = 1.0 / (1.0 + jnp.exp(-gate))
    gs = gate * sig
    act_ref[...] = (gs * up).astype(BF)
    dg = (da * up * sig * (1.0 + gate * (1.0 - sig))).astype(BF)
    du = (da * gs).astype(BF)
    dgu = jnp.concatenate([dg, du], axis=1)
    dgu_ref[...] = dgu
    part = dot(dgu, w_ref[:, : 2 * size], 1, 1)
    if not first:
        part = part + prev_ref[...]
    part_ref[...] = part.astype(part_ref.dtype)

def up_back(n2, cot, weight, prev, last, tile=256):
    count, width = n2.shape
    size = weight.shape[1] // 3
    row = lambda i: (i, 0)
    full = lambda i: (0, 0)
    ins = [n2, cot, weight] + ([] if prev is None else [prev])
    specs = [pl.BlockSpec((tile, width), row), pl.BlockSpec((tile, width), row), pl.BlockSpec((width, 3 * size), full, pipeline_mode=pl.Buffered(1))]
    if prev is not None:
        specs.append(pl.BlockSpec((tile, width), row))
    return pl.pallas_call(
        functools.partial(up_body, prev is None, last),
        grid=(count // tile,),
        in_specs=specs,
        out_specs=[pl.BlockSpec((tile, size), row), pl.BlockSpec((tile, 2 * size), row), pl.BlockSpec((tile, width), row)],
        out_shape=[jax.ShapeDtypeStruct((count, size), BF), jax.ShapeDtypeStruct((count, 2 * size), BF), jax.ShapeDtypeStruct((count, width), BF if last else F32)],
        compiler_params=pltpu.CompilerParams(vmem_limit_bytes=VMEM),
        cost_estimate=pl.CostEstimate(flops=2 * count * width * size * 5, bytes_accessed=12 * count * width, transcendentals=count * size),
        name="swiglu_part",
    )(*ins)

def grad_body(n2a, n2b, cota, cotb, dgua, dgub, acta, actb, o_ref):
    size = acta.shape[1]
    gu = dot(n2a[...], dgua[...], 0, 0) + dot(n2b[...], dgub[...], 0, 0)
    o_ref[:, : 2 * size] = gu.astype(BF)
    dt = dot(cota[...], acta[...], 0, 0) + dot(cotb[...], actb[...], 0, 0)
    o_ref[:, 2 * size :] = dt.astype(BF)


def ffn_grads(n2, cot, dgu, act, tile=256):
    count, width = n2[0].shape
    size = act[0].shape[1]
    col = lambda i: (0, i)
    full = lambda i: (0, 0)
    return pl.pallas_call(
        grad_body,
        grid=(width // tile,),
        in_specs=[pl.BlockSpec((count, tile), col)] * 4
        + [pl.BlockSpec((count, 2 * size), full, pipeline_mode=pl.Buffered(1))] * 2
        + [pl.BlockSpec((count, size), full, pipeline_mode=pl.Buffered(1))] * 2,
        out_specs=pl.BlockSpec((tile, 3 * size), lambda i: (i, 0)),
        out_shape=jax.ShapeDtypeStruct((width, 3 * size), BF),
        compiler_params=pltpu.CompilerParams(vmem_limit_bytes=VMEM),
        cost_estimate=pl.CostEstimate(
            flops=4 * count * width * size * 3,
            bytes_accessed=16 * count * width,
            transcendentals=0,
        ),
        name="swiglu_grads",
    )(*n2, *cot, *dgu, *act)


def attn_grad_body(na, ga, ha, hb, ma, mb, o_ref):
    cols = ga.shape[1]
    o_ref[:, :cols] = dot(na[...], ga[...], 0, 0).astype(BF)
    o_ref[:, cols:] = (dot(ha[...], ma[...], 0, 0) + dot(hb[...], mb[...], 0, 0)).astype(BF)


def attn_grads(normed, grads, hidden, mixed, tile=256):
    width = normed.shape[1]
    col = lambda i: (0, i)
    ins = [normed, grads, *hidden, *mixed]
    cols = grads.shape[1] + mixed[0].shape[1]

    def tiled(value):
        return pl.BlockSpec((value.shape[0], tile), col)

    def whole(value):
        return pl.BlockSpec(value.shape, lambda i: (0, 0), pipeline_mode=pl.Buffered(1))

    return pl.pallas_call(
        attn_grad_body,
        grid=(width // tile,),
        in_specs=[tiled(normed), whole(grads)]
        + [tiled(v) for v in hidden]
        + [whole(v) for v in mixed],
        out_specs=pl.BlockSpec((tile, cols), lambda i: (i, 0)),
        out_shape=jax.ShapeDtypeStruct((width, cols), BF),
        compiler_params=pltpu.CompilerParams(vmem_limit_bytes=VMEM),
        cost_estimate=pl.CostEstimate(
            flops=2 * normed.shape[0] * width * cols,
            bytes_accessed=8 * normed.shape[0] * width,
            transcendentals=0,
        ),
        name="attn_grads",
    )(*ins)


def out_body(*refs):
    count = len(refs) // 2
    total = dot(refs[0][...], refs[count][...], 1, 1)
    for j in range(1, count):
        total = total + dot(refs[j][...], refs[count + j][...], 1, 1)
    refs[-1][...] = total.astype(BF)


def down(acts, weights, tile=256):
    count, size = acts[0].shape
    width = weights[0].shape[0]
    row = lambda i: (i, 0)
    return pl.pallas_call(
        out_body,
        grid=(count // tile,),
        in_specs=[pl.BlockSpec((tile, size), row) for _ in acts]
        + [
            pl.BlockSpec((width, size), lambda i: (0, 2), pipeline_mode=pl.Buffered(1))
            for _ in weights
        ],
        out_specs=pl.BlockSpec((tile, width), row),
        out_shape=jax.ShapeDtypeStruct((count, width), BF),
        compiler_params=pltpu.CompilerParams(vmem_limit_bytes=VMEM),
        cost_estimate=pl.CostEstimate(
            flops=2 * count * width * size * len(acts),
            bytes_accessed=8 * count * width,
            transcendentals=0,
        ),
        name="swiglu_down",
    )(*acts, *weights)


def peers(dps, shards):
    dp, sh = lax.axis_index("dp"), lax.axis_index("shard")
    groups = dps // 2
    near = []
    for r in range(1, 2 * shards):
        there = sh
        for bit in (1, 2):
            there = flip(there, bit) if r % shards & bit else there
        near.append((flip(dp, 1) if r >= shards else dp, there))
    far = [
        (lax.rem(dp // 2 + p, groups) * 2 + lax.rem(dp, 2), sh) for p in range(1, groups)
    ]
    return near, far, lax.rem(dp, 2) * shards + sh, dp // 2


def meet(targets):
    barrier = pltpu.get_barrier_semaphore()
    for target in targets:
        pl.semaphore_signal(barrier, inc=1, device_id=target, device_id_type=MESH)
    pl.semaphore_wait(barrier, len(targets))


def exchange(values, slots, mine, targets, source, send, recv, base):
    source[...] = values
    slots[mine] = values
    copies = [
        pltpu.make_async_remote_copy(
            src_ref=source,
            dst_ref=slots.at[mine],
            send_sem=send.at[base + n],
            recv_sem=recv.at[base + n],
            device_id=target,
            device_id_type=MESH,
        )
        for n, target in enumerate(targets)
    ]
    for copy in copies:
        copy.start()
    for copy in copies:
        copy.wait()
    total = slots[0]
    for n in range(1, slots.shape[0]):
        total = total + slots[n]
    return total


def two_stages(values, near, far, me, outer, bufs):
    slots_near, slots_far, from_near, from_far, send, recv = bufs
    total = exchange(values, slots_near, me, near, from_near, send, recv, 0)
    return exchange(total, slots_far, outer, far, from_far, send, recv, len(near))


def sum_scratch(shape, dps, shards):
    count = 2 * shards - 1 + dps // 2 - 1
    return [
        pltpu.VMEM((2 * shards,) + shape, F32),
        pltpu.VMEM((dps // 2,) + shape, F32),
        pltpu.VMEM(shape, F32),
        pltpu.VMEM(shape, F32),
        pltpu.SemaphoreType.DMA((count,)),
        pltpu.SemaphoreType.DMA((count,)),
    ]


def pick(x, first, second):
    low = jnp.where(x == 0, first.astype(F32), second.astype(F32)).astype(BF)
    high = jnp.where(x == 0, second.astype(F32), first.astype(F32)).astype(BF)
    return low, high


def finish_body(
    dps, shards, piece_ref, sq_ref, q_ref, k_ref, v_ref, o_ref, norm_ref, theirs, pair, *bufs
):
    near, far, me, outer = peers(dps, shards)
    rows = piece_ref.shape[0] // 2
    qc = q_ref.shape[1] // 2
    x = lax.rem(lax.axis_index("dp"), 2)
    meet(near + far)
    copy = pltpu.make_async_remote_copy(
        src_ref=piece_ref.at[pl.ds(pl.multiple_of((1 - x) * rows, rows), rows)],
        dst_ref=theirs,
        send_sem=pair.at[0],
        recv_sem=pair.at[1],
        device_id=(flip(lax.axis_index("dp"), 1), lax.axis_index("shard")),
        device_id_type=MESH,
    )
    copy.start()
    mine = piece_ref[pl.ds(pl.multiple_of(x * rows, rows), rows), :]
    wide = mine.astype(F32)
    squares = jnp.sum(wide * wide)
    copy.wait()
    got = theirs[...]
    wide = got.astype(F32)
    squares = squares + jnp.sum(wide * wide)
    low, high = pick(x, mine, got)
    q_ref[:, :qc] = low[:, :qc]
    q_ref[:, qc:] = high[:, :qc]
    k_ref[...] = jnp.concatenate([low[:, qc : qc + HD], high[:, qc : qc + HD]], axis=1)
    vc, oc = qc + HD, qc + 2 * HD
    v_ref[...] = jnp.concatenate([low[:, vc:oc], high[:, vc:oc]], axis=1)
    o_ref[:qc] = low[:, oc:].astype(F32).T.astype(BF)
    o_ref[qc:] = high[:, oc:].astype(F32).T.astype(BF)
    norm_ref[...] = jnp.sqrt(
        two_stages(sq_ref[...] + squares, near, far, me, outer, bufs)
    )


def finish(piece, squares, dps, shards, number):
    rows, cols = piece.shape[0] // 2, piece.shape[1]
    qc = (cols - 2 * HD) // 2
    vmem = pl.BlockSpec(memory_space=pltpu.VMEM)
    return pl.pallas_call(
        functools.partial(finish_body, dps, shards),
        in_specs=[vmem, vmem],
        out_specs=[vmem] * 5,
        out_shape=[
            jax.ShapeDtypeStruct((rows, 2 * qc), BF),
            jax.ShapeDtypeStruct((rows, 2 * HD), BF),
            jax.ShapeDtypeStruct((rows, 2 * HD), BF),
            jax.ShapeDtypeStruct((2 * qc, rows), BF),
            jax.ShapeDtypeStruct(squares.shape, F32),
        ],
        scratch_shapes=[pltpu.VMEM((rows, cols), BF), pltpu.SemaphoreType.DMA((2,))]
        + sum_scratch(squares.shape, dps, shards),
        compiler_params=pltpu.CompilerParams(collective_id=number, has_side_effects=True),
        name="finish",
    )(piece, squares)


def collect_body(count, size, x_ref, *refs):
    ins, (g_ref, u_ref, d_ref, sq_ref) = refs[: 2 * count], refs[2 * count :]
    x = x_ref[0]
    total = jnp.zeros((1, 1), F32)
    for j in range(count):
        size_in = ins[2 * j + 1].shape[0]
        mine = ins[2 * j][pl.ds(pl.multiple_of(x * size_in, size_in), size_in), :]
        theirs = ins[2 * j + 1][...]
        for h, piece in enumerate(pick(x, mine, theirs)):
            wide = piece.astype(F32)
            total = total + jnp.sum(wide * wide, keepdims=True)
            span = pl.ds((h * count + j) * size, size)
            g_ref[:, span] = piece[:, :size]
            u_ref[:, span] = piece[:, size : 2 * size]
            d_ref[span, :] = wide[:, 2 * size :].T.astype(BF)
    sq_ref[...] = jnp.broadcast_to(total, sq_ref.shape)


def collect(x, pairs):
    rows, size = pairs[0][1].shape[0], pairs[0][1].shape[1] // 3
    wide = 2 * len(pairs) * size
    vmem = pl.BlockSpec(memory_space=pltpu.VMEM)
    ins = [v for pair in pairs for v in pair]
    return pl.pallas_call(
        functools.partial(collect_body, len(pairs), size),
        in_specs=[pl.BlockSpec(memory_space=pltpu.SMEM)] + [vmem] * len(ins),
        out_specs=[vmem] * 4,
        out_shape=[
            jax.ShapeDtypeStruct((rows, wide), BF),
            jax.ShapeDtypeStruct((rows, wide), BF),
            jax.ShapeDtypeStruct((wide, rows), BF),
            jax.ShapeDtypeStruct((8, 128), F32),
        ],
        compiler_params=pltpu.CompilerParams(vmem_limit_bytes=VMEM),
        name="collect",
    )(x.reshape(1), *ins)


PARTS = 4


def flip(value, bit):
    return value + bit * (1 - 2 * lax.rem(value // bit, 2))


def neighbours():
    dp, sh = lax.axis_index("dp"), lax.axis_index("shard")
    return (flip(dp, 1), sh), (dp, flip(sh, 2)), (dp, flip(sh, 1))


def remote(src, dst, sems, n, target):
    return pltpu.make_async_remote_copy(
        src_ref=src,
        dst_ref=dst,
        send_sem=sems.at[0, n],
        recv_sem=sems.at[1, n],
        device_id=target,
        device_id_type=MESH,
    )


class Job:

    def __init__(self, even, odd, scratch, targets, y_first=()):
        self.y_first = y_first
        self.even, self.odd = even, odd
        self.got, self.out1, self.in1, self.out2, self.in2, self.own, self.sems, self.local = scratch
        self.x, self.y, self.core = targets
        self.rows = even.shape[1] // PARTS

    @staticmethod
    def scratch(rows, width):
        part = rows // PARTS
        return [
            pltpu.VMEM((4, rows, width), BF),
            pltpu.VMEM((PARTS, 2, part, width), BF),
            pltpu.VMEM((PARTS, 2, part, width), BF),
            pltpu.VMEM((PARTS, part, width), BF),
            pltpu.VMEM((PARTS, part, width), BF),
            pltpu.VMEM((rows, width), BF),
            pltpu.SemaphoreType.DMA((2, 6 * PARTS)),
            pltpu.SemaphoreType.DMA((PARTS,)),
        ]

    def span(self, s):
        return pl.ds(s * self.rows, self.rows)

    def over_x(self, s):
        return s not in self.y_first

    def copy(self, stage, s, src, dst, target):
        return remote(src, dst, self.sems, stage * PARTS + s, target)

    def to_core(self, s):
        span = self.span(s)
        return self.copy(0, s, self.odd.at[:, span], self.got.at[:, span], self.core)

    def to_first(self, s):
        target = self.x if self.over_x(s) else self.y
        return self.copy(1, s, self.out1.at[s], self.in1.at[s], target)

    def to_second(self, s):
        target = self.y if self.over_x(s) else self.x
        return self.copy(2, s, self.out2.at[s], self.in2.at[s], target)

    def start(self):
        for s in range(PARTS):
            self.to_core(s).start()

    def pair(self, k, s):
        return self.even[k, self.span(s)].astype(F32) + self.got[k, self.span(s)].astype(F32)

    def first(self, s):
        self.to_core(s).wait_recv()
        self.out1[s, 0] = self.pair(2 if self.over_x(s) else 1, s).astype(BF)
        self.out1[s, 1] = self.pair(3, s).astype(BF)
        self.to_first(s).start()

    def second(self, s):
        self.to_first(s).wait_recv()
        near = self.pair(1 if self.over_x(s) else 2, s)
        self.out2[s] = (near + self.in1[s, 1].astype(F32)).astype(BF)
        self.to_second(s).start()

    def total(self, s):
        self.to_second(s).wait_recv()
        return self.pair(0, s) + self.in1[s, 0].astype(F32) + self.in2[s].astype(F32)

    def sent(self):
        for s in range(PARTS):
            self.to_core(s).wait_send()
            self.to_first(s).wait_send()
            self.to_second(s).wait_send()


    def keep(self, s, place):
        return pltpu.make_async_copy(self.own.at[self.span(s)], place, self.local.at[s])

    def spread_copies(self, s, mine, theirs):
        span = self.span(s)
        own = self.own.at[span]
        if self.over_x(s):
            near = self.copy(3, s, own, mine.at[1, 0, span], self.x)
            far = self.copy(4, s, mine.at[:, 0, span], mine.at[:, 1, span], self.y)
        else:
            near = self.copy(3, s, own, mine.at[0, 1, span], self.y)
            far = self.copy(4, s, mine.at[0, :, span], mine.at[1, :, span], self.x)
        core = self.copy(5, s, mine.at[:, :, span], theirs.at[:, :, span], self.core)
        return self.keep(s, mine.at[0, 0, span]), near, far, core


    def line_copies(self, s, whole):
        me = lax.axis_index("shard")
        size = self.rows * PARTS

        def place(owner):
            at = pl.multiple_of(owner * size + s * self.rows, self.rows)
            return whole.at[pl.ds(at, self.rows)]

        own = self.own.at[self.span(s)]
        near = self.copy(3, s, own, place(me), self.y)
        core = self.copy(4, s, own, place(me), self.core)
        other = place(flip(me, 2))
        return self.keep(s, place(me)), near, core, self.copy(5, s, other, other, self.core)

    def line_start(self, s, whole):
        for copy in self.line_copies(s, whole)[:3]:
            copy.start()

    def line_core(self, s, whole):
        keep, near, core, far = self.line_copies(s, whole)
        keep.wait()
        near.wait_recv()
        far.start()

    def line_end(self, whole):
        for s in range(PARTS):
            _, near, core, far = self.line_copies(s, whole)
            core.wait_recv()
            far.wait_recv()
            for copy in (near, core, far):
                copy.wait_send()
        self.sent()


def run_job(job, mine, theirs, produce, filler=None):
    blocks = range(PARTS)
    job.start()
    for s in blocks:
        job.first(s)
    if filler is not None:
        filler(0)
    for s in blocks:
        job.second(s)
    if filler is not None:
        filler(1)
    copies = [job.spread_copies(s, mine, theirs) for s in blocks]
    for s in blocks:
        job.own[job.span(s)] = produce(s, job.total(s)).astype(BF)
        copies[s][0].start()
        copies[s][1].start()
    for keep, near, far, core in copies:
        keep.wait()
        near.wait_recv()
        far.start()
    for keep, near, far, core in copies:
        far.wait_recv()
        core.start()
    if filler is not None:
        filler(2)
    for keep, near, far, core in copies:
        core.wait_recv()
        for copy in (near, far, core):
            copy.wait_send()
    job.sent()


def rms_of(values):
    return lax.rsqrt(jnp.mean(values * values, axis=1, keepdims=True) + EPS)


def norm_back_of(values, gain, grad):
    inverse = rms_of(values)
    scaled = grad * gain
    total = jnp.sum(grad * values * inverse, axis=0, keepdims=True)
    mean = jnp.mean(scaled * values, axis=1, keepdims=True)
    return total, inverse * scaled - values * (inverse * inverse * inverse * mean)


def mid_body(
    even, odd, tok_ref, gain_ref, cot_ref, mine, theirs, hidden_ref, cot_mine, cot_theirs, *scratch
):
    targets = neighbours()
    xs, ys, core = targets
    sh = lax.axis_index("shard")
    quarter = cot_ref.shape[0] // 4
    cot_sem, keeps = scratch[8:]
    local = []
    for n, (half, dy, owner) in enumerate(
        (
            (cot_mine, 0, sh),
            (cot_mine, 1, flip(sh, 2)),
            (cot_theirs, 0, flip(sh, 1)),
            (cot_theirs, 1, flip(flip(sh, 1), 2)),
        )
    ):
        src = cot_ref.at[pl.ds(pl.multiple_of(owner * quarter, quarter), quarter)]
        local.append(pltpu.make_async_copy(src, half.at[0, dy], keeps.at[n]))
    for copy in local:
        copy.start()
    meet(targets)
    job = Job(even, odd, scratch[:8], targets, (1, 3))
    rows = quarter // PARTS
    over_x, over_y, over_core, over_far = [], [], [], []
    for s in range(PARTS):
        span = pl.ds(s * rows, rows)
        own = cot_ref.at[pl.ds(pl.multiple_of(sh * quarter + s * rows, rows), rows)]
        near, far = cot_mine.at[1, 0, span], cot_mine.at[1, 1, span]
        over_x.append(remote(own, near, cot_sem, s, xs))
        over_y.append(remote(near, far, cot_sem, PARTS + s, ys))
        over_core.append(remote(near, cot_theirs.at[1, 0, span], cot_sem, 2 * PARTS + s, core))
        over_far.append(remote(far, cot_theirs.at[1, 1, span], cot_sem, 3 * PARTS + s, core))

    def cotangents(part):
        for s in range(PARTS):
            if part == 0:
                over_x[s].start()
            elif part == 1:
                over_x[s].wait_recv()
                over_y[s].start()
                over_core[s].start()
            else:
                over_y[s].wait_recv()
                over_far[s].start()

    def produce(s, total):
        hidden = tok_ref[job.span(s)].astype(F32) + total
        hidden_ref[job.span(s)] = hidden
        return hidden * rms_of(hidden) * gain_ref[...]

    run_job(job, mine, theirs, produce, cotangents)
    for copy in local:
        copy.wait()
    for copies in (over_core, over_far):
        for copy in copies:
            copy.wait_recv()
    for copies in (over_x, over_y, over_core, over_far):
        for copy in copies:
            copy.wait_send()


def back_body(even, odd, hidden_ref, cot_ref, gain_ref, *rest):
    ins, (mine, theirs, gh_ref, gg_ref, dw_ref), scratch = rest[:8], rest[8:13], rest[13:]
    held, (tiles, load, store) = scratch[8:16], scratch[16:]
    targets = neighbours()
    loads = [
        pltpu.make_async_copy(src, dst, load.at[n]) for n, (src, dst) in enumerate(zip(ins, held))
    ]
    for copy in loads:
        copy.start()
    meet(targets)
    job = Job(even, odd, scratch[:8], targets, (1, 3))
    na, nb, ca, cb, ga, gb, aa, ab = held
    size = aa.shape[1]
    step = tiles.shape[1]
    half = dw_ref.shape[0] // step // 2

    def filler(part):
        if part == 2:
            return
        if part == 0:
            for copy in loads:
                copy.wait()

        def tile(n, carry):
            i = part * half + n
            cols = pl.ds(pl.multiple_of(i * step, step), step)
            slot = lax.rem(n, 2)
            copy = pltpu.make_async_copy(tiles.at[slot], dw_ref.at[cols], store.at[slot])

            @pl.when(n >= 2)
            def _():
                copy.wait()

            gu = dot(na[:, cols], ga[...], 0, 0) + dot(nb[:, cols], gb[...], 0, 0)
            tiles[slot, :, : 2 * size] = gu.astype(BF)
            dt = dot(ca[:, cols], aa[...], 0, 0) + dot(cb[:, cols], ab[...], 0, 0)
            tiles[slot, :, 2 * size :] = dt.astype(BF)
            copy.start()
            return carry

        lax.fori_loop(0, half, tile, 0)
        for n in (0, 1):
            cols = pl.ds(part * half * step, step)
            pltpu.make_async_copy(tiles.at[n], dw_ref.at[cols], store.at[n]).wait()

    totals = []

    def produce(s, total):
        gain_total, through = norm_back_of(hidden_ref[job.span(s)], gain_ref[...], total)
        totals.append(gain_total)
        grad_hidden = cot_ref[job.span(s)].astype(F32) + through
        gh_ref[job.span(s)] = grad_hidden
        return grad_hidden

    run_job(job, mine, theirs, produce, filler)
    gg_ref[...] = sum(totals[1:], totals[0])


def trade(piece, theirs, sems):
    size = theirs.shape[0]
    x = lax.rem(lax.axis_index("dp"), 2)
    src = piece.at[pl.ds(pl.multiple_of((1 - x) * size, size), size)]
    return remote(src, theirs, sems, 0, neighbours()[0])


def end_body(
    dps, shards, even, odd, tok_ref, gh_ref, gain_ref, gg_ref, piece, in_ref, sum_ref, theirs, *scratch
):
    near, far, me, outer = peers(dps, shards)
    meet(near + far)
    job = Job(even, odd, scratch[:8], neighbours())
    swapped = trade(piece, theirs, scratch[8])
    blocks = range(PARTS)
    totals = []
    job.start()
    for s in blocks:
        job.first(s)
    swapped.start()
    for s in blocks:
        job.second(s)
    for s in blocks:
        span = job.span(s)
        values = tok_ref[span].astype(F32)
        gain_total, through = norm_back_of(values, gain_ref[...], job.total(s))
        totals.append(gain_total)
        job.own[span] = (gh_ref[span] + through).astype(BF)
        job.line_start(s, in_ref)
    gains = jnp.concatenate([sum(totals[1:], totals[0]), gg_ref[...]], axis=0)
    sum_ref[...] = two_stages(gains, near, far, me, outer, scratch[9:])
    for s in blocks:
        job.line_core(s, in_ref)
    job.line_end(in_ref)
    swapped.wait()


def entry_body(tok_ref, keep_ref, send_ref, both, piece, hop_x, hop_y, hop_core, weight_sem, keeps):
    xs, ys, core = neighbours()
    sh = lax.axis_index("shard")
    x = lax.rem(lax.axis_index("dp"), 2)
    length = tok_ref.shape[0]
    quarter = length // 4
    rows = quarter // PARTS
    size = keep_ref.shape[0]
    mine = piece.at[pl.ds(pl.multiple_of(x * size, size), size)]
    local = [
        pltpu.make_async_copy(keep_ref, mine, keeps.at[0]),
        pltpu.make_async_copy(tok_ref, both.at[pl.ds(0, length)], keeps.at[1]),
    ]
    for copy in local:
        copy.start()
    meet((xs, ys, core))

    def rows_of(ref, base, owner, s):
        return ref.at[pl.ds(pl.multiple_of(base + owner * quarter + s * rows, rows), rows)]

    over_x, over_y, over_core, over_far = [], [], [], []
    for s in range(PARTS):
        near, far = rows_of(both, length, sh, s), rows_of(both, length, flip(sh, 2), s)
        over_x.append(remote(rows_of(tok_ref, 0, sh, s), near, hop_x, s, xs))
        over_y.append(remote(near, near, hop_y, s, ys))
        over_core.append(remote(near, near, hop_core, s, core))
        over_far.append(remote(far, far, hop_core, PARTS + s, core))
    moving = remote(send_ref, mine, weight_sem, 0, xs)
    for copy in over_x:
        copy.start()
    moving.start()
    for s in range(PARTS):
        over_x[s].wait_recv()
        over_y[s].start()
        over_core[s].start()
    for s in range(PARTS):
        over_y[s].wait_recv()
        over_far[s].start()
    moving.wait()
    for copy in over_core + over_far:
        copy.wait()
    for copy in over_x + over_y:
        copy.wait_send()
    for copy in local:
        copy.wait()


def entry(tokens, keep, sent):
    length, width = tokens.shape
    dma = pltpu.SemaphoreType.DMA
    return pl.pallas_call(
        entry_body,
        in_specs=[ANY] * 3,
        out_specs=[ANY] * 2,
        out_shape=[
            jax.ShapeDtypeStruct((2 * length, width), BF),
            jax.ShapeDtypeStruct((2 * keep.shape[0], keep.shape[1]), BF),
        ],
        scratch_shapes=[
            dma((2, PARTS)),
            dma((2, PARTS)),
            dma((2, 2 * PARTS)),
            dma((2, 1)),
            dma((2,)),
        ],
        compiler_params=pltpu.CompilerParams(
            collective_id=6, has_side_effects=True, vmem_limit_bytes=8 << 20
        ),
        name="entry",
    )(tokens, keep, sent)


ANY = pl.BlockSpec(memory_space=pl.ANY)
IN_VMEM = pl.BlockSpec(memory_space=pltpu.VMEM)
BIG = 60 << 20


def mid_stage(even, odd, tokens_own, gain, cotangent):
    _, rows, width = even.shape
    half = jax.ShapeDtypeStruct((2, 2, rows, width), BF)
    return pl.pallas_call(
        mid_body,
        in_specs=[IN_VMEM, ANY, IN_VMEM, IN_VMEM, ANY],
        out_specs=[ANY, ANY, IN_VMEM, ANY, ANY],
        out_shape=[half, half, jax.ShapeDtypeStruct((rows, width), F32), half, half],
        scratch_shapes=Job.scratch(rows, width)
        + [pltpu.SemaphoreType.DMA((2, 4 * PARTS)), pltpu.SemaphoreType.DMA((4,))],
        compiler_params=pltpu.CompilerParams(
            collective_id=3, has_side_effects=True, vmem_limit_bytes=VMEM
        ),
        name="mid_stage",
    )(even, odd, tokens_own, gain, cotangent)


def back_stage(even, odd, hidden, cot_own, gain, *filling, tile=256):
    _, rows, width = even.shape
    size = filling[-1].shape[1]
    spread_shape = jax.ShapeDtypeStruct((2, 2, rows, width), BF)
    return pl.pallas_call(
        back_body,
        in_specs=[IN_VMEM, ANY, IN_VMEM, IN_VMEM, IN_VMEM] + [ANY] * 8,
        out_specs=[ANY, ANY, IN_VMEM, IN_VMEM, ANY],
        out_shape=[
            spread_shape,
            spread_shape,
            jax.ShapeDtypeStruct((rows, width), F32),
            jax.ShapeDtypeStruct((1, width), F32),
            jax.ShapeDtypeStruct((width, 3 * size), BF),
        ],
        scratch_shapes=Job.scratch(rows, width)
        + [pltpu.VMEM(value.shape, BF) for value in filling]
        + [
            pltpu.VMEM((2, tile, 3 * size), BF),
            pltpu.SemaphoreType.DMA((8,)),
            pltpu.SemaphoreType.DMA((2,)),
        ],
        compiler_params=pltpu.CompilerParams(
            collective_id=4, has_side_effects=True, vmem_limit_bytes=BIG
        ),
        name="back_stage",
    )(even, odd, hidden, cot_own, gain, *filling)


def end_stage(even, odd, tokens_own, grad_hidden, gain, gain_grad, piece, dps, shards):
    _, rows, width = even.shape
    theirs = jax.ShapeDtypeStruct((piece.shape[0] // 2, piece.shape[1]), BF)
    return pl.pallas_call(
        functools.partial(end_body, dps, shards),
        in_specs=[IN_VMEM, ANY] + [IN_VMEM] * 4 + [ANY],
        out_specs=[ANY, IN_VMEM, ANY],
        out_shape=[
            jax.ShapeDtypeStruct((shards * rows, width), BF),
            jax.ShapeDtypeStruct((2, width), F32),
            theirs,
        ],
        scratch_shapes=Job.scratch(rows, width)
        + [pltpu.SemaphoreType.DMA((2, 1))]
        + sum_scratch((2, width), dps, shards),
        compiler_params=pltpu.CompilerParams(
            collective_id=5, has_side_effects=True, vmem_limit_bytes=VMEM
        ),
        name="end_stage",
    )(even, odd, tokens_own, grad_hidden, gain, gain_grad, piece)


def after(*values):
    return lax.optimization_barrier(values)


def build(dps, shards):
    total = dps * shards
    axes = ("dp", "shard")
    zgroups = [[i for i in range(dps) if i % 2 == p] for p in (0, 1)]

    def swap(values, dx, ds):
        pairs = [
            (i, ((i // shards) ^ dx) * shards + ((i % shards) ^ ds)) for i in range(total)
        ]
        return lax.ppermute(values, axes, pairs)

    def gather(piece):
        return lax.all_gather(piece, "dp", axis=0, tiled=True, axis_index_groups=zgroups)

    def scatter(whole):
        return lax.psum_scatter(
            whole, "dp", scatter_dimension=0, tiled=True, axis_index_groups=zgroups
        )


    def on_device(
        tokens,
        block_ids,
        cotangent,
        gain_first,
        w_query,
        w_key,
        w_value,
        w_output,
        gain_second,
        w_gate,
        w_up,
        w_down,
        moment_first,
        moment_query,
        moment_key,
        moment_value,
        moment_output,
        moment_second,
        moment_gate,
        moment_up,
        moment_down,
        step,
        rate,
    ):
        length = block_ids.shape[1]
        width = tokens.shape[1]
        group = H // KV
        dp = lax.axis_index("dp")
        me = lax.axis_index("shard")
        x = lax.rem(dp, 2)
        quarter = length // shards
        rows = w_query.shape[0]

        def half(values, which):
            size = values.shape[1] // 2
            return lax.dynamic_slice_in_dim(values, which * size, size, axis=1)

        def ordered(mine, theirs, axis=0):
            first = jnp.where(x == 0, mine, theirs)
            second = jnp.where(x == 0, theirs, mine)
            return jnp.concatenate([first, second], axis=axis)

        def natural(parts):
            stacked = jnp.stack(parts)
            return jnp.concatenate(
                [
                    lax.dynamic_index_in_dim(stacked, me ^ q, axis=0, keepdims=False)
                    for q in range(shards)
                ],
                axis=0,
            )

        def cut(values, ds):
            return lax.dynamic_slice_in_dim(values, (me ^ ds) * quarter, quarter, axis=0)

        def halves(own, other):
            return [
                jnp.stack([cut(own, dc), cut(own, dc + 2), cut(other, dc), cut(other, dc + 2)])
                for dc in (0, 1)
            ]

        def streams(mine, theirs):
            return [
                natural([mine[k], theirs[k], mine[k + 1], theirs[k + 1]]) for k in (0, 2)
            ]

        def flat(values):
            return values.reshape(-1, values.shape[-1])

        low_q = w_query.astype(BF)
        low_k = w_key.astype(BF)
        low_v = w_value.astype(BF)
        low_o = w_output.astype(BF).T
        qc = group * HD
        cols = qc + 2 * HD

        def attn_half(which):
            return jnp.concatenate([half(low, which) for low in (low_q, low_k, low_v, low_o)], axis=1)

        gains = jnp.stack([gain_first, gain_second]).astype(BF)
        gains = jnp.pad(gains, ((0, 14), (0, cols + qc - rows)))
        sent = swap(jnp.concatenate([attn_half(1 - x), gains], axis=0), 1, 0)
        piece = jnp.concatenate(
            [ordered(attn_half(x), sent[:rows]), ordered(gains, sent[rows:])], axis=0
        )
        groups = dps // 2

        blocks_x = swap(block_ids, 1, 0)
        low_g = w_gate.astype(BF)
        low_u = w_up.astype(BF)
        low_d = w_down.astype(BF).T
        size = low_g.shape[1] // 2 // CHUNKS

        def ffn_part(which, j):
            return jnp.concatenate(
                [half(low, which)[:, j * size : (j + 1) * size] for low in (low_g, low_u, low_d)],
                axis=1,
            )

        both, first_part = entry(
            after(tokens, piece)[0], ffn_part(x, 0), ffn_part(1 - x, 0)
        )
        ffn_weights = [gather(first_part)]
        packed, both, send_second = after(gather(piece), both, ffn_part(1 - x, 1))
        second_part = ordered(ffn_part(x, 1), swap(send_second, 1, 0))
        packed = packed.reshape(groups, 2 * rows + 32, cols + qc)
        qkv_weight = packed[:, : 2 * rows, :cols].reshape(width, cols)
        out_weight = packed[:, : 2 * rows, cols:].reshape(width, qc)
        tails = packed[:, 2 * rows :].reshape(groups, 2, 16, cols + qc)
        gain_one = tails[:, :, 0, :rows].reshape(1, width).astype(F32)
        gain_two = tails[:, :, 1, :rows].reshape(1, width).astype(F32)

        cosine, sine = rope_tables(length, group)

        normed, query, key, value = qkv(both, gain_one, qkv_weight, cosine, sine, group)
        blocks = jnp.concatenate([block_ids, blocks_x], axis=0)
        block_rows = blocks[:, None, :]
        block_cols = blocks.reshape(2 * length, 1)
        mixed, lse = attend(query, key, value, block_rows, block_cols, length)
        mixed, second_part = after(mixed, second_part)
        ffn_weights.append(gather(second_part))
        mixed_own, mixed_other = mixed[:length], mixed[length:]
        mixed_mine, mixed_theirs = halves(mixed_own, mixed_other)

        def project(values, weight):
            partial = jnp.einsum("atk,dk->atd", values, weight, preferred_element_type=F32)
            return partial.astype(BF)

        tokens_own = cut(tokens, 0)
        mine, theirs, hidden, cot_mine, cot_theirs = mid_stage(
            project(mixed_mine, out_weight),
            project(mixed_theirs, out_weight),
            tokens_own,
            gain_two,
            cotangent,
        )
        two_mine, two_theirs = flat(mine), flat(theirs)
        cot_mine, cot_theirs = flat(cot_mine), flat(cot_theirs)

        shape = (4, quarter, width)
        acts_mine = []
        acts_theirs = []
        part_mine = part_theirs = None
        first_grads = None
        for j in range(CHUNKS):
            last = j == CHUNKS - 1
            weight = ffn_weights[j]
            theirs_in = two_theirs
            if first_grads is not None:
                theirs_in, first_grads = after(two_theirs, first_grads)
            act_theirs, gu_theirs, part_theirs = up_back(
                theirs_in, cot_theirs, weight, part_theirs, last
            )
            mine_in = two_mine
            if last:
                mine_in, part_theirs = after(two_mine, part_theirs)
            act_mine, gu_mine, part_mine = up_back(mine_in, cot_mine, weight, part_mine, last)
            acts_mine.append(act_mine)
            acts_theirs.append(act_theirs)

            if not last:
                first_grads = ffn_grads(
                    (two_mine, two_theirs),
                    (cot_mine, cot_theirs),
                    (gu_mine, gu_theirs),
                    (act_mine, act_theirs),
                )
        mine, theirs, grad_hidden, gain_grad_two, last_grads = back_stage(
            part_mine.reshape(shape),
            part_theirs.reshape(shape),
            hidden,
            cut(cotangent, 0),
            gain_two,
            two_mine,
            two_theirs,
            cot_mine,
            cot_theirs,
            gu_mine,
            gu_theirs,
            act_mine,
            act_theirs,
        )
        gh_mine = mine.reshape(shape)
        gh_theirs = theirs.reshape(shape)
        first_piece = scatter(first_grads)
        last_piece = scatter(last_grads)
        grad_mixed_mine = project(gh_mine, out_weight.T)
        grad_mixed_theirs = project(gh_theirs, out_weight.T)
        grad_mixed = streams(grad_mixed_mine, grad_mixed_theirs)
        grad_mixed, first_piece = after(grad_mixed, first_piece)
        grad_q, grad_kv, output, first_theirs = attend_back(
            query,
            key,
            value,
            block_rows,
            block_cols,
            lse,
            jnp.concatenate(grad_mixed, axis=0),
            cosine,
            sine,
            length,
            down(acts_mine, ffn_weights).reshape(shape),
            down(acts_theirs, ffn_weights).reshape(shape),
            hidden,
            first_piece,
        )
        grad_qkv = jnp.concatenate([grad_q, grad_kv], axis=1)
        d_attn = attn_grads(
            normed,
            grad_qkv,
            (flat(gh_mine), flat(gh_theirs)),
            (flat(mixed_mine), flat(mixed_theirs)),
        )
        grad_attn = scatter(d_attn)
        gq_mine, gq_theirs = halves(grad_qkv[:length], grad_qkv[length:])
        gq_mine, gq_theirs, d_attn = after(gq_mine, gq_theirs, d_attn)
        input_grad, gain_grads, last_theirs = end_stage(
            project(gq_mine, qkv_weight),
            project(gq_theirs, qkv_weight),
            tokens_own,
            grad_hidden,
            gain_one,
            gain_grad_two,
            last_piece,
            dps,
            shards,
        )
        input_grad = input_grad.astype(F32)

        pairs = [(first_piece, first_theirs), (last_piece, last_theirs)]
        own_g, own_u, own_d, squares = collect(x, pairs)
        gain_grads = lax.dynamic_slice_in_dim(gain_grads, dp * rows, rows, axis=1)
        first_shard = (me == 0).astype(F32)
        squares = squares + first_shard * jnp.sum(gain_grads * gain_grads)
        grad_attn, squares, output, own_g, own_u, own_d = after(
            grad_attn, squares, output, own_g, own_u, own_d
        )
        own_q, own_k, own_v, own_o, norm = finish(grad_attn, squares, dps, shards, 2)
        global_norm = norm[0, 0]
        owned = (gain_grads[0], own_q, own_k, own_v, own_o, gain_grads[1], own_g, own_u, own_d)
        factor = jnp.minimum(1.0, CLIP / global_norm)
        rate_now = rate * jnp.minimum(1.0, (step.astype(F32) + 1.0) / WARMUP)
        masters = (gain_first, w_query, w_key, w_value, w_output, gain_second, w_gate, w_up, w_down)
        moments = (
            moment_first,
            moment_query,
            moment_key,
            moment_value,
            moment_output,
            moment_second,
            moment_gate,
            moment_up,
            moment_down,
        )
        momenta = [
            0.5 * moment + 0.5 * (factor * gradient) for moment, gradient in zip(moments, owned)
        ]
        updated = [master - rate_now * momentum for master, momentum in zip(masters, momenta)]
        return (output, input_grad, global_norm, *momenta, *updated)

    return on_device


def solution(mesh):
    rows, both, back = P("dp"), P("dp", "shard"), P("shard", "dp")
    tokens = P("dp", None)
    params = (rows, both, both, both, back, rows, both, both, back)
    in_specs = (tokens, tokens, tokens, *params, *params, P(), P())
    out_specs = (tokens, tokens, P(), *params, *params)
    return jax.shard_map(
        build(mesh.shape["dp"], mesh.shape["shard"]),
        mesh=mesh,
        in_specs=in_specs,
        out_specs=out_specs,
        check_vma=False,
    )
```

```python
import functools

import jax
import jax.numpy as jnp
from jax import lax
from jax.experimental import pallas as pl
from jax.experimental.pallas import tpu as pltpu
from jax.sharding import PartitionSpec as P

H = 32
KV = 8
CLIP = 4096
WARMUP = 2000
THETA = 10000000.0
CHUNKS = 2
MESH = pl.DeviceIdType.MESH


BF = jnp.bfloat16
F32 = jnp.float32
HD = 64
EPS = 1e-05
NEGATIVE = -1e30
VMEM = 60 << 20

def dot(a, b, ca, cb):
    return lax.dot_general(a, b, (((ca,), (cb,)), ((), ())), preferred_element_type=F32)

def swap_halves(v):
    n = v.shape[1]
    lane = lax.broadcasted_iota(jnp.int32, v.shape, 1)
    return jnp.where(lane % HD < HD // 2, pltpu.roll(v, n - HD // 2, 1), pltpu.roll(v, HD // 2, 1))

def qkv_body(tok_ref, gain_ref, w_ref, cos_ref, sin_ref, normed_ref, q_ref, k_ref, v_ref):
    x = tok_ref[...].astype(F32)
    inv = lax.rsqrt(jnp.mean(x * x, axis=1, keepdims=True) + EPS)
    normed = (x * inv * gain_ref[...]).astype(BF)
    normed_ref[...] = normed
    lin = dot(normed, w_ref[...], 1, 0)
    heads = q_ref.shape[0]
    qc = heads * HD
    rot = lin * cos_ref[...] + swap_halves(lin) * sin_ref[...]
    for h in range(heads):
        q_ref[h] = (rot[:, h * HD : (h + 1) * HD]).astype(BF)
    k_ref[...] = rot[:, qc : qc + HD].astype(BF)
    v_ref[...] = rot[:, qc + HD :].astype(BF)

def qkv(tokens, gain, weight, cos, sin, heads, tile=256):
    count, width = tokens.shape
    cols = weight.shape[1]
    length = cos.shape[0]
    per = length // tile
    full = lambda i: (0, 0)
    row = lambda i: (i, 0)
    return pl.pallas_call(
        qkv_body,
        grid=(count // tile,),
        in_specs=[
            pl.BlockSpec((tile, width), row),
            pl.BlockSpec((1, width), full),
            pl.BlockSpec((width, cols), full),
            pl.BlockSpec((tile, cols), lambda i: (i % per, 0)),
            pl.BlockSpec((tile, cols), lambda i: (i % per, 0)),
        ],
        out_specs=[
            pl.BlockSpec((tile, width), row),
            pl.BlockSpec((heads, tile, HD), lambda i: (0, i, 0)),
            pl.BlockSpec((tile, HD), row),
            pl.BlockSpec((tile, HD), row),
        ],
        out_shape=[
            jax.ShapeDtypeStruct((count, width), BF),
            jax.ShapeDtypeStruct((heads, count, HD), BF),
            jax.ShapeDtypeStruct((count, HD), BF),
            jax.ShapeDtypeStruct((count, HD), BF),
        ],
        compiler_params=pltpu.CompilerParams(vmem_limit_bytes=VMEM),
        cost_estimate=pl.CostEstimate(flops=2 * count * width * cols, bytes_accessed=4 * count * width, transcendentals=0),
        name="qkv_rope",
    )(tokens, gain, weight, cos, sin)

def fwd_body(limits, q_ref, k_ref, v_ref, brow_ref, bcol_ref, o_ref, lse_ref):
    heads, tile, _ = q_ref.shape
    i = pl.program_id(1)
    def run(keys):
        k = k_ref[:keys]
        v = v_ref[:keys]
        allowed = brow_ref[0][:, :keys] <= bcol_ref[...]
        outs = []
        lses = []
        for h in range(heads):
            s = dot(q_ref[h] * BF(0.125), k, 1, 1)
            s = jnp.where(allowed, s, NEGATIVE)
            m = jnp.max(s, axis=1, keepdims=True)
            p = jnp.exp(s - m)
            l = jnp.sum(p, axis=1, keepdims=True)
            o = dot(p.astype(BF), v, 1, 0) / l
            outs.append(o.astype(BF))
            lses.append(m + jnp.log(l))
        o_ref[...] = jnp.concatenate(outs, axis=1)
        lse_ref[...] = jnp.concatenate(lses, axis=1)
    for n, keys in enumerate(limits):
        @pl.when(i == n)
        def _(keys=keys):
            run(keys)

def attend(q, k, v, brow, bcol, length, tile=256, most=256):
    heads, count, _ = q.shape
    seqs = count // length
    per = length // tile
    limits = tuple(min(length, (n + 1) * tile + most) for n in range(per))
    return pl.pallas_call(
        functools.partial(fwd_body, limits),
        grid=(seqs, per),
        in_specs=[
            pl.BlockSpec((heads, tile, HD), lambda b, i: (0, b * per + i, 0)),
            pl.BlockSpec((length, HD), lambda b, i: (b, 0)),
            pl.BlockSpec((length, HD), lambda b, i: (b, 0)),
            pl.BlockSpec((1, 1, length), lambda b, i: (b, 0, 0)),
            pl.BlockSpec((tile, 1), lambda b, i: (b * per + i, 0)),
        ],
        out_specs=[
            pl.BlockSpec((tile, heads * HD), lambda b, i: (b * per + i, 0)),
            pl.BlockSpec((tile, heads), lambda b, i: (b * per + i, 0)),
        ],
        out_shape=[
            jax.ShapeDtypeStruct((count, heads * HD), BF),
            jax.ShapeDtypeStruct((count, heads), F32),
        ],
        compiler_params=pltpu.CompilerParams(vmem_limit_bytes=VMEM),
        cost_estimate=pl.CostEstimate(flops=4 * heads * count * length * HD * 4, bytes_accessed=count * 2048, transcendentals=heads * count * length),
        name="attend",
    )(q, k, v, brow, bcol)

def bwd_body(
    limits,
    q_ref,
    k_ref,
    v_ref,
    brow_ref,
    bcol_ref,
    lse_ref,
    do_ref,
    cos_ref,
    sin_ref,
    kcos_ref,
    ksin_ref,
    even,
    odd,
    hidden_ref,
    dq_ref,
    dkv_ref,
    out_ref,
    dk_acc,
    dv_acc,
    *scratch
):
    heads, tile, _ = q_ref.shape
    i = pl.program_id(1)
    turn = pl.program_id(0) * pl.num_programs(1) + i
    targets = neighbours()
    job = Job(even, odd, scratch, targets)

    def produce(s, total):
        return hidden_ref[job.span(s)] + total

    @pl.when(turn == 0)
    def _():
        meet(targets)

    for t in range(8):

        @pl.when(turn == t)
        def _(t=t):
            line_turn(job, t, out_ref, produce)

    @pl.when(i == 0)
    def _():
        dk_acc[...] = jnp.zeros_like(dk_acc)
        dv_acc[...] = jnp.zeros_like(dv_acc)
    def run(keys):
        k = k_ref[:keys]
        v = v_ref[:keys]
        allowed = brow_ref[0][:, :keys] <= bcol_ref[...]
        dqs = []
        dk = jnp.zeros((HD, keys), F32)
        dv = jnp.zeros((HD, keys), F32)
        for h in range(heads):
            q = q_ref[h] * BF(0.125)
            do = do_ref[:, h * HD : (h + 1) * HD]
            s = dot(q, k, 1, 1)
            s = jnp.where(allowed, s, NEGATIVE)
            p = jnp.exp(s - lse_ref[:, h : h + 1])
            dp = dot(do, v, 1, 1)
            pdp = p * dp
            delta = jnp.sum(pdp, axis=1, keepdims=True)
            ds = (pdp - p * delta).astype(BF)
            dqs.append(dot(ds, k, 1, 0) * 0.125)
            dk = dk + dot(q, ds, 0, 0)
            dv = dv + dot(do, p.astype(BF), 0, 0)
        dk_acc[:, :keys] += dk
        dv_acc[:, :keys] += dv
        dq = jnp.concatenate(dqs, axis=1)
        dq_ref[...] = (dq * cos_ref[...] - swap_halves(dq) * sin_ref[...]).astype(BF)
    for n, keys in enumerate(limits):
        @pl.when(i == n)
        def _(keys=keys):
            run(keys)

    @pl.when(turn == 7)
    def _():
        for t in range(8, TURNS):
            line_turn(job, t, out_ref, produce)
        job.line_end(out_ref)

    @pl.when(i == len(limits) - 1)
    def _():
        both = jnp.concatenate([dk_acc[...], dv_acc[...]], axis=0).T
        dkv_ref[...] = (both * kcos_ref[...] - swap_halves(both) * ksin_ref[...]).astype(BF)

def attend_back(
    q, k, v, brow, bcol, lse, do, cos, sin, length, even, odd, hidden, tile=256, most=256
):
    heads, count, _ = q.shape
    seqs = count // length
    per = length // tile
    qc = heads * HD
    limits = tuple(min(length, (n + 1) * tile + most) for n in range(per))
    rowm = lambda b, i: (b * per + i, 0)
    return pl.pallas_call(
        functools.partial(bwd_body, limits),
        grid=(seqs, per),
        in_specs=[
            pl.BlockSpec((heads, tile, HD), lambda b, i: (0, b * per + i, 0)),
            pl.BlockSpec((length, HD), lambda b, i: (b, 0)),
            pl.BlockSpec((length, HD), lambda b, i: (b, 0)),
            pl.BlockSpec((1, 1, length), lambda b, i: (b, 0, 0)),
            pl.BlockSpec((tile, 1), rowm),
            pl.BlockSpec((tile, heads), rowm),
            pl.BlockSpec((tile, qc), rowm),
            pl.BlockSpec((tile, qc), lambda b, i: (i, 0)),
            pl.BlockSpec((tile, qc), lambda b, i: (i, 0)),
            pl.BlockSpec((length, 2 * HD), lambda b, i: (0, qc // (2 * HD))),
            pl.BlockSpec((length, 2 * HD), lambda b, i: (0, qc // (2 * HD))),
            IN_VMEM,
            ANY,
            IN_VMEM,
        ],
        out_specs=[
            pl.BlockSpec((tile, qc), rowm),
            pl.BlockSpec((length, 2 * HD), lambda b, i: (b, 0)),
            ANY,
        ],
        out_shape=[
            jax.ShapeDtypeStruct((count, qc), BF),
            jax.ShapeDtypeStruct((count, 2 * HD), BF),
            jax.ShapeDtypeStruct((length, even.shape[2]), BF),
        ],
        scratch_shapes=[pltpu.VMEM((HD, length), F32), pltpu.VMEM((HD, length), F32)]
        + Job.scratch(even.shape[1], even.shape[2]),
        compiler_params=pltpu.CompilerParams(
            collective_id=7, has_side_effects=True, vmem_limit_bytes=VMEM
        ),
        cost_estimate=pl.CostEstimate(flops=10 * heads * count * length * HD * 4, bytes_accessed=count * 4096, transcendentals=heads * count * length),
        name="attend_back",
    )(q, k, v, brow, bcol, lse, do, cos, sin, cos, sin, even, odd, hidden)

def rope_tables(length, heads):
    positions = jnp.arange(length, dtype=jnp.int32).astype(F32)
    powers = -2.0 * jnp.arange(HD // 2, dtype=F32) / HD
    angles = positions[:, None] * jnp.power(THETA, powers)[None, :]
    c = jnp.cos(angles); s = jnp.sin(angles)
    cos = jnp.concatenate([jnp.tile(jnp.concatenate([c, c], axis=1), (1, heads + 1)), jnp.ones((length, HD), F32)], axis=1)
    sin = jnp.concatenate([jnp.tile(jnp.concatenate([-s, s], axis=1), (1, heads + 1)), jnp.zeros((length, HD), F32)], axis=1)
    return cos, sin

def up_body(first, last, n2_ref, cot_ref, w_ref, *rest):
    if first:
        act_ref, dgu_ref, part_ref = rest
    else:
        prev_ref, act_ref, dgu_ref, part_ref = rest
    size = act_ref.shape[1]
    gu = dot(n2_ref[...], w_ref[:, : 2 * size], 1, 0)
    da = dot(cot_ref[...], w_ref[:, 2 * size :], 1, 0)
    gate, up = gu[:, :size], gu[:, size:]
    sig = 1.0 / (1.0 + jnp.exp(-gate))
    gs = gate * sig
    act_ref[...] = (gs * up).astype(BF)
    dg = (da * up * sig * (1.0 + gate * (1.0 - sig))).astype(BF)
    du = (da * gs).astype(BF)
    dgu = jnp.concatenate([dg, du], axis=1)
    dgu_ref[...] = dgu
    part = dot(dgu, w_ref[:, : 2 * size], 1, 1)
    if not first:
        part = part + prev_ref[...]
    part_ref[...] = part.astype(part_ref.dtype)

def up_back(n2, cot, weight, prev, last, tile=256):
    count, width = n2.shape
    size = weight.shape[1] // 3
    row = lambda i: (i, 0)
    full = lambda i: (0, 0)
    ins = [n2, cot, weight] + ([] if prev is None else [prev])
    specs = [pl.BlockSpec((tile, width), row), pl.BlockSpec((tile, width), row), pl.BlockSpec((width, 3 * size), full, pipeline_mode=pl.Buffered(1))]
    if prev is not None:
        specs.append(pl.BlockSpec((tile, width), row))
    return pl.pallas_call(
        functools.partial(up_body, prev is None, last),
        grid=(count // tile,),
        in_specs=specs,
        out_specs=[pl.BlockSpec((tile, size), row), pl.BlockSpec((tile, 2 * size), row), pl.BlockSpec((tile, width), row)],
        out_shape=[jax.ShapeDtypeStruct((count, size), BF), jax.ShapeDtypeStruct((count, 2 * size), BF), jax.ShapeDtypeStruct((count, width), BF if last else F32)],
        compiler_params=pltpu.CompilerParams(vmem_limit_bytes=VMEM),
        cost_estimate=pl.CostEstimate(flops=2 * count * width * size * 5, bytes_accessed=12 * count * width, transcendentals=count * size),
        name="swiglu_part",
    )(*ins)

def grad_body(n2a, n2b, cota, cotb, dgua, dgub, acta, actb, o_ref):
    size = acta.shape[1]
    gu = dot(n2a[...], dgua[...], 0, 0) + dot(n2b[...], dgub[...], 0, 0)
    o_ref[:, : 2 * size] = gu.astype(BF)
    dt = dot(cota[...], acta[...], 0, 0) + dot(cotb[...], actb[...], 0, 0)
    o_ref[:, 2 * size :] = dt.astype(BF)


def ffn_grads(n2, cot, dgu, act, tile=256):
    count, width = n2[0].shape
    size = act[0].shape[1]
    col = lambda i: (0, i)
    full = lambda i: (0, 0)
    return pl.pallas_call(
        grad_body,
        grid=(width // tile,),
        in_specs=[pl.BlockSpec((count, tile), col)] * 4
        + [pl.BlockSpec((count, 2 * size), full, pipeline_mode=pl.Buffered(1))] * 2
        + [pl.BlockSpec((count, size), full, pipeline_mode=pl.Buffered(1))] * 2,
        out_specs=pl.BlockSpec((tile, 3 * size), lambda i: (i, 0)),
        out_shape=jax.ShapeDtypeStruct((width, 3 * size), BF),
        compiler_params=pltpu.CompilerParams(vmem_limit_bytes=VMEM),
        cost_estimate=pl.CostEstimate(
            flops=4 * count * width * size * 3,
            bytes_accessed=16 * count * width,
            transcendentals=0,
        ),
        name="swiglu_grads",
    )(*n2, *cot, *dgu, *act)


def attn_grad_body(na, ga, ha, hb, ma, mb, o_ref):
    cols = ga.shape[1]
    o_ref[:, :cols] = dot(na[...], ga[...], 0, 0).astype(BF)
    o_ref[:, cols:] = (dot(ha[...], ma[...], 0, 0) + dot(hb[...], mb[...], 0, 0)).astype(BF)


def attn_grads(normed, grads, hidden, mixed, tile=256):
    width = normed.shape[1]
    col = lambda i: (0, i)
    ins = [normed, grads, *hidden, *mixed]
    cols = grads.shape[1] + mixed[0].shape[1]

    def tiled(value):
        return pl.BlockSpec((value.shape[0], tile), col)

    def whole(value):
        return pl.BlockSpec(value.shape, lambda i: (0, 0), pipeline_mode=pl.Buffered(1))

    return pl.pallas_call(
        attn_grad_body,
        grid=(width // tile,),
        in_specs=[tiled(normed), whole(grads)]
        + [tiled(v) for v in hidden]
        + [whole(v) for v in mixed],
        out_specs=pl.BlockSpec((tile, cols), lambda i: (i, 0)),
        out_shape=jax.ShapeDtypeStruct((width, cols), BF),
        compiler_params=pltpu.CompilerParams(vmem_limit_bytes=VMEM),
        cost_estimate=pl.CostEstimate(
            flops=2 * normed.shape[0] * width * cols,
            bytes_accessed=8 * normed.shape[0] * width,
            transcendentals=0,
        ),
        name="attn_grads",
    )(*ins)


def peers(dps, shards):
    dp, sh = lax.axis_index("dp"), lax.axis_index("shard")
    groups = dps // 2
    near = []
    for r in range(1, 2 * shards):
        there = sh
        for bit in (1, 2):
            there = flip(there, bit) if r % shards & bit else there
        near.append((flip(dp, 1) if r >= shards else dp, there))
    far = [
        (lax.rem(dp // 2 + p, groups) * 2 + lax.rem(dp, 2), sh) for p in range(1, groups)
    ]
    return near, far, lax.rem(dp, 2) * shards + sh, dp // 2


def meet(targets):
    barrier = pltpu.get_barrier_semaphore()
    for target in targets:
        pl.semaphore_signal(barrier, inc=1, device_id=target, device_id_type=MESH)
    pl.semaphore_wait(barrier, len(targets))


def exchange(values, slots, mine, targets, source, send, recv, base):
    source[...] = values
    slots[mine] = values
    copies = [
        pltpu.make_async_remote_copy(
            src_ref=source,
            dst_ref=slots.at[mine],
            send_sem=send.at[base + n],
            recv_sem=recv.at[base + n],
            device_id=target,
            device_id_type=MESH,
        )
        for n, target in enumerate(targets)
    ]
    for copy in copies:
        copy.start()
    for copy in copies:
        copy.wait()
    total = slots[0]
    for n in range(1, slots.shape[0]):
        total = total + slots[n]
    return total


def two_stages(values, near, far, me, outer, bufs):
    slots_near, slots_far, from_near, from_far, send, recv = bufs
    total = exchange(values, slots_near, me, near, from_near, send, recv, 0)
    return exchange(total, slots_far, outer, far, from_far, send, recv, len(near))


def sum_scratch(shape, dps, shards):
    count = 2 * shards - 1 + dps // 2 - 1
    return [
        pltpu.VMEM((2 * shards,) + shape, F32),
        pltpu.VMEM((dps // 2,) + shape, F32),
        pltpu.VMEM(shape, F32),
        pltpu.VMEM(shape, F32),
        pltpu.SemaphoreType.DMA((count,)),
        pltpu.SemaphoreType.DMA((count,)),
    ]


def pick(x, first, second):
    low = jnp.where(x == 0, first.astype(F32), second.astype(F32)).astype(BF)
    high = jnp.where(x == 0, second.astype(F32), first.astype(F32)).astype(BF)
    return low, high


def finish_body(dps, shards, count, piece_ref, theirs, sq_ref, *refs):
    ins, outs, scratch = refs[: 2 * count], refs[2 * count : 2 * count + 8], refs[2 * count + 8 :]
    q_ref, k_ref, v_ref, o_ref, g_ref, u_ref, d_ref, norm_ref = outs
    bufs = scratch
    near, far, me, outer = peers(dps, shards)
    rows = piece_ref.shape[0] // 2
    qc = q_ref.shape[1] // 2
    x = lax.rem(lax.axis_index("dp"), 2)
    here = pl.ds(pl.multiple_of(x * rows, rows), rows)
    squares = jnp.zeros((1, 1), F32)
    half = g_ref.shape[1] // 2
    at = 0
    for j in range(count):
        size = ins[2 * j].shape[1] // 3
        for h, piece in enumerate(pick(x, ins[2 * j][here, :], ins[2 * j + 1][...])):
            wide = piece.astype(F32)
            squares = squares + jnp.sum(wide * wide, keepdims=True)
            span = pl.ds(h * half + at, size)
            g_ref[:, span] = piece[:, :size]
            u_ref[:, span] = piece[:, size : 2 * size]
            d_ref[span, :] = wide[:, 2 * size :].T.astype(BF)
        at = at + size
    mine = piece_ref[here, :]
    wide = mine.astype(F32)
    squares = squares + jnp.sum(wide * wide, keepdims=True)
    got = theirs[...]
    wide = got.astype(F32)
    squares = squares + jnp.sum(wide * wide, keepdims=True)
    values = sq_ref[...] + jnp.broadcast_to(squares, sq_ref.shape)
    meet(near + far)
    norm_ref[...] = jnp.sqrt(two_stages(values, near, far, me, outer, bufs))
    low, high = pick(x, mine, got)
    q_ref[:, :qc] = low[:, :qc]
    q_ref[:, qc:] = high[:, :qc]
    k_ref[...] = jnp.concatenate([low[:, qc : qc + HD], high[:, qc : qc + HD]], axis=1)
    vc, oc = qc + HD, qc + 2 * HD
    v_ref[...] = jnp.concatenate([low[:, vc:oc], high[:, vc:oc]], axis=1)
    o_ref[:qc] = low[:, oc:].astype(F32).T.astype(BF)
    o_ref[qc:] = high[:, oc:].astype(F32).T.astype(BF)


def finish(piece, theirs, squares, pairs, dps, shards, number):
    rows, cols = piece.shape[0] // 2, piece.shape[1]
    qc = (cols - 2 * HD) // 2
    wide = 2 * sum(other.shape[1] // 3 for _, other in pairs)
    vmem = pl.BlockSpec(memory_space=pltpu.VMEM)
    ins = [v for pair in pairs for v in pair]
    shapes = ((rows, 2 * qc), (rows, 2 * HD), (rows, 2 * HD), (2 * qc, rows))
    shapes = shapes + ((rows, wide), (rows, wide), (wide, rows))
    return pl.pallas_call(
        functools.partial(finish_body, dps, shards, len(pairs)),
        in_specs=[vmem] * (3 + len(ins)),
        out_specs=[vmem] * 8,
        out_shape=[jax.ShapeDtypeStruct(shape, BF) for shape in shapes]
        + [jax.ShapeDtypeStruct(squares.shape, F32)],
        scratch_shapes=sum_scratch(squares.shape, dps, shards),
        compiler_params=pltpu.CompilerParams(
            collective_id=number, has_side_effects=True, vmem_limit_bytes=VMEM
        ),
        name="finish",
    )(piece, theirs, squares, *ins)


PARTS = 8


def flip(value, bit):
    return value + bit * (1 - 2 * lax.rem(value // bit, 2))


def neighbours():
    dp, sh = lax.axis_index("dp"), lax.axis_index("shard")
    return (flip(dp, 1), sh), (dp, flip(sh, 2)), (dp, flip(sh, 1))


def remote(src, dst, sems, n, target):
    return pltpu.make_async_remote_copy(
        src_ref=src,
        dst_ref=dst,
        send_sem=sems.at[0, n],
        recv_sem=sems.at[1, n],
        device_id=target,
        device_id_type=MESH,
    )


class Job:

    def __init__(self, even, odd, scratch, targets, y_first=()):
        self.y_first = y_first
        self.even, self.odd = even, odd
        self.got, self.out1, self.in1, self.out2, self.in2, self.own, self.sems, self.local = scratch
        self.x, self.y, self.core = targets
        self.rows = even.shape[1] // PARTS

    @staticmethod
    def scratch(rows, width):
        part = rows // PARTS
        return [
            pltpu.VMEM((4, rows, width), BF),
            pltpu.VMEM((PARTS, 2, part, width), BF),
            pltpu.VMEM((PARTS, 2, part, width), BF),
            pltpu.VMEM((PARTS, part, width), BF),
            pltpu.VMEM((PARTS, part, width), BF),
            pltpu.VMEM((rows, width), BF),
            pltpu.SemaphoreType.DMA((2, 6 * PARTS)),
            pltpu.SemaphoreType.DMA((PARTS,)),
        ]

    def span(self, s):
        return pl.ds(s * self.rows, self.rows)

    def over_x(self, s):
        return s not in self.y_first

    def copy(self, stage, s, src, dst, target):
        return remote(src, dst, self.sems, stage * PARTS + s, target)

    def to_core(self, s):
        span = self.span(s)
        return self.copy(0, s, self.odd.at[:, span], self.got.at[:, span], self.core)

    def to_first(self, s):
        target = self.x if self.over_x(s) else self.y
        return self.copy(1, s, self.out1.at[s], self.in1.at[s], target)

    def to_second(self, s):
        target = self.y if self.over_x(s) else self.x
        return self.copy(2, s, self.out2.at[s], self.in2.at[s], target)

    def start(self):
        for s in range(4):
            self.to_core(s).start()

    def pair(self, k, s):
        return self.even[k, self.span(s)].astype(F32) + self.got[k, self.span(s)].astype(F32)

    def first(self, s):
        self.to_core(s).wait_recv()
        if s + 4 < PARTS:
            self.to_core(s + 4).start()
        self.out1[s, 0] = self.pair(2 if self.over_x(s) else 1, s).astype(BF)
        self.out1[s, 1] = self.pair(3, s).astype(BF)
        self.to_first(s).start()

    def second(self, s):
        self.to_first(s).wait_recv()
        near = self.pair(1 if self.over_x(s) else 2, s)
        self.out2[s] = (near + self.in1[s, 1].astype(F32)).astype(BF)
        self.to_second(s).start()

    def total(self, s):
        self.to_second(s).wait_recv()
        return self.pair(0, s) + self.in1[s, 0].astype(F32) + self.in2[s].astype(F32)

    def sent(self):
        for s in range(PARTS):
            self.to_core(s).wait_send()
            self.to_first(s).wait_send()
            self.to_second(s).wait_send()


    def keep(self, s, place):
        return pltpu.make_async_copy(self.own.at[self.span(s)], place, self.local.at[s])

    def spread_copies(self, s, mine, theirs):
        span = self.span(s)
        own = self.own.at[span]
        if self.over_x(s):
            near = self.copy(3, s, own, mine.at[1, 0, span], self.x)
            far = self.copy(4, s, mine.at[:, 0, span], mine.at[:, 1, span], self.y)
        else:
            near = self.copy(3, s, own, mine.at[0, 1, span], self.y)
            far = self.copy(4, s, mine.at[0, :, span], mine.at[1, :, span], self.x)
        core = self.copy(5, s, mine.at[:, :, span], theirs.at[:, :, span], self.core)
        return self.keep(s, mine.at[0, 0, span]), near, far, core


    def line_copies(self, s, whole):
        me = lax.axis_index("shard")
        size = self.rows * PARTS

        def place(owner):
            at = pl.multiple_of(owner * size + s * self.rows, self.rows)
            return whole.at[pl.ds(at, self.rows)]

        own = self.own.at[self.span(s)]
        near = self.copy(3, s, own, place(me), self.y)
        core = self.copy(4, s, own, place(me), self.core)
        other = place(flip(me, 2))
        return self.keep(s, place(me)), near, core, self.copy(5, s, other, other, self.core)

    def line_start(self, s, whole):
        for copy in self.line_copies(s, whole)[:3]:
            copy.start()

    def line_core(self, s, whole):
        keep, near, core, far = self.line_copies(s, whole)
        keep.wait()
        near.wait_recv()
        far.start()

    def line_end(self, whole):
        for s in range(PARTS):
            _, near, core, far = self.line_copies(s, whole)
            core.wait_recv()
            far.wait_recv()
            for copy in (near, core, far):
                copy.wait_send()
        self.sent()


def run_job(job, mine, theirs, produce, hook, window=4, lag=2):
    copies = [job.spread_copies(s, mine, theirs) for s in range(PARTS)]
    job.start()
    for s in range(window):
        job.first(s)
    for t in range(PARTS + 3 * lag):
        hook(t)
        if t < PARTS:
            job.second(t)
            if t + window < PARTS:
                job.first(t + window)
        if 0 <= t - lag < PARTS:
            s = t - lag
            job.own[job.span(s)] = produce(s, job.total(s)).astype(BF)
            copies[s][0].start()
            copies[s][1].start()
        if 0 <= t - 2 * lag < PARTS:
            keep, near, far, _ = copies[t - 2 * lag]
            keep.wait()
            near.wait_recv()
            far.start()
        if 0 <= t - 3 * lag < PARTS:
            _, _, far, core = copies[t - 3 * lag]
            far.wait_recv()
            core.start()
    for _, near, far, core in copies:
        core.wait_recv()
        for copy in (near, far, core):
            copy.wait_send()
    job.sent()


def line_turn(job, t, whole, produce, window=4, lag=2):
    if t == 0:
        job.start()
        for s in range(window):
            job.first(s)
    if 0 <= t - 1 < PARTS:
        job.second(t - 1)
        if t - 1 + window < PARTS:
            job.first(t - 1 + window)
    if 0 <= t - 1 - lag < PARTS:
        s = t - 1 - lag
        job.own[job.span(s)] = produce(s, job.total(s)).astype(BF)
        job.line_start(s, whole)
    if 0 <= t - 1 - 2 * lag < PARTS:
        job.line_core(t - 1 - 2 * lag, whole)


TURNS = PARTS + 5


def rms_of(values):
    return lax.rsqrt(jnp.mean(values * values, axis=1, keepdims=True) + EPS)


def norm_back_of(values, gain, grad):
    inverse = rms_of(values)
    scaled = grad * gain
    total = jnp.sum(grad * values * inverse, axis=0, keepdims=True)
    mean = jnp.mean(scaled * values, axis=1, keepdims=True)
    return total, inverse * scaled - values * (inverse * inverse * inverse * mean)


def mid_body(even, odd, tok_ref, gain_ref, mine, theirs, hidden_ref, *scratch):
    targets = neighbours()
    meet(targets)
    job = Job(even, odd, scratch, targets, range(1, PARTS, 2))

    def produce(s, total):
        hidden = tok_ref[job.span(s)].astype(F32) + total
        hidden_ref[job.span(s)] = hidden
        return hidden * rms_of(hidden) * gain_ref[...]

    run_job(job, mine, theirs, produce, lambda t: None)


def back_body(even, odd, hidden_ref, cot_ref, gain_ref, *rest):
    chunks = CHUNKS
    count = 6 + 3 * chunks
    ins, outs, scratch = rest[:count], rest[count : count + 7], rest[count + 7 :]
    mine, theirs, gh_ref, gg_ref, dw_ref, down_a, down_b = outs
    held = scratch[8 : 8 + count]
    tiles, store, load, down_tiles, down_store = scratch[8 + count :]
    targets = neighbours()
    loads = []
    for n, (src, dst) in enumerate(zip(ins, held)):
        wide = src.shape[1] - dst.shape[1]
        src = src.at[:, pl.ds(wide, dst.shape[1])] if wide else src
        loads.append(pltpu.make_async_copy(src, dst, load.at[n]))
    for copy in loads:
        copy.start()
    meet(targets)
    job = Job(even, odd, scratch[:8], targets, range(1, PARTS, 2))
    na, nb, ca, cb, ga, gb = held[:6]
    acts_a, acts_b, downs = held[6 : 6 + chunks], held[6 + chunks : 6 + 2 * chunks], held[6 + 2 * chunks :]
    aa, ab = acts_a[-1], acts_b[-1]
    size = aa.shape[1]
    step = tiles.shape[1]
    sites = 4
    half = dw_ref.shape[0] // step // sites
    rows = down_tiles.shape[1]

    def filler(part):
        if part == 0:
            for copy in loads:
                copy.wait()

        def tile(n, carry):
            cols = pl.ds(pl.multiple_of((part * half + n) * step, step), step)
            gu = dot(na[:, cols], ga[...], 0, 0) + dot(nb[:, cols], gb[...], 0, 0)
            tiles[n, :, : 2 * size] = gu.astype(BF)
            dt = dot(ca[:, cols], aa[...], 0, 0) + dot(cb[:, cols], ab[...], 0, 0)
            tiles[n, :, 2 * size :] = dt.astype(BF)
            pltpu.make_async_copy(tiles.at[n], dw_ref.at[cols], store.at[n]).start()
            return carry

        lax.fori_loop(0, half, tile, 0)
        span = pl.ds(part * rows, rows)
        for n, (acts, out) in enumerate(((acts_a, down_a), (acts_b, down_b))):
            total = dot(acts[0][span], downs[0][...], 1, 1)
            for j in range(1, chunks):
                total = total + dot(acts[j][span], downs[j][...], 1, 1)
            down_tiles[n] = total.astype(BF)
            pltpu.make_async_copy(down_tiles.at[n], out.at[span], down_store.at[n]).start()

    def settle(part):
        span = pl.ds(part * rows, rows)
        for n in range(half):
            cols = pl.ds((part * half + n) * step, step)
            pltpu.make_async_copy(tiles.at[n], dw_ref.at[cols], store.at[n]).wait()
        for n, out in enumerate((down_a, down_b)):
            pltpu.make_async_copy(down_tiles.at[n], out.at[span], down_store.at[n]).wait()

    def hook(t):
        if t % 2 == 0 and t // 2 < sites:
            if t > 0:
                settle(t // 2 - 1)
            filler(t // 2)

    totals = []

    def produce(s, total):
        gain_total, through = norm_back_of(hidden_ref[job.span(s)], gain_ref[...], total)
        totals.append(gain_total)
        grad_hidden = cot_ref[job.span(s)].astype(F32) + through
        gh_ref[job.span(s)] = grad_hidden
        return grad_hidden

    run_job(job, mine, theirs, produce, hook)
    settle(sites - 1)
    gg_ref[...] = sum(totals[1:], totals[0])


def trade(piece, theirs, sems):
    size = theirs.shape[0]
    x = lax.rem(lax.axis_index("dp"), 2)
    src = piece.at[pl.ds(pl.multiple_of((1 - x) * size, size), size)]
    return remote(src, theirs, sems, 0, neighbours()[0])


def end_body(
    dps, shards, even, odd, tok_ref, gh_ref, gain_ref, gg_ref, piece, in_ref, sum_ref, theirs, *scratch
):
    near, far, me, outer = peers(dps, shards)
    meet(near + far)
    job = Job(even, odd, scratch[:8], neighbours(), (1, 4, 7))
    swapped = trade(piece, theirs, scratch[8])
    totals = []

    def produce(s, total):
        span = job.span(s)
        gain_total, through = norm_back_of(tok_ref[span].astype(F32), gain_ref[...], total)
        totals.append(gain_total)
        return gh_ref[span] + through

    for t in range(TURNS):
        line_turn(job, t, in_ref, produce)
        if t == 4:
            swapped.start()
    gains = jnp.concatenate([sum(totals[1:], totals[0]), gg_ref[...]], axis=0)
    sum_ref[...] = two_stages(gains, near, far, me, outer, scratch[9:])
    job.line_end(in_ref)
    swapped.wait()


def entry_body(tok_ref, keep_ref, send_ref, both, piece, hop_x, hop_y, hop_core, weight_sem, keeps):
    xs, ys, core = neighbours()
    sh = lax.axis_index("shard")
    x = lax.rem(lax.axis_index("dp"), 2)
    length = tok_ref.shape[0]
    quarter = length // 4
    rows = quarter // PARTS
    size = keep_ref.shape[0]
    mine = piece.at[pl.ds(pl.multiple_of(x * size, size), size)]
    local = [
        pltpu.make_async_copy(keep_ref, mine, keeps.at[0]),
        pltpu.make_async_copy(tok_ref, both.at[pl.ds(0, length)], keeps.at[1]),
    ]
    for copy in local:
        copy.start()
    meet((xs, ys, core))

    def rows_of(ref, base, owner, s):
        return ref.at[pl.ds(pl.multiple_of(base + owner * quarter + s * rows, rows), rows)]

    over_x, over_y, over_core, over_far = [], [], [], []
    for s in range(PARTS):
        near, far = rows_of(both, length, sh, s), rows_of(both, length, flip(sh, 2), s)
        over_x.append(remote(rows_of(tok_ref, 0, sh, s), near, hop_x, s, xs))
        over_y.append(remote(near, near, hop_y, s, ys))
        over_core.append(remote(near, near, hop_core, s, core))
        over_far.append(remote(far, far, hop_core, PARTS + s, core))
    moving = remote(send_ref, mine, weight_sem, 0, xs)
    for copy in over_x:
        copy.start()
    moving.start()
    for s in range(PARTS):
        over_x[s].wait_recv()
        over_y[s].start()
        over_core[s].start()
    for s in range(PARTS):
        over_y[s].wait_recv()
        over_far[s].start()
    moving.wait()
    for copy in over_core + over_far:
        copy.wait()
    for copy in over_x + over_y:
        copy.wait_send()
    for copy in local:
        copy.wait()


def entry(tokens, keep, sent):
    length, width = tokens.shape
    dma = pltpu.SemaphoreType.DMA
    return pl.pallas_call(
        entry_body,
        in_specs=[ANY] * 3,
        out_specs=[ANY] * 2,
        out_shape=[
            jax.ShapeDtypeStruct((2 * length, width), BF),
            jax.ShapeDtypeStruct((2 * keep.shape[0], keep.shape[1]), BF),
        ],
        scratch_shapes=[
            dma((2, PARTS)),
            dma((2, PARTS)),
            dma((2, 2 * PARTS)),
            dma((2, 1)),
            dma((2,)),
        ],
        compiler_params=pltpu.CompilerParams(
            collective_id=6, has_side_effects=True, vmem_limit_bytes=8 << 20
        ),
        name="entry",
    )(tokens, keep, sent)


ANY = pl.BlockSpec(memory_space=pl.ANY)
IN_VMEM = pl.BlockSpec(memory_space=pltpu.VMEM)
BIG = 60 << 20


def mid_stage(even, odd, tokens_own, gain):
    _, rows, width = even.shape
    half = jax.ShapeDtypeStruct((2, 2, rows, width), BF)
    return pl.pallas_call(
        mid_body,
        in_specs=[IN_VMEM, ANY, IN_VMEM, IN_VMEM],
        out_specs=[ANY, ANY, IN_VMEM],
        out_shape=[half, half, jax.ShapeDtypeStruct((rows, width), F32)],
        scratch_shapes=Job.scratch(rows, width),
        compiler_params=pltpu.CompilerParams(
            collective_id=3, has_side_effects=True, vmem_limit_bytes=VMEM
        ),
        name="mid_stage",
    )(even, odd, tokens_own, gain)


def back_stage(even, odd, hidden, cot_own, gain, halves, acts, weights, tile=256):
    _, rows, width = even.shape
    count = halves[0].shape[0]
    sizes = [act.shape[1] for act in acts[0]]
    filling = list(halves) + list(acts[0]) + list(acts[1]) + list(weights)
    held = [pltpu.VMEM(v.shape, BF) for v in filling[: 6 + 2 * len(sizes)]]
    held += [pltpu.VMEM((width, size), BF) for size in sizes]
    spread_shape = jax.ShapeDtypeStruct((2, 2, rows, width), BF)
    down_shape = jax.ShapeDtypeStruct((count, width), BF)
    dma = pltpu.SemaphoreType.DMA
    return pl.pallas_call(
        back_body,
        in_specs=[IN_VMEM, ANY, IN_VMEM, IN_VMEM, IN_VMEM] + [ANY] * len(filling),
        out_specs=[ANY, ANY, IN_VMEM, IN_VMEM, ANY, ANY, ANY],
        out_shape=[
            spread_shape,
            spread_shape,
            jax.ShapeDtypeStruct((rows, width), F32),
            jax.ShapeDtypeStruct((1, width), F32),
            jax.ShapeDtypeStruct((width, 3 * sizes[-1]), BF),
            down_shape,
            down_shape,
        ],
        scratch_shapes=Job.scratch(rows, width)
        + held
        + [
            pltpu.VMEM((width // tile // 4, tile, 3 * sizes[-1]), BF),
            dma((width // tile // 4,)),
            dma((len(filling),)),
            pltpu.VMEM((2, count // 4, width), BF),
            dma((2,)),
        ],
        compiler_params=pltpu.CompilerParams(
            collective_id=4, has_side_effects=True, vmem_limit_bytes=BIG
        ),
        name="back_stage",
    )(even, odd, hidden, cot_own, gain, *filling)


def end_stage(even, odd, tokens_own, grad_hidden, gain, gain_grad, piece, dps, shards):
    _, rows, width = even.shape
    theirs = jax.ShapeDtypeStruct((piece.shape[0] // 2, piece.shape[1]), BF)
    return pl.pallas_call(
        functools.partial(end_body, dps, shards),
        in_specs=[IN_VMEM, ANY] + [IN_VMEM] * 4 + [ANY],
        out_specs=[ANY, IN_VMEM, ANY],
        out_shape=[
            jax.ShapeDtypeStruct((shards * rows, width), BF),
            jax.ShapeDtypeStruct((2, width), F32),
            theirs,
        ],
        scratch_shapes=Job.scratch(rows, width)
        + [pltpu.SemaphoreType.DMA((2, 1))]
        + sum_scratch((2, width), dps, shards),
        compiler_params=pltpu.CompilerParams(
            collective_id=5, has_side_effects=True, vmem_limit_bytes=VMEM
        ),
        name="end_stage",
    )(even, odd, tokens_own, grad_hidden, gain, gain_grad, piece)


def update_body(count, norm_ref, rate_ref, *refs):
    factor = jnp.minimum(1.0, CLIP / norm_ref[0:1, 0:1])
    rate = rate_ref[0]
    for n in range(count):
        master, moment, grad = (refs[3 * n + k] for k in range(3))
        new_moment, new_master = refs[3 * count + 2 * n], refs[3 * count + 2 * n + 1]
        momentum = 0.5 * moment[...] + 0.5 * (factor * grad[...].astype(F32))
        new_moment[...] = momentum
        new_master[...] = master[...] - rate * momentum


def update(norm, rate, masters, moments, grads, steps=8):
    count = len(masters)

    def block(value):
        if value.shape[0] == 1:
            return pl.BlockSpec(value.shape, lambda i: (0, 0))
        return pl.BlockSpec((value.shape[0] // steps, value.shape[1]), lambda i: (i, 0))

    ins = [v for triple in zip(masters, moments, grads) for v in triple]
    outs = [v for master in masters for v in (master, master)]
    values = pl.pallas_call(
        functools.partial(update_body, count),
        grid=(steps,),
        in_specs=[
            pl.BlockSpec(norm.shape, lambda i: (0, 0)),
            pl.BlockSpec(memory_space=pltpu.SMEM),
        ]
        + [block(v) for v in ins],
        out_specs=[block(v) for v in outs],
        out_shape=[jax.ShapeDtypeStruct(v.shape, F32) for v in outs],
        compiler_params=pltpu.CompilerParams(vmem_limit_bytes=VMEM),
        name="update",
    )(norm, rate.reshape(1), *ins)
    return values[0::2], values[1::2]


def after(*values):
    return lax.optimization_barrier(values)


def build(dps, shards):
    total = dps * shards
    axes = ("dp", "shard")
    zgroups = [[i for i in range(dps) if i % 2 == p] for p in (0, 1)]

    def swap(values, dx, ds):
        pairs = [
            (i, ((i // shards) ^ dx) * shards + ((i % shards) ^ ds)) for i in range(total)
        ]
        return lax.ppermute(values, axes, pairs)

    def gather(piece):
        return lax.all_gather(piece, "dp", axis=0, tiled=True, axis_index_groups=zgroups)

    def scatter(whole):
        return lax.psum_scatter(
            whole, "dp", scatter_dimension=0, tiled=True, axis_index_groups=zgroups
        )


    def on_device(
        tokens,
        block_ids,
        cotangent,
        gain_first,
        w_query,
        w_key,
        w_value,
        w_output,
        gain_second,
        w_gate,
        w_up,
        w_down,
        moment_first,
        moment_query,
        moment_key,
        moment_value,
        moment_output,
        moment_second,
        moment_gate,
        moment_up,
        moment_down,
        step,
        rate,
    ):
        length = block_ids.shape[1]
        width = tokens.shape[1]
        group = H // KV
        dp = lax.axis_index("dp")
        me = lax.axis_index("shard")
        x = lax.rem(dp, 2)
        quarter = length // shards
        rows = w_query.shape[0]

        def half(values, which):
            size = values.shape[1] // 2
            return lax.dynamic_slice_in_dim(values, which * size, size, axis=1)

        def ordered(mine, theirs, axis=0):
            first = jnp.where(x == 0, mine, theirs)
            second = jnp.where(x == 0, theirs, mine)
            return jnp.concatenate([first, second], axis=axis)

        def natural(parts):
            stacked = jnp.stack(parts)
            return jnp.concatenate(
                [
                    lax.dynamic_index_in_dim(stacked, me ^ q, axis=0, keepdims=False)
                    for q in range(shards)
                ],
                axis=0,
            )

        def cut(values, ds):
            return lax.dynamic_slice_in_dim(values, (me ^ ds) * quarter, quarter, axis=0)

        def halves(own, other):
            return [
                jnp.stack([cut(own, dc), cut(own, dc + 2), cut(other, dc), cut(other, dc + 2)])
                for dc in (0, 1)
            ]

        def streams(mine, theirs):
            return [
                natural([mine[k], theirs[k], mine[k + 1], theirs[k + 1]]) for k in (0, 2)
            ]

        def flat(values):
            return values.reshape(-1, values.shape[-1])

        low_q = w_query.astype(BF)
        low_k = w_key.astype(BF)
        low_v = w_value.astype(BF)
        low_o = w_output.astype(BF).T
        qc = group * HD
        cols = qc + 2 * HD

        def attn_half(which):
            return jnp.concatenate([half(low, which) for low in (low_q, low_k, low_v, low_o)], axis=1)

        gains = jnp.stack([gain_first, gain_second]).astype(BF)
        gains = jnp.pad(gains, ((0, 14), (0, cols + qc - rows)))
        sent = swap(jnp.concatenate([attn_half(1 - x), gains], axis=0), 1, 0)
        piece = jnp.concatenate(
            [ordered(attn_half(x), sent[:rows]), ordered(gains, sent[rows:])], axis=0
        )
        groups = dps // 2

        blocks_x = swap(block_ids, 1, 0)
        low_g = w_gate.astype(BF)
        low_u = w_up.astype(BF)
        low_d = w_down.astype(BF).T
        units = low_g.shape[1] // 2
        sizes = (units * 5 // 8, units * 3 // 8)
        offsets = (0, sizes[0])

        def ffn_part(which, j):
            return jnp.concatenate(
                [
                    lax.dynamic_slice_in_dim(low, which * units + offsets[j], sizes[j], axis=1)
                    for low in (low_g, low_u, low_d)
                ],
                axis=1,
            )

        both, first_part = entry(
            after(tokens, piece)[0], ffn_part(x, 0), ffn_part(1 - x, 0)
        )
        ffn_weights = [gather(first_part)]
        cot_own = [cut(cotangent, ds) for ds in range(shards)]
        packed, both, send_cot = after(gather(piece), both, cot_own[0])
        cot_x = swap(send_cot, 1, 0)
        packed = packed.reshape(groups, 2 * rows + 32, cols + qc)
        qkv_weight = packed[:, : 2 * rows, :cols].reshape(width, cols)
        out_weight = packed[:, : 2 * rows, cols:].reshape(width, qc)
        tails = packed[:, 2 * rows :].reshape(groups, 2, 16, cols + qc)
        gain_one = tails[:, :, 0, :rows].reshape(1, width).astype(F32)
        gain_two = tails[:, :, 1, :rows].reshape(1, width).astype(F32)

        cosine, sine = rope_tables(length, group)

        normed, query, key, value = qkv(both, gain_one, qkv_weight, cosine, sine, group)
        query, cot_x, send_second = after(query, cot_x, ffn_part(1 - x, 1))
        second_part = ordered(ffn_part(x, 1), swap(send_second, 1, 0))
        cot_xy = swap(cot_x, 0, 2)
        blocks = jnp.concatenate([block_ids, blocks_x], axis=0)
        block_rows = blocks[:, None, :]
        block_cols = blocks.reshape(2 * length, 1)
        mixed, lse = attend(query, key, value, block_rows, block_cols, length)
        mixed, second_part, cot_xy = after(mixed, second_part, cot_xy)
        cot_x = jnp.stack([cot_x, cot_xy])
        cot_core = swap(cot_x, 0, 1)
        cot_mine = flat(jnp.concatenate([jnp.stack([cot_own[0], cot_own[2]]), cot_x], axis=0))
        cot_theirs = flat(jnp.concatenate([jnp.stack([cot_own[1], cot_own[3]]), cot_core], axis=0))
        ffn_weights.append(gather(second_part))
        mixed_own, mixed_other = mixed[:length], mixed[length:]
        mixed_mine, mixed_theirs = halves(mixed_own, mixed_other)

        def project(values, weight):
            partial = jnp.einsum("atk,dk->atd", values, weight, preferred_element_type=F32)
            return partial.astype(BF)

        tokens_own = cut(tokens, 0)
        mine, theirs, hidden = mid_stage(
            project(mixed_mine, out_weight),
            project(mixed_theirs, out_weight),
            tokens_own,
            gain_two,
        )
        two_mine, two_theirs = flat(mine), flat(theirs)

        shape = (4, quarter, width)
        acts_mine = []
        acts_theirs = []
        part_mine = part_theirs = None
        first_grads = None
        for j in range(CHUNKS):
            last = j == CHUNKS - 1
            weight = ffn_weights[j]
            theirs_in = two_theirs
            if first_grads is not None:
                theirs_in, first_grads = after(two_theirs, first_grads)
            act_theirs, gu_theirs, part_theirs = up_back(
                theirs_in, cot_theirs, weight, part_theirs, last
            )
            mine_in = two_mine
            if last:
                mine_in, part_theirs = after(two_mine, part_theirs)
            act_mine, gu_mine, part_mine = up_back(mine_in, cot_mine, weight, part_mine, last)
            acts_mine.append(act_mine)
            acts_theirs.append(act_theirs)

            if not last:
                first_grads = ffn_grads(
                    (two_mine, two_theirs),
                    (cot_mine, cot_theirs),
                    (gu_mine, gu_theirs),
                    (act_mine, act_theirs),
                )
        mine, theirs, grad_hidden, gain_grad_two, last_grads, out_mine, out_theirs = back_stage(
            part_mine.reshape(shape),
            part_theirs.reshape(shape),
            hidden,
            cut(cotangent, 0),
            gain_two,
            (two_mine, two_theirs, cot_mine, cot_theirs, gu_mine, gu_theirs),
            (acts_mine, acts_theirs),
            ffn_weights,
        )
        gh_mine = mine.reshape(shape)
        gh_theirs = theirs.reshape(shape)
        first_piece = scatter(first_grads)
        last_piece = scatter(last_grads)
        grad_mixed_mine = project(gh_mine, out_weight.T)
        grad_mixed_theirs = project(gh_theirs, out_weight.T)
        grad_mixed = streams(grad_mixed_mine, grad_mixed_theirs)
        grad_q, grad_kv, output = attend_back(
            query,
            key,
            value,
            block_rows,
            block_cols,
            lse,
            jnp.concatenate(grad_mixed, axis=0),
            cosine,
            sine,
            length,
            out_mine.reshape(shape),
            out_theirs.reshape(shape),
            hidden,
        )
        grad_q, first_piece = after(grad_q, first_piece)
        first_theirs = swap(
            lax.dynamic_slice_in_dim(first_piece, (1 - x) * rows, rows, axis=0), 1, 0
        )
        grad_qkv = jnp.concatenate([grad_q, grad_kv], axis=1)
        d_attn = attn_grads(
            normed,
            grad_qkv,
            (flat(gh_mine), flat(gh_theirs)),
            (flat(mixed_mine), flat(mixed_theirs)),
        )
        grad_attn = scatter(d_attn)
        gq_mine, gq_theirs = halves(grad_qkv[:length], grad_qkv[length:])
        gq_mine, gq_theirs, d_attn = after(gq_mine, gq_theirs, d_attn)
        even_in, odd_in, first_theirs = after(
            project(gq_mine, qkv_weight), project(gq_theirs, qkv_weight), first_theirs
        )
        input_grad, gain_grads, last_theirs = end_stage(
            even_in,
            odd_in,
            tokens_own,
            grad_hidden,
            gain_one,
            gain_grad_two,
            last_piece,
            dps,
            shards,
        )
        grad_attn, input_grad, gain_grads = after(grad_attn, input_grad, gain_grads)
        attn_theirs = swap(
            lax.dynamic_slice_in_dim(grad_attn, (1 - x) * rows, rows, axis=0), 1, 0
        )
        input_grad, gain_grads, attn_theirs = after(
            input_grad.astype(F32), gain_grads, attn_theirs
        )

        pairs = [(first_piece, first_theirs), (last_piece, last_theirs)]
        gain_grads = lax.dynamic_slice_in_dim(gain_grads, dp * rows, rows, axis=1)
        first_shard = (me == 0).astype(F32)
        squares = jnp.broadcast_to(first_shard * jnp.sum(gain_grads * gain_grads), (8, 128))
        own_q, own_k, own_v, own_o, own_g, own_u, own_d, norm = finish(
            grad_attn, attn_theirs, squares, pairs, dps, shards, 2
        )
        global_norm = norm[0, 0]
        owned = (gain_grads[0], own_q, own_k, own_v, own_o, gain_grads[1], own_g, own_u, own_d)
        rate_now = rate * jnp.minimum(1.0, (step.astype(F32) + 1.0) / WARMUP)
        masters = (gain_first, w_query, w_key, w_value, w_output, gain_second, w_gate, w_up, w_down)
        moments = (
            moment_first,
            moment_query,
            moment_key,
            moment_value,
            moment_output,
            moment_second,
            moment_gate,
            moment_up,
            moment_down,
        )
        lists = [
            [v.reshape(1, -1) if v.ndim == 1 else v for v in values]
            for values in (masters, moments, owned)
        ]
        momenta, updated = (
            [v.reshape(-1) if v.shape[0] == 1 else v for v in values]
            for values in update(norm, rate_now, *lists)
        )
        return (output, input_grad, global_norm, *momenta, *updated)

    return on_device


def solution(mesh):
    rows, both, back = P("dp"), P("dp", "shard"), P("shard", "dp")
    tokens = P("dp", None)
    params = (rows, both, both, both, back, rows, both, both, back)
    in_specs = (tokens, tokens, tokens, *params, *params, P(), P())
    out_specs = (tokens, tokens, P(), *params, *params)
    return jax.shard_map(
        build(mesh.shape["dp"], mesh.shape["shard"]),
        mesh=mesh,
        in_specs=in_specs,
        out_specs=out_specs,
        check_vma=False,
    )
```

```python
import functools

import jax
import jax.numpy as jnp
import numpy as np
from jax import lax
from jax.experimental import pallas as pl
from jax.experimental.pallas import tpu as pltpu
from jax.sharding import PartitionSpec as P

H = 32
KV = 8
CLIP = 4096
WARMUP = 2000
THETA = 10000000.0
CHUNKS = 2
MESH = pl.DeviceIdType.MESH


BF = jnp.bfloat16
F32 = jnp.float32
HD = 64
EPS = 1e-05
NEGATIVE = -1e30
VMEM = 60 << 20

def dot(a, b, ca, cb):
    return lax.dot_general(a, b, (((ca,), (cb,)), ((), ())), preferred_element_type=F32)

def swap_halves(v):
    n = v.shape[1]
    lane = lax.broadcasted_iota(jnp.int32, v.shape, 1)
    return jnp.where(lane % HD < HD // 2, pltpu.roll(v, n - HD // 2, 1), pltpu.roll(v, HD // 2, 1))

def qkv_body(
    tok_ref, gain_ref, w_ref, cos_ref, sin_ref, cot_ref, normed_ref, q_ref, k_ref, v_ref, near, sems
):
    rows = near.shape[0]
    at = pl.multiple_of(lax.axis_index("shard") * rows, rows)
    target = neighbours()[0]
    moving = remote(cot_ref.at[pl.ds(at, rows)], near, sems, 0, target)

    @pl.when(pl.program_id(0) == 0)
    def _():
        meet((target,))
        moving.start()

    x = tok_ref[...].astype(F32)
    inv = lax.rsqrt(jnp.mean(x * x, axis=1, keepdims=True) + EPS)
    normed = (x * inv * gain_ref[...]).astype(BF)
    normed_ref[...] = normed
    heads = q_ref.shape[0]
    qc = heads * HD
    groups, cols = w_ref.shape[0], qc + 2 * HD
    deep = normed.shape[1] // groups
    lin = sum(
        dot(normed[:, g * deep : (g + 1) * deep], w_ref[g, :deep, :cols], 1, 0)
        for g in range(groups)
    )
    rot = lin * cos_ref[...] + swap_halves(lin) * sin_ref[...]
    for h in range(heads):
        q_ref[h] = (rot[:, h * HD : (h + 1) * HD]).astype(BF)
    k_ref[...] = rot[:, qc : qc + HD].astype(BF)
    v_ref[...] = rot[:, qc + HD :].astype(BF)

    @pl.when(pl.program_id(0) == pl.num_programs(0) - 1)
    def _():
        moving.wait()


def qkv(tokens, gain, weight, cos, sin, cotangent, heads, tile=256):
    count, width = tokens.shape
    length, cols = cos.shape
    per = length // tile
    full = lambda i: (0, 0)
    row = lambda i: (i, 0)
    return pl.pallas_call(
        qkv_body,
        grid=(count // tile,),
        in_specs=[
            pl.BlockSpec((tile, width), row),
            pl.BlockSpec((1, width), full),
            pl.BlockSpec(weight.shape, lambda i: (0, 0, 0)),
            pl.BlockSpec((tile, cols), lambda i: (i % per, 0)),
            pl.BlockSpec((tile, cols), lambda i: (i % per, 0)),
            ANY,
        ],
        out_specs=[
            pl.BlockSpec((tile, width), row),
            pl.BlockSpec((heads, tile, HD), lambda i: (0, i, 0)),
            pl.BlockSpec((tile, HD), row),
            pl.BlockSpec((tile, HD), row),
            ANY,
        ],
        out_shape=[
            jax.ShapeDtypeStruct((count, width), BF),
            jax.ShapeDtypeStruct((heads, count, HD), BF),
            jax.ShapeDtypeStruct((count, HD), BF),
            jax.ShapeDtypeStruct((count, HD), BF),
            jax.ShapeDtypeStruct((cotangent.shape[0] // 4, width), BF),
        ],
        scratch_shapes=[pltpu.SemaphoreType.DMA((2, 1))],
        compiler_params=pltpu.CompilerParams(
            collective_id=10, has_side_effects=True, vmem_limit_bytes=VMEM
        ),
        cost_estimate=pl.CostEstimate(flops=2 * count * width * cols, bytes_accessed=4 * count * width, transcendentals=0),
        name="qkv_rope",
    )(tokens, gain, weight, cos, sin, cotangent)

def fwd_body(
    limits,
    q_ref,
    k_ref,
    v_ref,
    brow_ref,
    bcol_ref,
    near,
    sent,
    o_ref,
    lse_ref,
    far,
    near_core,
    far_core,
    theirs,
    sems
):
    heads, tile, _ = q_ref.shape
    i = pl.program_id(1)
    turn = pl.program_id(0) * pl.num_programs(1) + i
    targets = neighbours()
    over_y = remote(near, far, sems, 0, targets[1])
    over_core = remote(near, near_core, sems, 1, targets[2])
    last = remote(far, far_core, sems, 2, targets[2])
    over_x = remote(sent, theirs, sems, 3, targets[0])

    @pl.when(turn == 0)
    def _():
        meet(targets)
        over_y.start()
        over_x.start()
        over_core.start()

    def run(keys):
        k = k_ref[:keys]
        v = v_ref[:keys]
        allowed = brow_ref[0][:, :keys] <= bcol_ref[...]
        outs = []
        lses = []
        for h in range(heads):
            s = dot(q_ref[h] * BF(0.125), k, 1, 1)
            s = jnp.where(allowed, s, NEGATIVE)
            m = jnp.max(s, axis=1, keepdims=True)
            p = jnp.exp(s - m)
            l = jnp.sum(p, axis=1, keepdims=True)
            o = dot(p.astype(BF), v, 1, 0) / l
            outs.append(o.astype(BF))
            lses.append(m + jnp.log(l))
        o_ref[...] = jnp.concatenate(outs, axis=1)
        lse_ref[...] = jnp.concatenate(lses, axis=1)
    for n, keys in enumerate(limits):
        @pl.when(i == n)
        def _(keys=keys):
            run(keys)

    @pl.when(turn == pl.num_programs(0) * pl.num_programs(1) - 1)
    def _():
        over_y.wait_recv()
        last.start()
        over_x.wait()
        over_core.wait()
        over_y.wait_send()
        last.wait()


def attend(q, k, v, brow, bcol, near, sent, length, tile=256, most=256):
    heads, count, _ = q.shape
    seqs = count // length
    per = length // tile
    limits = tuple(min(length, (n + 1) * tile + most) for n in range(per))
    return pl.pallas_call(
        functools.partial(fwd_body, limits),
        grid=(seqs, per),
        in_specs=[
            pl.BlockSpec((heads, tile, HD), lambda b, i: (0, b * per + i, 0)),
            pl.BlockSpec((length, HD), lambda b, i: (b, 0)),
            pl.BlockSpec((length, HD), lambda b, i: (b, 0)),
            pl.BlockSpec((1, 1, length), lambda b, i: (b, 0, 0)),
            pl.BlockSpec((tile, 1), lambda b, i: (b * per + i, 0)),
            ANY,
            ANY,
        ],
        out_specs=[
            pl.BlockSpec((tile, heads * HD), lambda b, i: (b * per + i, 0)),
            pl.BlockSpec((tile, heads), lambda b, i: (b * per + i, 0)),
            ANY,
            ANY,
            ANY,
            ANY,
        ],
        out_shape=[
            jax.ShapeDtypeStruct((count, heads * HD), BF),
            jax.ShapeDtypeStruct((count, heads), F32),
            *[jax.ShapeDtypeStruct(near.shape, BF)] * 3,
            jax.ShapeDtypeStruct(sent.shape, BF),
        ],
        scratch_shapes=[pltpu.SemaphoreType.DMA((2, 4))],
        compiler_params=pltpu.CompilerParams(
            collective_id=11, has_side_effects=True, vmem_limit_bytes=VMEM
        ),
        cost_estimate=pl.CostEstimate(flops=4 * heads * count * length * HD * 4, bytes_accessed=count * 2048, transcendentals=heads * count * length),
        name="attend",
    )(q, k, v, brow, bcol, near, sent)

def bwd_body(
    limits,
    q_ref,
    k_ref,
    v_ref,
    brow_ref,
    bcol_ref,
    lse_ref,
    do_ref,
    cos_ref,
    sin_ref,
    kcos_ref,
    ksin_ref,
    even,
    odd,
    hidden_ref,
    dq_ref,
    dkv_ref,
    out_ref,
    dk_acc,
    dv_acc,
    *scratch
):
    heads, tile, _ = q_ref.shape
    i = pl.program_id(1)
    turn = pl.program_id(0) * pl.num_programs(1) + i
    targets = neighbours()
    job = Job(even, odd, scratch, targets)

    def produce(s, total):
        return hidden_ref[job.span(s)] + total

    @pl.when(turn == 0)
    def _():
        meet(targets)

    for t in range(8):

        @pl.when(turn == t)
        def _(t=t):
            line_turn(job, t, out_ref, produce)

    @pl.when(i == 0)
    def _():
        dk_acc[...] = jnp.zeros_like(dk_acc)
        dv_acc[...] = jnp.zeros_like(dv_acc)
    def run(keys):
        k = k_ref[:keys]
        v = v_ref[:keys]
        allowed = brow_ref[0][:, :keys] <= bcol_ref[...]
        dqs = []
        dk = jnp.zeros((HD, keys), F32)
        dv = jnp.zeros((HD, keys), F32)
        for h in range(heads):
            q = q_ref[h] * BF(0.125)
            do = do_ref[:, h * HD : (h + 1) * HD]
            s = dot(q, k, 1, 1)
            s = jnp.where(allowed, s, NEGATIVE)
            p = jnp.exp(s - lse_ref[:, h : h + 1])
            dp = dot(do, v, 1, 1)
            pdp = p * dp
            delta = jnp.sum(pdp, axis=1, keepdims=True)
            ds = (pdp - p * delta).astype(BF)
            dqs.append(dot(ds, k, 1, 0) * 0.125)
            dk = dk + dot(q, ds, 0, 0)
            dv = dv + dot(do, p.astype(BF), 0, 0)
        dk_acc[:, :keys] += dk
        dv_acc[:, :keys] += dv
        dq = jnp.concatenate(dqs, axis=1)
        dq_ref[...] = (dq * cos_ref[...] - swap_halves(dq) * sin_ref[...]).astype(BF)
    for n, keys in enumerate(limits):
        @pl.when(i == n)
        def _(keys=keys):
            run(keys)

    @pl.when(turn == 7)
    def _():
        for t in range(8, TURNS):
            line_turn(job, t, out_ref, produce)
        job.line_end(out_ref)

    @pl.when(i == len(limits) - 1)
    def _():
        both = jnp.concatenate([dk_acc[...], dv_acc[...]], axis=0).T
        dkv_ref[...] = (both * kcos_ref[...] - swap_halves(both) * ksin_ref[...]).astype(BF)

def attend_back(
    q, k, v, brow, bcol, lse, do, cos, sin, length, even, odd, hidden, tile=256, most=256
):
    heads, count, _ = q.shape
    seqs = count // length
    per = length // tile
    qc = heads * HD
    limits = tuple(min(length, (n + 1) * tile + most) for n in range(per))
    rowm = lambda b, i: (b * per + i, 0)
    return pl.pallas_call(
        functools.partial(bwd_body, limits),
        grid=(seqs, per),
        in_specs=[
            pl.BlockSpec((heads, tile, HD), lambda b, i: (0, b * per + i, 0)),
            pl.BlockSpec((length, HD), lambda b, i: (b, 0)),
            pl.BlockSpec((length, HD), lambda b, i: (b, 0)),
            pl.BlockSpec((1, 1, length), lambda b, i: (b, 0, 0)),
            pl.BlockSpec((tile, 1), rowm),
            pl.BlockSpec((tile, heads), rowm),
            pl.BlockSpec((tile, qc), rowm),
            pl.BlockSpec((tile, qc), lambda b, i: (i, 0)),
            pl.BlockSpec((tile, qc), lambda b, i: (i, 0)),
            pl.BlockSpec((length, 2 * HD), lambda b, i: (0, qc // (2 * HD))),
            pl.BlockSpec((length, 2 * HD), lambda b, i: (0, qc // (2 * HD))),
            IN_VMEM,
            ANY,
            IN_VMEM,
        ],
        out_specs=[
            pl.BlockSpec((tile, qc), rowm),
            pl.BlockSpec((length, 2 * HD), lambda b, i: (b, 0)),
            ANY,
        ],
        out_shape=[
            jax.ShapeDtypeStruct((count, qc), BF),
            jax.ShapeDtypeStruct((count, 2 * HD), BF),
            jax.ShapeDtypeStruct((length, even.shape[2]), BF),
        ],
        scratch_shapes=[pltpu.VMEM((HD, length), F32), pltpu.VMEM((HD, length), F32)]
        + Job.scratch(even.shape[1], even.shape[2]),
        compiler_params=pltpu.CompilerParams(
            collective_id=7, has_side_effects=True, vmem_limit_bytes=VMEM
        ),
        cost_estimate=pl.CostEstimate(flops=10 * heads * count * length * HD * 4, bytes_accessed=count * 4096, transcendentals=heads * count * length),
        name="attend_back",
    )(q, k, v, brow, bcol, lse, do, cos, sin, cos, sin, even, odd, hidden)

def rope_tables(length, heads):
    positions = np.arange(length, dtype=np.float32)
    powers = np.float32(-2.0) * np.arange(HD // 2, dtype=np.float32) / np.float32(HD)
    angles = positions[:, None] * np.power(np.float32(THETA), powers)[None, :]
    c, s = np.cos(angles), np.sin(angles)
    zeros = np.zeros((length, HD), np.float32)
    cos = [c, c] * (heads + 1) + [zeros + 1]
    sin = [-s, s] * (heads + 1) + [zeros]
    return (jnp.asarray(np.concatenate(v, axis=1).astype(np.float32)) for v in (cos, sin))


def up_body(first, last, n2_ref, cot_ref, w_ref, *rest):
    if first:
        act_ref, dgu_ref, part_ref = rest
    else:
        prev_ref, act_ref, dgu_ref, part_ref = rest
    size = act_ref.shape[1]
    gu = dot(n2_ref[...], w_ref[:, : 2 * size], 1, 0)
    da = dot(cot_ref[...], w_ref[:, 2 * size :], 1, 0)
    gate, up = gu[:, :size], gu[:, size:]
    sig = 1.0 / (1.0 + jnp.exp(-gate))
    gs = gate * sig
    act_ref[...] = (gs * up).astype(BF)
    dg = (da * up * sig * (1.0 + gate * (1.0 - sig))).astype(BF)
    du = (da * gs).astype(BF)
    dgu = jnp.concatenate([dg, du], axis=1)
    dgu_ref[...] = dgu
    part = dot(dgu, w_ref[:, : 2 * size], 1, 1)
    if not first:
        part = part + prev_ref[...]
    part_ref[...] = part.astype(part_ref.dtype)

def up_back(n2, cot, weight, prev, last, tile=256):
    count, width = n2.shape
    size = weight.shape[1] // 3
    row = lambda i: (i, 0)
    full = lambda i: (0, 0)
    ins = [n2, cot, weight] + ([] if prev is None else [prev])
    specs = [pl.BlockSpec((tile, width), row), pl.BlockSpec((tile, width), row), pl.BlockSpec((width, 3 * size), full, pipeline_mode=pl.Buffered(1))]
    if prev is not None:
        specs.append(pl.BlockSpec((tile, width), row))
    return pl.pallas_call(
        functools.partial(up_body, prev is None, last),
        grid=(count // tile,),
        in_specs=specs,
        out_specs=[pl.BlockSpec((tile, size), row), pl.BlockSpec((tile, 2 * size), row), pl.BlockSpec((tile, width), row)],
        out_shape=[jax.ShapeDtypeStruct((count, size), BF), jax.ShapeDtypeStruct((count, 2 * size), BF), jax.ShapeDtypeStruct((count, width), BF if last else F32)],
        compiler_params=pltpu.CompilerParams(vmem_limit_bytes=VMEM),
        cost_estimate=pl.CostEstimate(flops=2 * count * width * size * 5, bytes_accessed=12 * count * width, transcendentals=count * size),
        name="swiglu_part",
    )(*ins)

def grad_body(n2a, n2b, cota, cotb, dgua, dgub, acta, actb, o_ref):
    size = acta.shape[1]
    gu = dot(n2a[...], dgua[...], 0, 0) + dot(n2b[...], dgub[...], 0, 0)
    o_ref[:, : 2 * size] = gu.astype(BF)
    dt = dot(cota[...], acta[...], 0, 0) + dot(cotb[...], actb[...], 0, 0)
    o_ref[:, 2 * size :] = dt.astype(BF)


def ffn_grads(n2, cot, dgu, act, tile=256):
    count, width = n2[0].shape
    size = act[0].shape[1]
    col = lambda i: (0, i)
    full = lambda i: (0, 0)
    return pl.pallas_call(
        grad_body,
        grid=(width // tile,),
        in_specs=[pl.BlockSpec((count, tile), col)] * 4
        + [pl.BlockSpec((count, 2 * size), full, pipeline_mode=pl.Buffered(1))] * 2
        + [pl.BlockSpec((count, size), full, pipeline_mode=pl.Buffered(1))] * 2,
        out_specs=pl.BlockSpec((tile, 3 * size), lambda i: (i, 0)),
        out_shape=jax.ShapeDtypeStruct((width, 3 * size), BF),
        compiler_params=pltpu.CompilerParams(vmem_limit_bytes=VMEM),
        cost_estimate=pl.CostEstimate(
            flops=4 * count * width * size * 3,
            bytes_accessed=16 * count * width,
            transcendentals=0,
        ),
        name="swiglu_grads",
    )(*n2, *cot, *dgu, *act)


def attn_grad_body(
    na, ga, ha, hb, ma, mb, qa, qb, w_ref, piece, o_ref, even, odd, theirs, sems
):
    cols = ga.shape[1]
    step = pl.program_id(0)
    swapped = trade(piece, theirs, sems)

    @pl.when(step == 0)
    def _():
        meet(neighbours()[:1])
        swapped.start()

    o_ref[:, :cols] = dot(na[...], ga[...], 0, 0).astype(BF)
    o_ref[:, cols:] = (dot(ha[...], ma[...], 0, 0) + dot(hb[...], mb[...], 0, 0)).astype(BF)
    even[...] = dot(qa[...], w_ref[0], 1, 1).astype(BF)
    odd[...] = dot(qb[...], w_ref[0], 1, 1).astype(BF)

    @pl.when(step == pl.num_programs(0) - 1)
    def _():
        swapped.wait()


def attn_grads(normed, grads, hidden, mixed, halves, packed, piece, tile=256):
    width = normed.shape[1]
    count, cols = halves[0].shape
    col = lambda i: (0, i)
    tile = min(tile, width // packed.shape[0])
    per = width // packed.shape[0] // tile
    ins = [normed, grads, *hidden, *mixed, *halves, packed, piece]
    wide = cols + mixed[0].shape[1]

    def tiled(value):
        return pl.BlockSpec((value.shape[0], tile), col)

    def whole(value):
        return pl.BlockSpec(value.shape, lambda i: (0, 0), pipeline_mode=pl.Buffered(1))

    return pl.pallas_call(
        attn_grad_body,
        grid=(width // tile,),
        in_specs=[tiled(normed), whole(grads)]
        + [tiled(v) for v in hidden]
        + [whole(v) for v in (*mixed, *halves)]
        + [pl.BlockSpec((1, tile, cols), lambda i: (i // per, i % per, 0)), ANY],
        out_specs=[
            pl.BlockSpec((tile, wide), lambda i: (i, 0)),
            pl.BlockSpec((count, tile), col),
            pl.BlockSpec((count, tile), col),
            ANY,
        ],
        out_shape=[
            jax.ShapeDtypeStruct((width, wide), BF),
            jax.ShapeDtypeStruct((count, width), BF),
            jax.ShapeDtypeStruct((count, width), BF),
            jax.ShapeDtypeStruct((piece.shape[0] // 2, piece.shape[1]), BF),
        ],
        scratch_shapes=[pltpu.SemaphoreType.DMA((2, 1))],
        compiler_params=pltpu.CompilerParams(
            collective_id=9, has_side_effects=True, vmem_limit_bytes=VMEM
        ),
        name="attn_grads",
    )(*ins)


def peers(dps, shards):
    dp, sh = lax.axis_index("dp"), lax.axis_index("shard")
    groups = dps // 2
    near = []
    for r in range(1, 2 * shards):
        there = sh
        for bit in (1, 2):
            there = flip(there, bit) if r % shards & bit else there
        near.append((flip(dp, 1) if r >= shards else dp, there))
    far = [
        (lax.rem(dp // 2 + p, groups) * 2 + lax.rem(dp, 2), sh) for p in range(1, groups)
    ]
    return near, far, lax.rem(dp, 2) * shards + sh, dp // 2


def greet(targets):
    barrier = pltpu.get_barrier_semaphore()
    for target in targets:
        pl.semaphore_signal(barrier, inc=1, device_id=target, device_id_type=MESH)


def meet(targets):
    greet(targets)
    pl.semaphore_wait(pltpu.get_barrier_semaphore(), len(targets))


def exchange(values, slots, mine, targets, source, send, recv, base):
    source[...] = values
    slots[mine] = values
    copies = [
        pltpu.make_async_remote_copy(
            src_ref=source,
            dst_ref=slots.at[mine],
            send_sem=send.at[base + n],
            recv_sem=recv.at[base + n],
            device_id=target,
            device_id_type=MESH,
        )
        for n, target in enumerate(targets)
    ]
    for copy in copies:
        copy.start()
    for copy in copies:
        copy.wait()
    total = slots[0]
    for n in range(1, slots.shape[0]):
        total = total + slots[n]
    return total


def two_stages(values, near, far, me, outer, bufs):
    slots_near, slots_far, from_near, from_far, send, recv = bufs
    total = exchange(values, slots_near, me, near, from_near, send, recv, 0)
    return exchange(total, slots_far, outer, far, from_far, send, recv, len(near))


def sum_scratch(shape, dps, shards):
    count = 2 * shards - 1 + dps // 2 - 1
    return [
        pltpu.VMEM((2 * shards,) + shape, F32),
        pltpu.VMEM((dps // 2,) + shape, F32),
        pltpu.VMEM(shape, F32),
        pltpu.VMEM(shape, F32),
        pltpu.SemaphoreType.DMA((count,)),
        pltpu.SemaphoreType.DMA((count,)),
    ]


def pick(x, first, second):
    low = jnp.where(x == 0, first.astype(F32), second.astype(F32)).astype(BF)
    high = jnp.where(x == 0, second.astype(F32), first.astype(F32)).astype(BF)
    return low, high


def finish_body(dps, shards, count, piece_ref, gain_ref, *refs):
    ins, outs, scratch = refs[: 2 * count], refs[2 * count : 2 * count + 10], refs[2 * count + 10 :]
    q_ref, k_ref, v_ref, o_ref, g_ref, u_ref, d_ref, norm_ref, first_ref, second_ref = outs
    theirs, pair, *bufs = scratch
    near, far, me, outer = peers(dps, shards)
    rows = piece_ref.shape[0] // 2
    qc = q_ref.shape[1] // 2
    x = lax.rem(lax.axis_index("dp"), 2)
    here = pl.ds(pl.multiple_of(x * rows, rows), rows)
    meet(near + far)
    swapped = trade(piece_ref, theirs, pair)
    swapped.start()
    gains = gain_ref[lax.axis_index("dp")]
    first_ref[...] = gains[0:1]
    second_ref[...] = gains[1:2]
    once = jnp.where(lax.axis_index("shard") == 0, 1.0, 0.0)
    squares = once * jnp.sum(gains * gains, keepdims=True)
    half = g_ref.shape[1] // 2
    at = 0
    for j in range(count):
        size = ins[2 * j].shape[1] // 3
        for h, piece in enumerate(pick(x, ins[2 * j][here, :], ins[2 * j + 1][...])):
            wide = piece.astype(F32)
            squares = squares + jnp.sum(wide * wide, keepdims=True)
            span = pl.ds(h * half + at, size)
            g_ref[:, span] = piece[:, :size]
            u_ref[:, span] = piece[:, size : 2 * size]
            d_ref[span, :] = wide[:, 2 * size :].T.astype(BF)
        at = at + size
    mine = piece_ref[here, :]
    wide = mine.astype(F32)
    squares = squares + jnp.sum(wide * wide, keepdims=True)
    swapped.wait()
    got = theirs[...]
    wide = got.astype(F32)
    squares = squares + jnp.sum(wide * wide, keepdims=True)
    values = jnp.broadcast_to(squares, norm_ref.shape)
    norm_ref[...] = jnp.sqrt(two_stages(values, near, far, me, outer, bufs))
    low, high = pick(x, mine, got)
    q_ref[:, :qc] = low[:, :qc]
    q_ref[:, qc:] = high[:, :qc]
    k_ref[...] = jnp.concatenate([low[:, qc : qc + HD], high[:, qc : qc + HD]], axis=1)
    vc, oc = qc + HD, qc + 2 * HD
    v_ref[...] = jnp.concatenate([low[:, vc:oc], high[:, vc:oc]], axis=1)
    o_ref[:qc] = low[:, oc:].astype(F32).T.astype(BF)
    o_ref[qc:] = high[:, oc:].astype(F32).T.astype(BF)


def finish(piece, gains, pairs, dps, shards, number):
    rows, cols = piece.shape[0] // 2, piece.shape[1]
    qc = (cols - 2 * HD) // 2
    wide = 2 * sum(other.shape[1] // 3 for _, other in pairs)
    vmem = pl.BlockSpec(memory_space=pltpu.VMEM)
    ins = [v for pair in pairs for v in pair]
    shapes = ((rows, 2 * qc), (rows, 2 * HD), (rows, 2 * HD), (2 * qc, rows))
    shapes = shapes + ((rows, wide), (rows, wide), (wide, rows))
    return pl.pallas_call(
        functools.partial(finish_body, dps, shards, len(pairs)),
        in_specs=[vmem] * (2 + len(ins)),
        out_specs=[vmem] * 10,
        out_shape=[jax.ShapeDtypeStruct(shape, BF) for shape in shapes]
        + [jax.ShapeDtypeStruct(v, F32) for v in ((8, 128), (1, rows), (1, rows))],
        scratch_shapes=[pltpu.VMEM((rows, cols), BF), pltpu.SemaphoreType.DMA((2, 1))]
        + sum_scratch((8, 128), dps, shards),
        compiler_params=pltpu.CompilerParams(
            collective_id=number, has_side_effects=True, vmem_limit_bytes=VMEM
        ),
        name="finish",
    )(piece, gains, *ins)


PARTS = 8


def flip(value, bit):
    return value + bit * (1 - 2 * lax.rem(value // bit, 2))


def neighbours():
    dp, sh = lax.axis_index("dp"), lax.axis_index("shard")
    return (flip(dp, 1), sh), (dp, flip(sh, 2)), (dp, flip(sh, 1))


def remote(src, dst, sems, n, target):
    return pltpu.make_async_remote_copy(
        src_ref=src,
        dst_ref=dst,
        send_sem=sems.at[0, n],
        recv_sem=sems.at[1, n],
        device_id=target,
        device_id_type=MESH,
    )


class Job:

    def __init__(self, even, odd, scratch, targets, y_first=()):
        self.y_first = y_first
        self.even, self.odd = even, odd
        self.got, self.out1, self.in1, self.out2, self.in2, self.own, self.sems, self.local = scratch
        self.x, self.y, self.core = targets
        self.rows = even.shape[1] // PARTS

    @staticmethod
    def scratch(rows, width):
        part = rows // PARTS
        return [
            pltpu.VMEM((4, rows, width), BF),
            pltpu.VMEM((PARTS, 2, part, width), BF),
            pltpu.VMEM((PARTS, 2, part, width), BF),
            pltpu.VMEM((PARTS, part, width), BF),
            pltpu.VMEM((PARTS, part, width), BF),
            pltpu.VMEM((rows, width), BF),
            pltpu.SemaphoreType.DMA((2, 6 * PARTS)),
            pltpu.SemaphoreType.DMA((PARTS,)),
        ]

    def span(self, s):
        return pl.ds(s * self.rows, self.rows)

    def over_x(self, s):
        return s not in self.y_first

    def copy(self, stage, s, src, dst, target):
        return remote(src, dst, self.sems, stage * PARTS + s, target)

    def to_core(self, s):
        span = self.span(s)
        return self.copy(0, s, self.odd.at[:, span], self.got.at[:, span], self.core)

    def to_first(self, s):
        target = self.x if self.over_x(s) else self.y
        return self.copy(1, s, self.out1.at[s], self.in1.at[s], target)

    def to_second(self, s):
        target = self.y if self.over_x(s) else self.x
        return self.copy(2, s, self.out2.at[s], self.in2.at[s], target)

    def start(self):
        for s in range(4):
            self.to_core(s).start()

    def pair(self, k, s):
        return self.even[k, self.span(s)].astype(F32) + self.got[k, self.span(s)].astype(F32)

    def first(self, s):
        self.to_core(s).wait_recv()
        if s + 4 < PARTS:
            self.to_core(s + 4).start()
        self.out1[s, 0] = self.pair(2 if self.over_x(s) else 1, s).astype(BF)
        self.out1[s, 1] = self.pair(3, s).astype(BF)
        self.to_first(s).start()

    def second(self, s):
        self.to_first(s).wait_recv()
        near = self.pair(1 if self.over_x(s) else 2, s)
        self.out2[s] = (near + self.in1[s, 1].astype(F32)).astype(BF)
        self.to_second(s).start()

    def total(self, s):
        self.to_second(s).wait_recv()
        return self.pair(0, s) + self.in1[s, 0].astype(F32) + self.in2[s].astype(F32)

    def sent(self):
        for s in range(PARTS):
            self.to_core(s).wait_send()
            self.to_first(s).wait_send()
            self.to_second(s).wait_send()


    def keep(self, s, place):
        return pltpu.make_async_copy(self.own.at[self.span(s)], place, self.local.at[s])

    def spread_copies(self, s, mine, theirs):
        span = self.span(s)
        own = self.own.at[span]
        if self.over_x(s):
            near = self.copy(3, s, own, mine.at[1, 0, span], self.x)
            far = self.copy(4, s, mine.at[:, 0, span], mine.at[:, 1, span], self.y)
        else:
            near = self.copy(3, s, own, mine.at[0, 1, span], self.y)
            far = self.copy(4, s, mine.at[0, :, span], mine.at[1, :, span], self.x)
        core = self.copy(5, s, mine.at[:, :, span], theirs.at[:, :, span], self.core)
        return self.keep(s, mine.at[0, 0, span]), near, far, core


    def line_copies(self, s, whole):
        me = lax.axis_index("shard")
        size = self.rows * PARTS

        def place(owner):
            at = pl.multiple_of(owner * size + s * self.rows, self.rows)
            return whole.at[pl.ds(at, self.rows)]

        own = self.own.at[self.span(s)]
        near = self.copy(3, s, own, place(me), self.y)
        core = self.copy(4, s, own, place(me), self.core)
        other = place(flip(me, 2))
        return self.keep(s, place(me)), near, core, self.copy(5, s, other, other, self.core)

    def line_start(self, s, whole):
        for copy in self.line_copies(s, whole)[:3]:
            copy.start()

    def line_core(self, s, whole):
        keep, near, core, far = self.line_copies(s, whole)
        keep.wait()
        near.wait_recv()
        far.start()

    def line_end(self, whole):
        for s in range(PARTS):
            _, near, core, far = self.line_copies(s, whole)
            core.wait_recv()
            far.wait_recv()
            for copy in (near, core, far):
                copy.wait_send()
        self.sent()


def run_job(job, mine, theirs, produce, hook, window=4, lag=2):
    copies = [job.spread_copies(s, mine, theirs) for s in range(PARTS)]
    job.start()
    for s in range(window):
        job.first(s)
    for t in range(PARTS + 3 * lag):
        hook(t)
        if t < PARTS:
            job.second(t)
            if t + window < PARTS:
                job.first(t + window)
        if 0 <= t - lag < PARTS:
            s = t - lag
            job.own[job.span(s)] = produce(s, job.total(s)).astype(BF)
            copies[s][0].start()
            copies[s][1].start()
        if 0 <= t - 2 * lag < PARTS:
            keep, near, far, _ = copies[t - 2 * lag]
            keep.wait()
            near.wait_recv()
            far.start()
        if 0 <= t - 3 * lag < PARTS:
            _, _, far, core = copies[t - 3 * lag]
            far.wait_recv()
            core.start()
    for _, near, far, core in copies:
        core.wait_recv()
        for copy in (near, far, core):
            copy.wait_send()
    job.sent()


def line_turn(job, t, whole, produce, window=4, lag=2):
    if t == 0:
        job.start()
        for s in range(window):
            job.first(s)
    if 0 <= t - 1 < PARTS:
        job.second(t - 1)
        if t - 1 + window < PARTS:
            job.first(t - 1 + window)
    if 0 <= t - 1 - lag < PARTS:
        s = t - 1 - lag
        job.own[job.span(s)] = produce(s, job.total(s)).astype(BF)
        job.line_start(s, whole)
    if 0 <= t - 1 - 2 * lag < PARTS:
        job.line_core(t - 1 - 2 * lag, whole)


TURNS = PARTS + 5


def rms_of(values):
    return lax.rsqrt(jnp.mean(values * values, axis=1, keepdims=True) + EPS)


def norm_back_of(values, gain, grad):
    inverse = rms_of(values)
    scaled = grad * gain
    total = jnp.sum(grad * values * inverse, axis=0, keepdims=True)
    mean = jnp.mean(scaled * values, axis=1, keepdims=True)
    return total, inverse * scaled - values * (inverse * inverse * inverse * mean)


def mid_body(even, odd, tok_ref, gain_ref, mine, theirs, hidden_ref, *scratch):
    targets = neighbours()
    meet(targets)
    job = Job(even, odd, scratch, targets, range(1, PARTS, 2))

    def produce(s, total):
        hidden = tok_ref[job.span(s)].astype(F32) + total
        hidden_ref[job.span(s)] = hidden
        return hidden * rms_of(hidden) * gain_ref[...]

    run_job(job, mine, theirs, produce, lambda t: None)


def back_body(even, odd, hidden_ref, cot_ref, gain_ref, *rest):
    chunks = CHUNKS
    count = 6 + 3 * chunks
    ins, outs, scratch = rest[:count], rest[count : count + 7], rest[count + 7 :]
    mine, theirs, gh_ref, gg_ref, dw_ref, down_a, down_b = outs
    held = scratch[8 : 8 + count]
    tiles, store, load, down_tiles, down_store = scratch[8 + count :]
    targets = neighbours()
    loads = []
    for n, (src, dst) in enumerate(zip(ins, held)):
        wide = src.shape[1] - dst.shape[1]
        src = src.at[:, pl.ds(wide, dst.shape[1])] if wide else src
        loads.append(pltpu.make_async_copy(src, dst, load.at[n]))
    for copy in loads:
        copy.start()
    meet(targets)
    job = Job(even, odd, scratch[:8], targets, range(1, PARTS, 2))
    na, nb, ca, cb, ga, gb = held[:6]
    acts_a, acts_b, downs = held[6 : 6 + chunks], held[6 + chunks : 6 + 2 * chunks], held[6 + 2 * chunks :]
    aa, ab = acts_a[-1], acts_b[-1]
    size = aa.shape[1]
    step = tiles.shape[1]
    sites = 4
    half = dw_ref.shape[0] // step // sites
    rows = down_tiles.shape[1]

    def filler(part):
        if part == 0:
            for copy in loads:
                copy.wait()

        def tile(n, carry):
            cols = pl.ds(pl.multiple_of((part * half + n) * step, step), step)
            gu = dot(na[:, cols], ga[...], 0, 0) + dot(nb[:, cols], gb[...], 0, 0)
            tiles[n, :, : 2 * size] = gu.astype(BF)
            dt = dot(ca[:, cols], aa[...], 0, 0) + dot(cb[:, cols], ab[...], 0, 0)
            tiles[n, :, 2 * size :] = dt.astype(BF)
            pltpu.make_async_copy(tiles.at[n], dw_ref.at[cols], store.at[n]).start()
            return carry

        lax.fori_loop(0, half, tile, 0)
        span = pl.ds(part * rows, rows)
        for n, (acts, out) in enumerate(((acts_a, down_a), (acts_b, down_b))):
            total = dot(acts[0][span], downs[0][...], 1, 1)
            for j in range(1, chunks):
                total = total + dot(acts[j][span], downs[j][...], 1, 1)
            down_tiles[n] = total.astype(BF)
            pltpu.make_async_copy(down_tiles.at[n], out.at[span], down_store.at[n]).start()

    def settle(part):
        span = pl.ds(part * rows, rows)
        for n in range(half):
            cols = pl.ds((part * half + n) * step, step)
            pltpu.make_async_copy(tiles.at[n], dw_ref.at[cols], store.at[n]).wait()
        for n, out in enumerate((down_a, down_b)):
            pltpu.make_async_copy(down_tiles.at[n], out.at[span], down_store.at[n]).wait()

    def hook(t):
        if t % 2 == 0 and t // 2 < sites:
            if t > 0:
                settle(t // 2 - 1)
            filler(t // 2)

    totals = []

    def produce(s, total):
        gain_total, through = norm_back_of(hidden_ref[job.span(s)], gain_ref[...], total)
        totals.append(gain_total)
        grad_hidden = cot_ref[job.span(s)].astype(F32) + through
        gh_ref[job.span(s)] = grad_hidden
        return grad_hidden

    run_job(job, mine, theirs, produce, hook)
    settle(sites - 1)
    gg_ref[...] = sum(totals[1:], totals[0])


def trade(piece, theirs, sems):
    size = theirs.shape[0]
    x = lax.rem(lax.axis_index("dp"), 2)
    src = piece.at[pl.ds(pl.multiple_of((1 - x) * size, size), size)]
    return remote(src, theirs, sems, 0, neighbours()[0])


def end_body(
    dps, shards, even, odd, tok_ref, gh_ref, gain_ref, gg_ref, piece, in_ref, sum_ref, theirs, *scratch
):
    near, far, me, outer = peers(dps, shards)
    meet(near + far)
    job = Job(even, odd, scratch[:8], neighbours(), (1, 4, 7))
    swapped = trade(piece, theirs, scratch[8])
    totals = []

    def produce(s, total):
        span = job.span(s)
        gain_total, through = norm_back_of(tok_ref[span].astype(F32), gain_ref[...], total)
        totals.append(gain_total)
        return gh_ref[span] + through

    for t in range(TURNS):
        line_turn(job, t, in_ref, produce)
        if t == 4:
            swapped.start()
    gains = jnp.concatenate([sum(totals[1:], totals[0]), gg_ref[...]], axis=0)
    sum_ref[...] = two_stages(gains, near, far, me, outer, scratch[9:])
    job.line_end(in_ref)
    swapped.wait()


def open_body(q_ref, k_ref, v_ref, o_ref, gain_ref, piece, sent, sems):
    rows = q_ref.shape[0]
    qc = q_ref.shape[1] // 2
    x = lax.rem(lax.axis_index("dp"), 2)
    target = neighbours()[0]
    barrier = pltpu.get_barrier_semaphore()
    pl.semaphore_signal(barrier, inc=1, device_id=target, device_id_type=MESH)

    def fill(ref, base, which):
        at = pl.ds(pl.multiple_of(base, 16), rows)

        def narrow(value):
            return jnp.where(which == 0, value[:, :HD], value[:, HD:]).astype(BF)

        ref[at, :qc] = q_ref[:, pl.ds(pl.multiple_of(which * qc, qc), qc)].astype(BF)
        ref[at, qc : qc + HD] = narrow(k_ref[...])
        ref[at, qc + HD : qc + 2 * HD] = narrow(v_ref[...])
        out = o_ref[pl.ds(pl.multiple_of(which * qc, qc), qc), :]
        ref[at, qc + 2 * HD :] = out.T.astype(BF)

    fill(sent, 0, 1 - x)
    sent[rows:] = gain_ref[...]
    pl.semaphore_wait(barrier, 1)
    spots = (
        piece.at[pl.ds(pl.multiple_of(x * rows, 16), rows)],
        piece.at[pl.ds(pl.multiple_of(2 * rows + x * 16, 16), 16)],
    )
    copies = [
        remote(sent.at[pl.ds(0, rows)], spots[0], sems, 0, target),
        remote(sent.at[pl.ds(rows, 16)], spots[1], sems, 1, target),
    ]
    for copy in copies:
        copy.start()
    fill(piece, x * rows, x)
    piece[pl.ds(pl.multiple_of(2 * rows + x * 16, 16), 16)] = gain_ref[...]
    for copy in copies:
        copy.wait()


def opening(w_query, w_key, w_value, w_output, gains):
    rows, cols = w_query.shape[0], gains.shape[1]
    return pl.pallas_call(
        open_body,
        in_specs=[IN_VMEM] * 5,
        out_specs=IN_VMEM,
        out_shape=jax.ShapeDtypeStruct((2 * rows + 32, cols), BF),
        scratch_shapes=[
            pltpu.VMEM((rows + 16, cols), BF),
            pltpu.SemaphoreType.DMA((2, 2)),
        ],
        compiler_params=pltpu.CompilerParams(
            collective_id=8, has_side_effects=True, vmem_limit_bytes=16 << 20
        ),
        name="opening",
    )(w_query, w_key, w_value, w_output, gains)


def entry_body(tok_ref, keep_ref, send_ref, both, piece, hop_x, hop_y, hop_core, weight_sem, keeps):
    xs, ys, core = neighbours()
    sh = lax.axis_index("shard")
    x = lax.rem(lax.axis_index("dp"), 2)
    length = tok_ref.shape[0]
    quarter = length // 4
    rows = quarter // PARTS
    size = keep_ref.shape[0]
    mine = piece.at[pl.ds(pl.multiple_of(x * size, size), size)]
    local = [
        pltpu.make_async_copy(keep_ref, mine, keeps.at[0]),
        pltpu.make_async_copy(tok_ref, both.at[pl.ds(0, length)], keeps.at[1]),
    ]
    for copy in local:
        copy.start()
    meet((xs, ys, core))

    def rows_of(ref, base, owner, s):
        return ref.at[pl.ds(pl.multiple_of(base + owner * quarter + s * rows, rows), rows)]

    over_x, over_y, over_core, over_far = [], [], [], []
    for s in range(PARTS):
        near, far = rows_of(both, length, sh, s), rows_of(both, length, flip(sh, 2), s)
        over_x.append(remote(rows_of(tok_ref, 0, sh, s), near, hop_x, s, xs))
        over_y.append(remote(near, near, hop_y, s, ys))
        over_core.append(remote(near, near, hop_core, s, core))
        over_far.append(remote(far, far, hop_core, PARTS + s, core))
    moving = remote(send_ref, mine, weight_sem, 0, xs)
    for copy in over_x:
        copy.start()
    moving.start()
    for s in range(PARTS):
        over_x[s].wait_recv()
        over_y[s].start()
        over_core[s].start()
    for s in range(PARTS):
        over_y[s].wait_recv()
        over_far[s].start()
    moving.wait()
    for copy in over_core + over_far:
        copy.wait()
    for copy in over_x + over_y:
        copy.wait_send()
    for copy in local:
        copy.wait()


def entry(tokens, keep, sent):
    length, width = tokens.shape
    dma = pltpu.SemaphoreType.DMA
    return pl.pallas_call(
        entry_body,
        in_specs=[ANY] * 3,
        out_specs=[ANY] * 2,
        out_shape=[
            jax.ShapeDtypeStruct((2 * length, width), BF),
            jax.ShapeDtypeStruct((2 * keep.shape[0], keep.shape[1]), BF),
        ],
        scratch_shapes=[
            dma((2, PARTS)),
            dma((2, PARTS)),
            dma((2, 2 * PARTS)),
            dma((2, 1)),
            dma((2,)),
        ],
        compiler_params=pltpu.CompilerParams(
            collective_id=6, has_side_effects=True, vmem_limit_bytes=8 << 20
        ),
        name="entry",
    )(tokens, keep, sent)


ANY = pl.BlockSpec(memory_space=pl.ANY)
IN_VMEM = pl.BlockSpec(memory_space=pltpu.VMEM)
BIG = 60 << 20


def mid_stage(even, odd, tokens_own, gain):
    _, rows, width = even.shape
    half = jax.ShapeDtypeStruct((2, 2, rows, width), BF)
    return pl.pallas_call(
        mid_body,
        in_specs=[IN_VMEM, ANY, IN_VMEM, IN_VMEM],
        out_specs=[ANY, ANY, IN_VMEM],
        out_shape=[half, half, jax.ShapeDtypeStruct((rows, width), F32)],
        scratch_shapes=Job.scratch(rows, width),
        compiler_params=pltpu.CompilerParams(
            collective_id=3, has_side_effects=True, vmem_limit_bytes=VMEM
        ),
        name="mid_stage",
    )(even, odd, tokens_own, gain)


def back_stage(even, odd, hidden, cot_own, gain, halves, acts, weights, tile=256):
    _, rows, width = even.shape
    count = halves[0].shape[0]
    sizes = [act.shape[1] for act in acts[0]]
    filling = list(halves) + list(acts[0]) + list(acts[1]) + list(weights)
    held = [pltpu.VMEM(v.shape, BF) for v in filling[: 6 + 2 * len(sizes)]]
    held += [pltpu.VMEM((width, size), BF) for size in sizes]
    spread_shape = jax.ShapeDtypeStruct((2, 2, rows, width), BF)
    down_shape = jax.ShapeDtypeStruct((count, width), BF)
    dma = pltpu.SemaphoreType.DMA
    return pl.pallas_call(
        back_body,
        in_specs=[IN_VMEM, ANY, IN_VMEM, IN_VMEM, IN_VMEM] + [ANY] * len(filling),
        out_specs=[ANY, ANY, IN_VMEM, IN_VMEM, ANY, ANY, ANY],
        out_shape=[
            spread_shape,
            spread_shape,
            jax.ShapeDtypeStruct((rows, width), F32),
            jax.ShapeDtypeStruct((1, width), F32),
            jax.ShapeDtypeStruct((width, 3 * sizes[-1]), BF),
            down_shape,
            down_shape,
        ],
        scratch_shapes=Job.scratch(rows, width)
        + held
        + [
            pltpu.VMEM((width // tile // 4, tile, 3 * sizes[-1]), BF),
            dma((width // tile // 4,)),
            dma((len(filling),)),
            pltpu.VMEM((2, count // 4, width), BF),
            dma((2,)),
        ],
        compiler_params=pltpu.CompilerParams(
            collective_id=4, has_side_effects=True, vmem_limit_bytes=BIG
        ),
        name="back_stage",
    )(even, odd, hidden, cot_own, gain, *filling)


def end_stage(even, odd, tokens_own, grad_hidden, gain, gain_grad, piece, dps, shards):
    _, rows, width = even.shape
    theirs = jax.ShapeDtypeStruct((piece.shape[0] // 2, piece.shape[1]), BF)
    return pl.pallas_call(
        functools.partial(end_body, dps, shards),
        in_specs=[IN_VMEM, ANY] + [IN_VMEM] * 4 + [ANY],
        out_specs=[ANY, IN_VMEM, ANY],
        out_shape=[
            jax.ShapeDtypeStruct((shards * rows, width), BF),
            jax.ShapeDtypeStruct((2, width), F32),
            theirs,
        ],
        scratch_shapes=Job.scratch(rows, width)
        + [pltpu.SemaphoreType.DMA((2, 1))]
        + sum_scratch((2, width), dps, shards),
        compiler_params=pltpu.CompilerParams(
            collective_id=5, has_side_effects=True, vmem_limit_bytes=VMEM
        ),
        name="end_stage",
    )(even, odd, tokens_own, grad_hidden, gain, gain_grad, piece)


def update_body(count, norm_ref, rate_ref, out_ref, in_ref, *refs):
    refs, (new_out, new_in) = refs[:-2], refs[-2:]
    new_out[...] = out_ref[...]
    new_in[...] = in_ref[...].astype(F32)
    factor = jnp.minimum(1.0, CLIP / norm_ref[0:1, 0:1])
    rate = rate_ref[0]
    for n in range(count):
        master, moment, grad = (refs[3 * n + k] for k in range(3))
        new_moment, new_master = refs[3 * count + 2 * n], refs[3 * count + 2 * n + 1]
        momentum = 0.5 * moment[...] + 0.5 * (factor * grad[...].astype(F32))
        new_moment[...] = momentum
        new_master[...] = master[...] - rate * momentum


def update(norm, rate, output, input_grad, masters, moments, grads, steps=8):
    count = len(masters)

    def block(value):
        if value.shape[0] == 1:
            return pl.BlockSpec(value.shape, lambda i: (0, 0))
        return pl.BlockSpec((value.shape[0] // steps, value.shape[1]), lambda i: (i, 0))

    ins = [v for triple in zip(masters, moments, grads) for v in triple]
    outs = [v for master in masters for v in (master, master)]
    values = pl.pallas_call(
        functools.partial(update_body, count),
        grid=(steps,),
        in_specs=[
            pl.BlockSpec(norm.shape, lambda i: (0, 0)),
            pl.BlockSpec(memory_space=pltpu.SMEM),
            block(output),
            block(input_grad),
        ]
        + [block(v) for v in ins],
        out_specs=[block(v) for v in (*outs, output, input_grad)],
        out_shape=[jax.ShapeDtypeStruct(v.shape, F32) for v in outs]
        + [
            jax.ShapeDtypeStruct(output.shape, BF),
            jax.ShapeDtypeStruct(input_grad.shape, F32),
        ],
        compiler_params=pltpu.CompilerParams(vmem_limit_bytes=VMEM),
        name="update",
    )(norm, rate.reshape(1), output, input_grad, *ins)
    *values, output, input_grad = values
    return values[0::2], values[1::2], output, input_grad


def after(*values):
    return lax.optimization_barrier(values)


def build(dps, shards):
    total = dps * shards
    axes = ("dp", "shard")
    zgroups = [[i for i in range(dps) if i % 2 == p] for p in (0, 1)]

    def swap(values, dx, ds):
        pairs = [
            (i, ((i // shards) ^ dx) * shards + ((i % shards) ^ ds)) for i in range(total)
        ]
        return lax.ppermute(values, axes, pairs)

    def gather(piece):
        return lax.all_gather(piece, "dp", axis=0, tiled=True, axis_index_groups=zgroups)

    def scatter(whole):
        return lax.psum_scatter(
            whole, "dp", scatter_dimension=0, tiled=True, axis_index_groups=zgroups
        )


    def on_device(
        tokens,
        block_ids,
        cotangent,
        gain_first,
        w_query,
        w_key,
        w_value,
        w_output,
        gain_second,
        w_gate,
        w_up,
        w_down,
        moment_first,
        moment_query,
        moment_key,
        moment_value,
        moment_output,
        moment_second,
        moment_gate,
        moment_up,
        moment_down,
        step,
        rate,
    ):
        length = block_ids.shape[1]
        width = tokens.shape[1]
        group = H // KV
        dp = lax.axis_index("dp")
        me = lax.axis_index("shard")
        x = lax.rem(dp, 2)
        quarter = length // shards
        rows = w_query.shape[0]

        def half(values, which):
            size = values.shape[1] // 2
            return lax.dynamic_slice_in_dim(values, which * size, size, axis=1)

        def ordered(mine, theirs, axis=0):
            first = jnp.where(x == 0, mine, theirs)
            second = jnp.where(x == 0, theirs, mine)
            return jnp.concatenate([first, second], axis=axis)

        def natural(parts):
            stacked = jnp.stack(parts)
            return jnp.concatenate(
                [
                    lax.dynamic_index_in_dim(stacked, me ^ q, axis=0, keepdims=False)
                    for q in range(shards)
                ],
                axis=0,
            )

        def cut(values, ds):
            return lax.dynamic_slice_in_dim(values, (me ^ ds) * quarter, quarter, axis=0)

        def halves(own, other):
            return [
                jnp.stack([cut(own, dc), cut(own, dc + 2), cut(other, dc), cut(other, dc + 2)])
                for dc in (0, 1)
            ]

        def streams(mine, theirs):
            return [
                natural([mine[k], theirs[k], mine[k + 1], theirs[k + 1]]) for k in (0, 2)
            ]

        def flat(values):
            return values.reshape(-1, values.shape[-1])

        qc = group * HD
        cols = qc + 2 * HD
        gains = jnp.stack([gain_first, gain_second]).astype(BF)
        gains = jnp.pad(gains, ((0, 14), (0, cols + qc - rows)))
        piece = opening(w_query, w_key, w_value, w_output, gains)
        groups = dps // 2

        blocks_x = swap(block_ids, 1, 0)
        low_g = w_gate.astype(BF)
        low_u = w_up.astype(BF)
        low_d = w_down.astype(BF).T
        units = low_g.shape[1] // 2
        sizes = (units * 5 // 8, units * 3 // 8)
        offsets = (0, sizes[0])

        def ffn_part(which, j):
            return jnp.concatenate(
                [
                    lax.dynamic_slice_in_dim(low, which * units + offsets[j], sizes[j], axis=1)
                    for low in (low_g, low_u, low_d)
                ],
                axis=1,
            )

        both, first_part = entry(
            after(tokens, piece[:16, :128])[0], ffn_part(x, 0), ffn_part(1 - x, 0)
        )
        ffn_weights = [gather(first_part)]
        packed = gather(piece)
        packed = packed.reshape(groups, 2 * rows + 32, cols + qc)
        out_weight = packed[:, : 2 * rows, cols:].reshape(width, qc)
        tails = packed[:, 2 * rows :].reshape(groups, 2, 16, cols + qc)
        gain_one = tails[:, :, 0, :rows].reshape(1, width).astype(F32)
        gain_two = tails[:, :, 1, :rows].reshape(1, width).astype(F32)

        cosine, sine = rope_tables(length, group)

        normed, query, key, value, cot_near = qkv(
            both, gain_one, packed, cosine, sine, cotangent, group
        )
        blocks = jnp.concatenate([block_ids, blocks_x], axis=0)
        block_rows = blocks[:, None, :]
        block_cols = blocks.reshape(2 * length, 1)
        mixed, lse, cot_far, core_near, core_far, second_x = attend(
            query, key, value, block_rows, block_cols, cot_near, ffn_part(1 - x, 1), length
        )
        ffn_weights.append(gather(ordered(ffn_part(x, 1), second_x)))
        late, _ = after(cotangent, mixed[:16, :128])
        cot_own = [cut(late, ds) for ds in range(shards)]
        cot_mine = jnp.concatenate([cot_own[0], cot_own[2], cot_near, cot_far], axis=0)
        cot_theirs = jnp.concatenate([cot_own[1], cot_own[3], core_near, core_far], axis=0)
        mixed_own, mixed_other = mixed[:length], mixed[length:]
        mixed_mine, mixed_theirs = halves(mixed_own, mixed_other)

        def project(values, weight):
            partial = jnp.einsum("atk,dk->atd", values, weight, preferred_element_type=F32)
            return partial.astype(BF)

        tokens_own = cut(tokens, 0)
        mine, theirs, hidden = mid_stage(
            project(mixed_mine, out_weight),
            project(mixed_theirs, out_weight),
            tokens_own,
            gain_two,
        )
        two_mine, two_theirs = flat(mine), flat(theirs)

        shape = (4, quarter, width)
        acts_mine = []
        acts_theirs = []
        part_mine = part_theirs = None
        first_grads = None
        for j in range(CHUNKS):
            last = j == CHUNKS - 1
            weight = ffn_weights[j]
            theirs_in = two_theirs
            if first_grads is not None:
                theirs_in, first_grads = after(two_theirs, first_grads)
            act_theirs, gu_theirs, part_theirs = up_back(
                theirs_in, cot_theirs, weight, part_theirs, last
            )
            mine_in = two_mine
            if last:
                mine_in, part_theirs = after(two_mine, part_theirs)
            act_mine, gu_mine, part_mine = up_back(mine_in, cot_mine, weight, part_mine, last)
            acts_mine.append(act_mine)
            acts_theirs.append(act_theirs)

            if not last:
                first_grads = ffn_grads(
                    (two_mine, two_theirs),
                    (cot_mine, cot_theirs),
                    (gu_mine, gu_theirs),
                    (act_mine, act_theirs),
                )
        mine, theirs, grad_hidden, gain_grad_two, last_grads, out_mine, out_theirs = back_stage(
            part_mine.reshape(shape),
            part_theirs.reshape(shape),
            hidden,
            cut(cotangent, 0),
            gain_two,
            (two_mine, two_theirs, cot_mine, cot_theirs, gu_mine, gu_theirs),
            (acts_mine, acts_theirs),
            ffn_weights,
        )
        gh_mine = mine.reshape(shape)
        gh_theirs = theirs.reshape(shape)
        first_piece = scatter(first_grads)
        last_piece = scatter(last_grads)
        grad_mixed_mine = project(gh_mine, out_weight.T)
        grad_mixed_theirs = project(gh_theirs, out_weight.T)
        grad_mixed = streams(grad_mixed_mine, grad_mixed_theirs)
        grad_q, grad_kv, output = attend_back(
            query,
            key,
            value,
            block_rows,
            block_cols,
            lse,
            jnp.concatenate(grad_mixed, axis=0),
            cosine,
            sine,
            length,
            out_mine.reshape(shape),
            out_theirs.reshape(shape),
            hidden,
        )
        grad_qkv = jnp.concatenate([grad_q, grad_kv], axis=1)
        gq_mine, gq_theirs = halves(grad_qkv[:length], grad_qkv[length:])
        d_attn, even_in, odd_in, first_theirs = attn_grads(
            normed,
            grad_qkv,
            (flat(gh_mine), flat(gh_theirs)),
            (flat(mixed_mine), flat(mixed_theirs)),
            (flat(gq_mine), flat(gq_theirs)),
            packed,
            first_piece,
        )
        grad_attn = scatter(d_attn)
        input_grad, gain_grads, last_theirs = end_stage(
            even_in.reshape(shape),
            odd_in.reshape(shape),
            tokens_own,
            grad_hidden,
            gain_one,
            gain_grad_two,
            last_piece,
            dps,
            shards,
        )
        pairs = [(first_piece, first_theirs), (last_piece, last_theirs)]
        gain_rows = gain_grads.reshape(2, dps, rows).transpose(1, 0, 2)
        own_q, own_k, own_v, own_o, own_g, own_u, own_d, norm, own_first, own_second = finish(
            grad_attn, gain_rows, pairs, dps, shards, 2
        )
        global_norm = norm[0, 0]
        owned = (own_first, own_q, own_k, own_v, own_o, own_second, own_g, own_u, own_d)
        rate_now = rate * jnp.minimum(1.0, (step.astype(F32) + 1.0) / WARMUP)
        masters = (gain_first, w_query, w_key, w_value, w_output, gain_second, w_gate, w_up, w_down)
        moments = (
            moment_first,
            moment_query,
            moment_key,
            moment_value,
            moment_output,
            moment_second,
            moment_gate,
            moment_up,
            moment_down,
        )
        lists = [
            [v.reshape(1, -1) if v.ndim == 1 else v for v in values]
            for values in (masters, moments, owned)
        ]
        *parts, output, input_grad = update(norm, rate_now, output, input_grad, *lists)
        momenta, updated = (
            [v.reshape(-1) if v.shape[0] == 1 else v for v in values] for values in parts
        )
        return (output, input_grad, global_norm, *momenta, *updated)

    return on_device


def solution(mesh):
    rows, both, back = P("dp"), P("dp", "shard"), P("shard", "dp")
    tokens = P("dp", None)
    params = (rows, both, both, both, back, rows, both, both, back)
    in_specs = (tokens, tokens, tokens, *params, *params, P(), P())
    out_specs = (tokens, tokens, P(), *params, *params)
    return jax.shard_map(
        build(mesh.shape["dp"], mesh.shape["shard"]),
        mesh=mesh,
        in_specs=in_specs,
        out_specs=out_specs,
        check_vma=False,
    )
```

```python
import functools

import jax
import jax.numpy as jnp
import numpy as np
from jax import lax
from jax.experimental import pallas as pl
from jax.experimental.pallas import tpu as pltpu
from jax.sharding import PartitionSpec as P

H = 32
KV = 8
CLIP = 4096
WARMUP = 2000
THETA = 10000000.0
CHUNKS = 2
MESH = pl.DeviceIdType.MESH


BF = jnp.bfloat16
F32 = jnp.float32
HD = 64
EPS = 1e-05
NEGATIVE = -1e30
VMEM = 60 << 20

def dot(a, b, ca, cb):
    return lax.dot_general(a, b, (((ca,), (cb,)), ((), ())), preferred_element_type=F32)

def swap_halves(v):
    n = v.shape[1]
    lane = lax.broadcasted_iota(jnp.int32, v.shape, 1)
    return jnp.where(lane % HD < HD // 2, pltpu.roll(v, n - HD // 2, 1), pltpu.roll(v, HD // 2, 1))

def qkv_body(
    tok_ref, gain_ref, w_ref, cos_ref, sin_ref, cot_ref, normed_ref, q_ref, k_ref, v_ref, near, sems
):
    rows = near.shape[0]
    at = pl.multiple_of(lax.axis_index("shard") * rows, rows)
    target = neighbours()[0]
    moving = remote(cot_ref.at[pl.ds(at, rows)], near, sems, 0, target)

    @pl.when(pl.program_id(0) == 0)
    def _():
        meet((target,))
        moving.start()

    x = tok_ref[...].astype(F32)
    inv = lax.rsqrt(jnp.mean(x * x, axis=1, keepdims=True) + EPS)
    normed = (x * inv * gain_ref[...]).astype(BF)
    normed_ref[...] = normed
    heads = q_ref.shape[0]
    qc = heads * HD
    groups, cols = w_ref.shape[0], qc + 2 * HD
    deep = normed.shape[1] // groups
    lin = sum(
        dot(normed[:, g * deep : (g + 1) * deep], w_ref[g, :deep, :cols], 1, 0)
        for g in range(groups)
    )
    rot = lin * cos_ref[...] + swap_halves(lin) * sin_ref[...]
    for h in range(heads):
        q_ref[h] = (rot[:, h * HD : (h + 1) * HD]).astype(BF)
    k_ref[...] = rot[:, qc : qc + HD].astype(BF)
    v_ref[...] = rot[:, qc + HD :].astype(BF)

    @pl.when(pl.program_id(0) == pl.num_programs(0) - 1)
    def _():
        moving.wait()


def qkv(tokens, gain, weight, cos, sin, cotangent, heads, tile=256):
    count, width = tokens.shape
    length, cols = cos.shape
    per = length // tile
    full = lambda i: (0, 0)
    row = lambda i: (i, 0)
    return pl.pallas_call(
        qkv_body,
        grid=(count // tile,),
        in_specs=[
            pl.BlockSpec((tile, width), row),
            pl.BlockSpec((1, width), full),
            pl.BlockSpec(weight.shape, lambda i: (0, 0, 0)),
            pl.BlockSpec((tile, cols), lambda i: (i % per, 0)),
            pl.BlockSpec((tile, cols), lambda i: (i % per, 0)),
            ANY,
        ],
        out_specs=[
            pl.BlockSpec((tile, width), row),
            pl.BlockSpec((heads, tile, HD), lambda i: (0, i, 0)),
            pl.BlockSpec((tile, HD), row),
            pl.BlockSpec((tile, HD), row),
            ANY,
        ],
        out_shape=[
            jax.ShapeDtypeStruct((count, width), BF),
            jax.ShapeDtypeStruct((heads, count, HD), BF),
            jax.ShapeDtypeStruct((count, HD), BF),
            jax.ShapeDtypeStruct((count, HD), BF),
            jax.ShapeDtypeStruct((cotangent.shape[0] // 4, width), BF),
        ],
        scratch_shapes=[pltpu.SemaphoreType.DMA((2, 1))],
        compiler_params=pltpu.CompilerParams(
            collective_id=10, has_side_effects=True, vmem_limit_bytes=VMEM
        ),
        cost_estimate=pl.CostEstimate(flops=2 * count * width * cols, bytes_accessed=4 * count * width, transcendentals=0),
        name="qkv_rope",
    )(tokens, gain, weight, cos, sin, cotangent)

def fwd_body(
    limits,
    q_ref,
    k_ref,
    v_ref,
    brow_ref,
    bcol_ref,
    near,
    sent,
    o_ref,
    lse_ref,
    far,
    near_core,
    far_core,
    theirs,
    sems
):
    heads, tile, _ = q_ref.shape
    i = pl.program_id(1)
    turn = pl.program_id(0) * pl.num_programs(1) + i
    targets = neighbours()
    over_y = remote(near, far, sems, 0, targets[1])
    over_core = remote(near, near_core, sems, 1, targets[2])
    last = remote(far, far_core, sems, 2, targets[2])
    over_x = remote(sent, theirs, sems, 3, targets[0])

    @pl.when(turn == 0)
    def _():
        meet(targets)
        over_y.start()
        over_x.start()
        over_core.start()

    def run(keys):
        k = k_ref[:keys]
        v = v_ref[:keys]
        allowed = brow_ref[0][:, :keys] <= bcol_ref[...]
        outs = []
        lses = []
        for h in range(heads):
            s = dot(q_ref[h] * BF(0.125), k, 1, 1)
            s = jnp.where(allowed, s, NEGATIVE)
            m = jnp.max(s, axis=1, keepdims=True)
            p = jnp.exp(s - m)
            l = jnp.sum(p, axis=1, keepdims=True)
            o = dot(p.astype(BF), v, 1, 0) / l
            outs.append(o.astype(BF))
            lses.append(m + jnp.log(l))
        o_ref[...] = jnp.concatenate(outs, axis=1)
        lse_ref[...] = jnp.concatenate(lses, axis=1)
    for n, keys in enumerate(limits):
        @pl.when(i == n)
        def _(keys=keys):
            run(keys)

    @pl.when(turn == pl.num_programs(0) * pl.num_programs(1) - 1)
    def _():
        over_y.wait_recv()
        last.start()
        over_x.wait()
        over_core.wait()
        over_y.wait_send()
        last.wait()


def attend(q, k, v, brow, bcol, near, sent, length, tile=256, most=256):
    heads, count, _ = q.shape
    seqs = count // length
    per = length // tile
    limits = tuple(min(length, (n + 1) * tile + most) for n in range(per))
    return pl.pallas_call(
        functools.partial(fwd_body, limits),
        grid=(seqs, per),
        in_specs=[
            pl.BlockSpec((heads, tile, HD), lambda b, i: (0, b * per + i, 0)),
            pl.BlockSpec((length, HD), lambda b, i: (b, 0)),
            pl.BlockSpec((length, HD), lambda b, i: (b, 0)),
            pl.BlockSpec((1, 1, length), lambda b, i: (b, 0, 0)),
            pl.BlockSpec((tile, 1), lambda b, i: (b * per + i, 0)),
            ANY,
            ANY,
        ],
        out_specs=[
            pl.BlockSpec((tile, heads * HD), lambda b, i: (b * per + i, 0)),
            pl.BlockSpec((tile, heads), lambda b, i: (b * per + i, 0)),
            ANY,
            ANY,
            ANY,
            ANY,
        ],
        out_shape=[
            jax.ShapeDtypeStruct((count, heads * HD), BF),
            jax.ShapeDtypeStruct((count, heads), F32),
            *[jax.ShapeDtypeStruct(near.shape, BF)] * 3,
            jax.ShapeDtypeStruct(sent.shape, BF),
        ],
        scratch_shapes=[pltpu.SemaphoreType.DMA((2, 4))],
        compiler_params=pltpu.CompilerParams(
            collective_id=11, has_side_effects=True, vmem_limit_bytes=VMEM
        ),
        cost_estimate=pl.CostEstimate(flops=4 * heads * count * length * HD * 4, bytes_accessed=count * 2048, transcendentals=heads * count * length),
        name="attend",
    )(q, k, v, brow, bcol, near, sent)

def bwd_body(
    limits,
    q_ref,
    k_ref,
    v_ref,
    brow_ref,
    bcol_ref,
    lse_ref,
    do_ref,
    cos_ref,
    sin_ref,
    kcos_ref,
    ksin_ref,
    even,
    odd,
    hidden_ref,
    dq_ref,
    dkv_ref,
    out_ref,
    dk_acc,
    dv_acc,
    *scratch
):
    heads, tile, _ = q_ref.shape
    i = pl.program_id(1)
    turn = pl.program_id(0) * pl.num_programs(1) + i
    targets = neighbours()
    job = Job(even, odd, scratch, targets)

    def produce(s, total):
        return hidden_ref[job.span(s)] + total

    @pl.when(turn == 0)
    def _():
        meet(targets)

    for t in range(8):

        @pl.when(turn == t)
        def _(t=t):
            line_turn(job, t, out_ref, produce)

    @pl.when(i == 0)
    def _():
        dk_acc[...] = jnp.zeros_like(dk_acc)
        dv_acc[...] = jnp.zeros_like(dv_acc)
    def run(keys):
        k = k_ref[:keys]
        v = v_ref[:keys]
        allowed = brow_ref[0][:, :keys] <= bcol_ref[...]
        dqs = []
        dk = jnp.zeros((HD, keys), F32)
        dv = jnp.zeros((HD, keys), F32)
        for h in range(heads):
            q = q_ref[h] * BF(0.125)
            do = do_ref[:, h * HD : (h + 1) * HD]
            s = dot(q, k, 1, 1)
            s = jnp.where(allowed, s, NEGATIVE)
            p = jnp.exp(s - lse_ref[:, h : h + 1])
            dp = dot(do, v, 1, 1)
            pdp = p * dp
            delta = jnp.sum(pdp, axis=1, keepdims=True)
            ds = (pdp - p * delta).astype(BF)
            dqs.append(dot(ds, k, 1, 0) * 0.125)
            dk = dk + dot(q, ds, 0, 0)
            dv = dv + dot(do, p.astype(BF), 0, 0)
        dk_acc[:, :keys] += dk
        dv_acc[:, :keys] += dv
        dq = jnp.concatenate(dqs, axis=1)
        dq_ref[...] = (dq * cos_ref[...] - swap_halves(dq) * sin_ref[...]).astype(BF)
    for n, keys in enumerate(limits):
        @pl.when(i == n)
        def _(keys=keys):
            run(keys)

    @pl.when(turn == 7)
    def _():
        for t in range(8, TURNS):
            line_turn(job, t, out_ref, produce)
        job.line_end(out_ref)

    @pl.when(i == len(limits) - 1)
    def _():
        both = jnp.concatenate([dk_acc[...], dv_acc[...]], axis=0).T
        dkv_ref[...] = (both * kcos_ref[...] - swap_halves(both) * ksin_ref[...]).astype(BF)

def attend_back(
    q, k, v, brow, bcol, lse, do, cos, sin, length, even, odd, hidden, tile=256, most=256
):
    heads, count, _ = q.shape
    seqs = count // length
    per = length // tile
    qc = heads * HD
    limits = tuple(min(length, (n + 1) * tile + most) for n in range(per))
    rowm = lambda b, i: (b * per + i, 0)
    return pl.pallas_call(
        functools.partial(bwd_body, limits),
        grid=(seqs, per),
        in_specs=[
            pl.BlockSpec((heads, tile, HD), lambda b, i: (0, b * per + i, 0)),
            pl.BlockSpec((length, HD), lambda b, i: (b, 0)),
            pl.BlockSpec((length, HD), lambda b, i: (b, 0)),
            pl.BlockSpec((1, 1, length), lambda b, i: (b, 0, 0)),
            pl.BlockSpec((tile, 1), rowm),
            pl.BlockSpec((tile, heads), rowm),
            pl.BlockSpec((tile, qc), rowm),
            pl.BlockSpec((tile, qc), lambda b, i: (i, 0)),
            pl.BlockSpec((tile, qc), lambda b, i: (i, 0)),
            pl.BlockSpec((length, 2 * HD), lambda b, i: (0, qc // (2 * HD))),
            pl.BlockSpec((length, 2 * HD), lambda b, i: (0, qc // (2 * HD))),
            IN_VMEM,
            ANY,
            IN_VMEM,
        ],
        out_specs=[
            pl.BlockSpec((tile, qc), rowm),
            pl.BlockSpec((length, 2 * HD), lambda b, i: (b, 0)),
            ANY,
        ],
        out_shape=[
            jax.ShapeDtypeStruct((count, qc), BF),
            jax.ShapeDtypeStruct((count, 2 * HD), BF),
            jax.ShapeDtypeStruct((length, even.shape[2]), BF),
        ],
        scratch_shapes=[pltpu.VMEM((HD, length), F32), pltpu.VMEM((HD, length), F32)]
        + Job.scratch(even.shape[1], even.shape[2]),
        compiler_params=pltpu.CompilerParams(
            collective_id=7, has_side_effects=True, vmem_limit_bytes=VMEM
        ),
        cost_estimate=pl.CostEstimate(flops=10 * heads * count * length * HD * 4, bytes_accessed=count * 4096, transcendentals=heads * count * length),
        name="attend_back",
    )(q, k, v, brow, bcol, lse, do, cos, sin, cos, sin, even, odd, hidden)

def rope_tables(length, heads):
    positions = np.arange(length, dtype=np.float32)
    powers = np.float32(-2.0) * np.arange(HD // 2, dtype=np.float32) / np.float32(HD)
    angles = positions[:, None] * np.power(np.float32(THETA), powers)[None, :]
    c, s = np.cos(angles), np.sin(angles)
    zeros = np.zeros((length, HD), np.float32)
    cos = [c, c] * (heads + 1) + [zeros + 1]
    sin = [-s, s] * (heads + 1) + [zeros]
    return (jnp.asarray(np.concatenate(v, axis=1).astype(np.float32)) for v in (cos, sin))


def up_body(first, last, n2_ref, cot_ref, w_ref, *rest):
    if first:
        act_ref, dgu_ref, part_ref = rest
    else:
        prev_ref, act_ref, dgu_ref, part_ref = rest
    size = act_ref.shape[1]
    gu = dot(n2_ref[...], w_ref[:, : 2 * size], 1, 0)
    da = dot(cot_ref[...], w_ref[:, 2 * size :], 1, 0)
    gate, up = gu[:, :size], gu[:, size:]
    sig = 1.0 / (1.0 + jnp.exp(-gate))
    gs = gate * sig
    act_ref[...] = (gs * up).astype(BF)
    dg = (da * up * sig * (1.0 + gate * (1.0 - sig))).astype(BF)
    du = (da * gs).astype(BF)
    dgu = jnp.concatenate([dg, du], axis=1)
    dgu_ref[...] = dgu
    part = dot(dgu, w_ref[:, : 2 * size], 1, 1)
    if not first:
        part = part + prev_ref[...]
    part_ref[...] = part.astype(part_ref.dtype)

def up_back(n2, cot, weight, prev, last, tile=256):
    count, width = n2.shape
    size = weight.shape[1] // 3
    row = lambda i: (i, 0)
    full = lambda i: (0, 0)
    ins = [n2, cot, weight] + ([] if prev is None else [prev])
    specs = [pl.BlockSpec((tile, width), row), pl.BlockSpec((tile, width), row), pl.BlockSpec((width, 3 * size), full, pipeline_mode=pl.Buffered(1))]
    if prev is not None:
        specs.append(pl.BlockSpec((tile, width), row))
    return pl.pallas_call(
        functools.partial(up_body, prev is None, last),
        grid=(count // tile,),
        in_specs=specs,
        out_specs=[pl.BlockSpec((tile, size), row), pl.BlockSpec((tile, 2 * size), row), pl.BlockSpec((tile, width), row)],
        out_shape=[jax.ShapeDtypeStruct((count, size), BF), jax.ShapeDtypeStruct((count, 2 * size), BF), jax.ShapeDtypeStruct((count, width), BF if last else F32)],
        compiler_params=pltpu.CompilerParams(vmem_limit_bytes=VMEM),
        cost_estimate=pl.CostEstimate(flops=2 * count * width * size * 5, bytes_accessed=12 * count * width, transcendentals=count * size),
        name="swiglu_part",
    )(*ins)

def grad_body(n2a, n2b, cota, cotb, dgua, dgub, acta, actb, o_ref):
    size = acta.shape[1]
    gu = dot(n2a[...], dgua[...], 0, 0) + dot(n2b[...], dgub[...], 0, 0)
    o_ref[:, : 2 * size] = gu.astype(BF)
    dt = dot(cota[...], acta[...], 0, 0) + dot(cotb[...], actb[...], 0, 0)
    o_ref[:, 2 * size :] = dt.astype(BF)


def ffn_grads(n2, cot, dgu, act, tile=256):
    count, width = n2[0].shape
    size = act[0].shape[1]
    col = lambda i: (0, i)
    full = lambda i: (0, 0)
    return pl.pallas_call(
        grad_body,
        grid=(width // tile,),
        in_specs=[pl.BlockSpec((count, tile), col)] * 4
        + [pl.BlockSpec((count, 2 * size), full, pipeline_mode=pl.Buffered(1))] * 2
        + [pl.BlockSpec((count, size), full, pipeline_mode=pl.Buffered(1))] * 2,
        out_specs=pl.BlockSpec((tile, 3 * size), lambda i: (i, 0)),
        out_shape=jax.ShapeDtypeStruct((width, 3 * size), BF),
        compiler_params=pltpu.CompilerParams(vmem_limit_bytes=VMEM),
        cost_estimate=pl.CostEstimate(
            flops=4 * count * width * size * 3,
            bytes_accessed=16 * count * width,
            transcendentals=0,
        ),
        name="swiglu_grads",
    )(*n2, *cot, *dgu, *act)


def attn_grad_body(
    na, ga, ha, hb, ma, mb, qa, qb, w_ref, piece, o_ref, even, odd, theirs, sems
):
    cols = ga.shape[1]
    step = pl.program_id(0)
    swapped = trade(piece, theirs, sems)

    @pl.when(step == 0)
    def _():
        meet(neighbours()[:1])
        swapped.start()

    o_ref[:, :cols] = dot(na[...], ga[...], 0, 0).astype(BF)
    o_ref[:, cols:] = (dot(ha[...], ma[...], 0, 0) + dot(hb[...], mb[...], 0, 0)).astype(BF)
    even[...] = dot(qa[...], w_ref[0], 1, 1).astype(BF)
    odd[...] = dot(qb[...], w_ref[0], 1, 1).astype(BF)

    @pl.when(step == pl.num_programs(0) - 1)
    def _():
        swapped.wait()


def attn_grads(normed, grads, hidden, mixed, halves, packed, piece, tile=256):
    width = normed.shape[1]
    count, cols = halves[0].shape
    col = lambda i: (0, i)
    tile = min(tile, width // packed.shape[0])
    per = width // packed.shape[0] // tile
    ins = [normed, grads, *hidden, *mixed, *halves, packed, piece]
    wide = cols + mixed[0].shape[1]

    def tiled(value):
        return pl.BlockSpec((value.shape[0], tile), col)

    def whole(value):
        return pl.BlockSpec(value.shape, lambda i: (0, 0), pipeline_mode=pl.Buffered(1))

    return pl.pallas_call(
        attn_grad_body,
        grid=(width // tile,),
        in_specs=[tiled(normed), whole(grads)]
        + [tiled(v) for v in hidden]
        + [whole(v) for v in (*mixed, *halves)]
        + [pl.BlockSpec((1, tile, cols), lambda i: (i // per, i % per, 0)), ANY],
        out_specs=[
            pl.BlockSpec((tile, wide), lambda i: (i, 0)),
            pl.BlockSpec((count, tile), col),
            pl.BlockSpec((count, tile), col),
            ANY,
        ],
        out_shape=[
            jax.ShapeDtypeStruct((width, wide), BF),
            jax.ShapeDtypeStruct((count, width), BF),
            jax.ShapeDtypeStruct((count, width), BF),
            jax.ShapeDtypeStruct((piece.shape[0] // 2, piece.shape[1]), BF),
        ],
        scratch_shapes=[pltpu.SemaphoreType.DMA((2, 1))],
        compiler_params=pltpu.CompilerParams(
            collective_id=9, has_side_effects=True, vmem_limit_bytes=VMEM
        ),
        name="attn_grads",
    )(*ins)


def peers(dps, shards):
    dp, sh = lax.axis_index("dp"), lax.axis_index("shard")
    groups = dps // 2
    near = []
    for r in range(1, 2 * shards):
        there = sh
        for bit in (1, 2):
            there = flip(there, bit) if r % shards & bit else there
        near.append((flip(dp, 1) if r >= shards else dp, there))
    far = [
        (lax.rem(dp // 2 + p, groups) * 2 + lax.rem(dp, 2), sh) for p in range(1, groups)
    ]
    return near, far, lax.rem(dp, 2) * shards + sh, dp // 2


def greet(targets):
    barrier = pltpu.get_barrier_semaphore()
    for target in targets:
        pl.semaphore_signal(barrier, inc=1, device_id=target, device_id_type=MESH)


def meet(targets):
    greet(targets)
    pl.semaphore_wait(pltpu.get_barrier_semaphore(), len(targets))


def exchange(values, slots, mine, targets, source, send, recv, base):
    source[...] = values
    slots[mine] = values
    copies = [
        pltpu.make_async_remote_copy(
            src_ref=source,
            dst_ref=slots.at[mine],
            send_sem=send.at[base + n],
            recv_sem=recv.at[base + n],
            device_id=target,
            device_id_type=MESH,
        )
        for n, target in enumerate(targets)
    ]
    for copy in copies:
        copy.start()
    for copy in copies:
        copy.wait()
    total = slots[0]
    for n in range(1, slots.shape[0]):
        total = total + slots[n]
    return total


def two_stages(values, near, far, me, outer, bufs):
    slots_near, slots_far, from_near, from_far, send, recv = bufs
    total = exchange(values, slots_near, me, near, from_near, send, recv, 0)
    return exchange(total, slots_far, outer, far, from_far, send, recv, len(near))


def sum_scratch(shape, dps, shards):
    count = 2 * shards - 1 + dps // 2 - 1
    return [
        pltpu.VMEM((2 * shards,) + shape, F32),
        pltpu.VMEM((dps // 2,) + shape, F32),
        pltpu.VMEM(shape, F32),
        pltpu.VMEM(shape, F32),
        pltpu.SemaphoreType.DMA((count,)),
        pltpu.SemaphoreType.DMA((count,)),
    ]


def pick(x, first, second):
    low = jnp.where(x == 0, first.astype(F32), second.astype(F32)).astype(BF)
    high = jnp.where(x == 0, second.astype(F32), first.astype(F32)).astype(BF)
    return low, high


def finish_body(dps, shards, count, piece_ref, gain_ref, *refs):
    ins, outs, scratch = refs[: 2 * count], refs[2 * count : 2 * count + 10], refs[2 * count + 10 :]
    q_ref, k_ref, v_ref, o_ref, g_ref, u_ref, d_ref, norm_ref, first_ref, second_ref = outs
    theirs, pair, *bufs = scratch
    near, far, me, outer = peers(dps, shards)
    rows = piece_ref.shape[0] // 2
    qc = q_ref.shape[1] // 2
    x = lax.rem(lax.axis_index("dp"), 2)
    here = pl.ds(pl.multiple_of(x * rows, rows), rows)
    meet(near + far)
    swapped = trade(piece_ref, theirs, pair)
    swapped.start()
    gains = gain_ref[lax.axis_index("dp")]
    first_ref[...] = gains[0:1]
    second_ref[...] = gains[1:2]
    once = jnp.where(lax.axis_index("shard") == 0, 1.0, 0.0)
    squares = once * jnp.sum(gains * gains, keepdims=True)
    half = g_ref.shape[1] // 2
    at = 0
    for j in range(count):
        size = ins[2 * j].shape[1] // 3
        for h, piece in enumerate(pick(x, ins[2 * j][here, :], ins[2 * j + 1][...])):
            wide = piece.astype(F32)
            squares = squares + jnp.sum(wide * wide, keepdims=True)
            span = pl.ds(h * half + at, size)
            g_ref[:, span] = piece[:, :size]
            u_ref[:, span] = piece[:, size : 2 * size]
            d_ref[span, :] = wide[:, 2 * size :].T.astype(BF)
        at = at + size
    mine = piece_ref[here, :]
    wide = mine.astype(F32)
    squares = squares + jnp.sum(wide * wide, keepdims=True)
    swapped.wait()
    got = theirs[...]
    wide = got.astype(F32)
    squares = squares + jnp.sum(wide * wide, keepdims=True)
    values = jnp.broadcast_to(squares, norm_ref.shape)
    norm_ref[...] = jnp.sqrt(two_stages(values, near, far, me, outer, bufs))
    low, high = pick(x, mine, got)
    q_ref[:, :qc] = low[:, :qc]
    q_ref[:, qc:] = high[:, :qc]
    k_ref[...] = jnp.concatenate([low[:, qc : qc + HD], high[:, qc : qc + HD]], axis=1)
    vc, oc = qc + HD, qc + 2 * HD
    v_ref[...] = jnp.concatenate([low[:, vc:oc], high[:, vc:oc]], axis=1)
    o_ref[:qc] = low[:, oc:].astype(F32).T.astype(BF)
    o_ref[qc:] = high[:, oc:].astype(F32).T.astype(BF)


def finish(piece, gains, pairs, dps, shards, number):
    rows, cols = piece.shape[0] // 2, piece.shape[1]
    qc = (cols - 2 * HD) // 2
    wide = 2 * sum(other.shape[1] // 3 for _, other in pairs)
    vmem = pl.BlockSpec(memory_space=pltpu.VMEM)
    ins = [v for pair in pairs for v in pair]
    shapes = ((rows, 2 * qc), (rows, 2 * HD), (rows, 2 * HD), (2 * qc, rows))
    shapes = shapes + ((rows, wide), (rows, wide), (wide, rows))
    return pl.pallas_call(
        functools.partial(finish_body, dps, shards, len(pairs)),
        in_specs=[vmem] * (2 + len(ins)),
        out_specs=[vmem] * 10,
        out_shape=[jax.ShapeDtypeStruct(shape, BF) for shape in shapes]
        + [jax.ShapeDtypeStruct(v, F32) for v in ((8, 128), (1, rows), (1, rows))],
        scratch_shapes=[pltpu.VMEM((rows, cols), BF), pltpu.SemaphoreType.DMA((2, 1))]
        + sum_scratch((8, 128), dps, shards),
        compiler_params=pltpu.CompilerParams(
            collective_id=number, has_side_effects=True, vmem_limit_bytes=VMEM
        ),
        name="finish",
    )(piece, gains, *ins)


PARTS = 8


def flip(value, bit):
    return value + bit * (1 - 2 * lax.rem(value // bit, 2))


def neighbours():
    dp, sh = lax.axis_index("dp"), lax.axis_index("shard")
    return (flip(dp, 1), sh), (dp, flip(sh, 2)), (dp, flip(sh, 1))


def remote(src, dst, sems, n, target):
    return pltpu.make_async_remote_copy(
        src_ref=src,
        dst_ref=dst,
        send_sem=sems.at[0, n],
        recv_sem=sems.at[1, n],
        device_id=target,
        device_id_type=MESH,
    )


class Job:

    def __init__(self, even, odd, scratch, targets, y_first=()):
        self.y_first = y_first
        self.even, self.odd = even, odd
        self.got, self.out1, self.in1, self.out2, self.in2, self.own, self.sems, self.local = scratch
        self.x, self.y, self.core = targets
        self.rows = even.shape[1] // PARTS

    @staticmethod
    def scratch(rows, width):
        part = rows // PARTS
        return [
            pltpu.VMEM((4, rows, width), BF),
            pltpu.VMEM((PARTS, 2, part, width), BF),
            pltpu.VMEM((PARTS, 2, part, width), BF),
            pltpu.VMEM((PARTS, part, width), BF),
            pltpu.VMEM((PARTS, part, width), BF),
            pltpu.VMEM((rows, width), BF),
            pltpu.SemaphoreType.DMA((2, 6 * PARTS)),
            pltpu.SemaphoreType.DMA((PARTS,)),
        ]

    def span(self, s):
        return pl.ds(s * self.rows, self.rows)

    def over_x(self, s):
        return s not in self.y_first

    def copy(self, stage, s, src, dst, target):
        return remote(src, dst, self.sems, stage * PARTS + s, target)

    def to_core(self, s):
        span = self.span(s)
        return self.copy(0, s, self.odd.at[:, span], self.got.at[:, span], self.core)

    def to_first(self, s):
        target = self.x if self.over_x(s) else self.y
        return self.copy(1, s, self.out1.at[s], self.in1.at[s], target)

    def to_second(self, s):
        target = self.y if self.over_x(s) else self.x
        return self.copy(2, s, self.out2.at[s], self.in2.at[s], target)

    def start(self):
        for s in range(4):
            self.to_core(s).start()

    def pair(self, k, s):
        return self.even[k, self.span(s)].astype(F32) + self.got[k, self.span(s)].astype(F32)

    def first(self, s):
        self.to_core(s).wait_recv()
        if s + 4 < PARTS:
            self.to_core(s + 4).start()
        self.out1[s, 0] = self.pair(2 if self.over_x(s) else 1, s).astype(BF)
        self.out1[s, 1] = self.pair(3, s).astype(BF)
        self.to_first(s).start()

    def second(self, s):
        self.to_first(s).wait_recv()
        near = self.pair(1 if self.over_x(s) else 2, s)
        self.out2[s] = (near + self.in1[s, 1].astype(F32)).astype(BF)
        self.to_second(s).start()

    def total(self, s):
        self.to_second(s).wait_recv()
        return self.pair(0, s) + self.in1[s, 0].astype(F32) + self.in2[s].astype(F32)

    def sent(self):
        for s in range(PARTS):
            self.to_core(s).wait_send()
            self.to_first(s).wait_send()
            self.to_second(s).wait_send()


    def keep(self, s, place):
        return pltpu.make_async_copy(self.own.at[self.span(s)], place, self.local.at[s])

    def spread_copies(self, s, mine, theirs):
        span = self.span(s)
        own = self.own.at[span]
        if self.over_x(s):
            near = self.copy(3, s, own, mine.at[1, 0, span], self.x)
            far = self.copy(4, s, mine.at[:, 0, span], mine.at[:, 1, span], self.y)
        else:
            near = self.copy(3, s, own, mine.at[0, 1, span], self.y)
            far = self.copy(4, s, mine.at[0, :, span], mine.at[1, :, span], self.x)
        core = self.copy(5, s, mine.at[:, :, span], theirs.at[:, :, span], self.core)
        return self.keep(s, mine.at[0, 0, span]), near, far, core


    def line_copies(self, s, whole):
        me = lax.axis_index("shard")
        size = self.rows * PARTS

        def place(owner):
            at = pl.multiple_of(owner * size + s * self.rows, self.rows)
            return whole.at[pl.ds(at, self.rows)]

        own = self.own.at[self.span(s)]
        near = self.copy(3, s, own, place(me), self.y)
        core = self.copy(4, s, own, place(me), self.core)
        other = place(flip(me, 2))
        return self.keep(s, place(me)), near, core, self.copy(5, s, other, other, self.core)

    def line_start(self, s, whole):
        for copy in self.line_copies(s, whole)[:3]:
            copy.start()

    def line_core(self, s, whole):
        keep, near, core, far = self.line_copies(s, whole)
        keep.wait()
        near.wait_recv()
        far.start()

    def line_end(self, whole):
        for s in range(PARTS):
            _, near, core, far = self.line_copies(s, whole)
            core.wait_recv()
            far.wait_recv()
            for copy in (near, core, far):
                copy.wait_send()
        self.sent()


def run_job(job, mine, theirs, produce, hook, window=4, lag=2):
    copies = [job.spread_copies(s, mine, theirs) for s in range(PARTS)]
    job.start()
    for s in range(window):
        job.first(s)
    for t in range(PARTS + 3 * lag):
        hook(t)
        if t < PARTS:
            job.second(t)
            if t + window < PARTS:
                job.first(t + window)
        if 0 <= t - lag < PARTS:
            s = t - lag
            job.own[job.span(s)] = produce(s, job.total(s)).astype(BF)
            copies[s][0].start()
            copies[s][1].start()
        if 0 <= t - 2 * lag < PARTS:
            keep, near, far, _ = copies[t - 2 * lag]
            keep.wait()
            near.wait_recv()
            far.start()
        if 0 <= t - 3 * lag < PARTS:
            _, _, far, core = copies[t - 3 * lag]
            far.wait_recv()
            core.start()
    for _, near, far, core in copies:
        core.wait_recv()
        for copy in (near, far, core):
            copy.wait_send()
    job.sent()


def line_turn(job, t, whole, produce, window=3, lag=1):
    if t == 0:
        job.start()
        for s in range(window):
            job.first(s)
    if 0 <= t - 1 < PARTS:
        job.second(t - 1)
        if t - 1 + window < PARTS:
            job.first(t - 1 + window)
    if 0 <= t - 1 - lag < PARTS:
        s = t - 1 - lag
        job.own[job.span(s)] = produce(s, job.total(s)).astype(BF)
        job.line_start(s, whole)
    if 0 <= t - 1 - 2 * lag < PARTS:
        job.line_core(t - 1 - 2 * lag, whole)


TURNS = PARTS + 5


def rms_of(values):
    return lax.rsqrt(jnp.mean(values * values, axis=1, keepdims=True) + EPS)


def norm_back_of(values, gain, grad):
    inverse = rms_of(values)
    scaled = grad * gain
    total = jnp.sum(grad * values * inverse, axis=0, keepdims=True)
    mean = jnp.mean(scaled * values, axis=1, keepdims=True)
    return total, inverse * scaled - values * (inverse * inverse * inverse * mean)


def mid_body(even, odd, tok_ref, gain_ref, mine, theirs, hidden_ref, *scratch):
    targets = neighbours()
    meet(targets)
    job = Job(even, odd, scratch, targets, range(1, PARTS, 2))

    def produce(s, total):
        hidden = tok_ref[job.span(s)].astype(F32) + total
        hidden_ref[job.span(s)] = hidden
        return hidden * rms_of(hidden) * gain_ref[...]

    run_job(job, mine, theirs, produce, lambda t: None)


def back_body(even, odd, hidden_ref, cot_ref, gain_ref, *rest):
    chunks = CHUNKS
    count = 6 + 3 * chunks
    ins, outs, scratch = rest[:count], rest[count : count + 7], rest[count + 7 :]
    mine, theirs, gh_ref, gg_ref, dw_ref, down_a, down_b = outs
    held = scratch[8 : 8 + count]
    tiles, store, load, down_tiles, down_store = scratch[8 + count :]
    targets = neighbours()
    loads = []
    for n, (src, dst) in enumerate(zip(ins, held)):
        wide = src.shape[1] - dst.shape[1]
        src = src.at[:, pl.ds(wide, dst.shape[1])] if wide else src
        loads.append(pltpu.make_async_copy(src, dst, load.at[n]))
    for copy in loads:
        copy.start()
    meet(targets)
    job = Job(even, odd, scratch[:8], targets, range(1, PARTS, 2))
    na, nb, ca, cb, ga, gb = held[:6]
    acts_a, acts_b, downs = held[6 : 6 + chunks], held[6 + chunks : 6 + 2 * chunks], held[6 + 2 * chunks :]
    aa, ab = acts_a[-1], acts_b[-1]
    size = aa.shape[1]
    step = tiles.shape[1]
    sites = 4
    half = dw_ref.shape[0] // step // sites
    rows = down_tiles.shape[1]

    def filler(part):
        if part == 0:
            for copy in loads:
                copy.wait()

        def tile(n, carry):
            cols = pl.ds(pl.multiple_of((part * half + n) * step, step), step)
            gu = dot(na[:, cols], ga[...], 0, 0) + dot(nb[:, cols], gb[...], 0, 0)
            tiles[n, :, : 2 * size] = gu.astype(BF)
            dt = dot(ca[:, cols], aa[...], 0, 0) + dot(cb[:, cols], ab[...], 0, 0)
            tiles[n, :, 2 * size :] = dt.astype(BF)
            pltpu.make_async_copy(tiles.at[n], dw_ref.at[cols], store.at[n]).start()
            return carry

        lax.fori_loop(0, half, tile, 0)
        span = pl.ds(part * rows, rows)
        for n, (acts, out) in enumerate(((acts_a, down_a), (acts_b, down_b))):
            total = dot(acts[0][span], downs[0][...], 1, 1)
            for j in range(1, chunks):
                total = total + dot(acts[j][span], downs[j][...], 1, 1)
            down_tiles[n] = total.astype(BF)
            pltpu.make_async_copy(down_tiles.at[n], out.at[span], down_store.at[n]).start()

    def settle(part):
        span = pl.ds(part * rows, rows)
        for n in range(half):
            cols = pl.ds((part * half + n) * step, step)
            pltpu.make_async_copy(tiles.at[n], dw_ref.at[cols], store.at[n]).wait()
        for n, out in enumerate((down_a, down_b)):
            pltpu.make_async_copy(down_tiles.at[n], out.at[span], down_store.at[n]).wait()

    def hook(t):
        if t % 2 == 0 and t // 2 < sites:
            if t > 0:
                settle(t // 2 - 1)
            filler(t // 2)

    totals = []

    def produce(s, total):
        gain_total, through = norm_back_of(hidden_ref[job.span(s)], gain_ref[...], total)
        totals.append(gain_total)
        grad_hidden = cot_ref[job.span(s)].astype(F32) + through
        gh_ref[job.span(s)] = grad_hidden
        return grad_hidden

    run_job(job, mine, theirs, produce, hook)
    settle(sites - 1)
    gg_ref[...] = sum(totals[1:], totals[0])


def trade(piece, theirs, sems):
    size = theirs.shape[0]
    x = lax.rem(lax.axis_index("dp"), 2)
    src = piece.at[pl.ds(pl.multiple_of((1 - x) * size, size), size)]
    return remote(src, theirs, sems, 0, neighbours()[0])


def end_body(
    dps, shards, even, odd, tok_ref, gh_ref, gain_ref, gg_ref, piece, in_ref, sum_ref, theirs, *scratch
):
    near, far, me, outer = peers(dps, shards)
    meet(near + far)
    job = Job(even, odd, scratch[:8], neighbours(), (1, 4, 7))
    swapped = trade(piece, theirs, scratch[8])
    totals = []

    def produce(s, total):
        span = job.span(s)
        gain_total, through = norm_back_of(tok_ref[span].astype(F32), gain_ref[...], total)
        totals.append(gain_total)
        return gh_ref[span] + through

    for t in range(TURNS):
        line_turn(job, t, in_ref, produce, lag=2)
        if t == 6:
            swapped.start()
    gains = jnp.concatenate([sum(totals[1:], totals[0]), gg_ref[...]], axis=0)
    sum_ref[...] = two_stages(gains, near, far, me, outer, scratch[9:])
    job.line_end(in_ref)
    swapped.wait()


def open_body(q_ref, k_ref, v_ref, o_ref, gain_ref, piece, sent, sems):
    rows = q_ref.shape[0]
    qc = q_ref.shape[1] // 2
    x = lax.rem(lax.axis_index("dp"), 2)
    target = neighbours()[0]
    barrier = pltpu.get_barrier_semaphore()
    pl.semaphore_signal(barrier, inc=1, device_id=target, device_id_type=MESH)

    def fill(ref, base, which):
        at = pl.ds(pl.multiple_of(base, 16), rows)

        def narrow(value):
            return jnp.where(which == 0, value[:, :HD], value[:, HD:]).astype(BF)

        ref[at, :qc] = q_ref[:, pl.ds(pl.multiple_of(which * qc, qc), qc)].astype(BF)
        ref[at, qc : qc + HD] = narrow(k_ref[...])
        ref[at, qc + HD : qc + 2 * HD] = narrow(v_ref[...])
        out = o_ref[pl.ds(pl.multiple_of(which * qc, qc), qc), :]
        ref[at, qc + 2 * HD :] = out.T.astype(BF)

    fill(sent, 0, 1 - x)
    sent[rows:] = gain_ref[...]
    pl.semaphore_wait(barrier, 1)
    spots = (
        piece.at[pl.ds(pl.multiple_of(x * rows, 16), rows)],
        piece.at[pl.ds(pl.multiple_of(2 * rows + x * 16, 16), 16)],
    )
    copies = [
        remote(sent.at[pl.ds(0, rows)], spots[0], sems, 0, target),
        remote(sent.at[pl.ds(rows, 16)], spots[1], sems, 1, target),
    ]
    for copy in copies:
        copy.start()
    fill(piece, x * rows, x)
    piece[pl.ds(pl.multiple_of(2 * rows + x * 16, 16), 16)] = gain_ref[...]
    for copy in copies:
        copy.wait()


def opening(w_query, w_key, w_value, w_output, gains):
    rows, cols = w_query.shape[0], gains.shape[1]
    return pl.pallas_call(
        open_body,
        in_specs=[IN_VMEM] * 5,
        out_specs=IN_VMEM,
        out_shape=jax.ShapeDtypeStruct((2 * rows + 32, cols), BF),
        scratch_shapes=[
            pltpu.VMEM((rows + 16, cols), BF),
            pltpu.SemaphoreType.DMA((2, 2)),
        ],
        compiler_params=pltpu.CompilerParams(
            collective_id=8, has_side_effects=True, vmem_limit_bytes=16 << 20
        ),
        name="opening",
    )(w_query, w_key, w_value, w_output, gains)


def entry_body(tok_ref, keep_ref, send_ref, both, piece, hop_x, hop_y, hop_core, weight_sem, keeps):
    xs, ys, core = neighbours()
    sh = lax.axis_index("shard")
    x = lax.rem(lax.axis_index("dp"), 2)
    length = tok_ref.shape[0]
    quarter = length // 4
    rows = quarter // PARTS
    size = keep_ref.shape[0]
    mine = piece.at[pl.ds(pl.multiple_of(x * size, size), size)]
    local = [
        pltpu.make_async_copy(keep_ref, mine, keeps.at[0]),
        pltpu.make_async_copy(tok_ref, both.at[pl.ds(0, length)], keeps.at[1]),
    ]
    for copy in local:
        copy.start()
    meet((xs, ys, core))

    def rows_of(ref, base, owner, s):
        return ref.at[pl.ds(pl.multiple_of(base + owner * quarter + s * rows, rows), rows)]

    over_x, over_y, over_core, over_far = [], [], [], []
    for s in range(PARTS):
        near, far = rows_of(both, length, sh, s), rows_of(both, length, flip(sh, 2), s)
        over_x.append(remote(rows_of(tok_ref, 0, sh, s), near, hop_x, s, xs))
        over_y.append(remote(near, near, hop_y, s, ys))
        over_core.append(remote(near, near, hop_core, s, core))
        over_far.append(remote(far, far, hop_core, PARTS + s, core))
    moving = remote(send_ref, mine, weight_sem, 0, xs)
    for copy in over_x:
        copy.start()
    moving.start()
    for s in range(PARTS):
        over_x[s].wait_recv()
        over_y[s].start()
        over_core[s].start()
    for s in range(PARTS):
        over_y[s].wait_recv()
        over_far[s].start()
    moving.wait()
    for copy in over_core + over_far:
        copy.wait()
    for copy in over_x + over_y:
        copy.wait_send()
    for copy in local:
        copy.wait()


def entry(tokens, keep, sent):
    length, width = tokens.shape
    dma = pltpu.SemaphoreType.DMA
    return pl.pallas_call(
        entry_body,
        in_specs=[ANY] * 3,
        out_specs=[ANY] * 2,
        out_shape=[
            jax.ShapeDtypeStruct((2 * length, width), BF),
            jax.ShapeDtypeStruct((2 * keep.shape[0], keep.shape[1]), BF),
        ],
        scratch_shapes=[
            dma((2, PARTS)),
            dma((2, PARTS)),
            dma((2, 2 * PARTS)),
            dma((2, 1)),
            dma((2,)),
        ],
        compiler_params=pltpu.CompilerParams(
            collective_id=6, has_side_effects=True, vmem_limit_bytes=8 << 20
        ),
        name="entry",
    )(tokens, keep, sent)


ANY = pl.BlockSpec(memory_space=pl.ANY)
IN_VMEM = pl.BlockSpec(memory_space=pltpu.VMEM)
BIG = 60 << 20


def mid_stage(even, odd, tokens_own, gain):
    _, rows, width = even.shape
    half = jax.ShapeDtypeStruct((2, 2, rows, width), BF)
    return pl.pallas_call(
        mid_body,
        in_specs=[IN_VMEM, ANY, IN_VMEM, IN_VMEM],
        out_specs=[ANY, ANY, IN_VMEM],
        out_shape=[half, half, jax.ShapeDtypeStruct((rows, width), F32)],
        scratch_shapes=Job.scratch(rows, width),
        compiler_params=pltpu.CompilerParams(
            collective_id=3, has_side_effects=True, vmem_limit_bytes=VMEM
        ),
        name="mid_stage",
    )(even, odd, tokens_own, gain)


def back_stage(even, odd, hidden, cot_own, gain, halves, acts, weights, tile=256):
    _, rows, width = even.shape
    count = halves[0].shape[0]
    sizes = [act.shape[1] for act in acts[0]]
    filling = list(halves) + list(acts[0]) + list(acts[1]) + list(weights)
    held = [pltpu.VMEM(v.shape, BF) for v in filling[: 6 + 2 * len(sizes)]]
    held += [pltpu.VMEM((width, size), BF) for size in sizes]
    spread_shape = jax.ShapeDtypeStruct((2, 2, rows, width), BF)
    down_shape = jax.ShapeDtypeStruct((count, width), BF)
    dma = pltpu.SemaphoreType.DMA
    return pl.pallas_call(
        back_body,
        in_specs=[IN_VMEM, ANY, IN_VMEM, IN_VMEM, IN_VMEM] + [ANY] * len(filling),
        out_specs=[ANY, ANY, IN_VMEM, IN_VMEM, ANY, ANY, ANY],
        out_shape=[
            spread_shape,
            spread_shape,
            jax.ShapeDtypeStruct((rows, width), F32),
            jax.ShapeDtypeStruct((1, width), F32),
            jax.ShapeDtypeStruct((width, 3 * sizes[-1]), BF),
            down_shape,
            down_shape,
        ],
        scratch_shapes=Job.scratch(rows, width)
        + held
        + [
            pltpu.VMEM((width // tile // 4, tile, 3 * sizes[-1]), BF),
            dma((width // tile // 4,)),
            dma((len(filling),)),
            pltpu.VMEM((2, count // 4, width), BF),
            dma((2,)),
        ],
        compiler_params=pltpu.CompilerParams(
            collective_id=4, has_side_effects=True, vmem_limit_bytes=BIG
        ),
        name="back_stage",
    )(even, odd, hidden, cot_own, gain, *filling)


def end_stage(even, odd, tokens_own, grad_hidden, gain, gain_grad, piece, dps, shards):
    _, rows, width = even.shape
    theirs = jax.ShapeDtypeStruct((piece.shape[0] // 2, piece.shape[1]), BF)
    return pl.pallas_call(
        functools.partial(end_body, dps, shards),
        in_specs=[IN_VMEM, ANY] + [IN_VMEM] * 4 + [ANY],
        out_specs=[ANY, IN_VMEM, ANY],
        out_shape=[
            jax.ShapeDtypeStruct((shards * rows, width), BF),
            jax.ShapeDtypeStruct((2, width), F32),
            theirs,
        ],
        scratch_shapes=Job.scratch(rows, width)
        + [pltpu.SemaphoreType.DMA((2, 1))]
        + sum_scratch((2, width), dps, shards),
        compiler_params=pltpu.CompilerParams(
            collective_id=5, has_side_effects=True, vmem_limit_bytes=VMEM
        ),
        name="end_stage",
    )(even, odd, tokens_own, grad_hidden, gain, gain_grad, piece)


def update_body(count, norm_ref, rate_ref, out_ref, in_ref, *refs):
    refs, (new_out, new_in) = refs[:-2], refs[-2:]
    new_out[...] = out_ref[...]
    new_in[...] = in_ref[...].astype(F32)
    factor = jnp.minimum(1.0, CLIP / norm_ref[0:1, 0:1])
    rate = rate_ref[0]
    for n in range(count):
        master, moment, grad = (refs[3 * n + k] for k in range(3))
        new_moment, new_master = refs[3 * count + 2 * n], refs[3 * count + 2 * n + 1]
        momentum = 0.5 * moment[...] + 0.5 * (factor * grad[...].astype(F32))
        new_moment[...] = momentum
        new_master[...] = master[...] - rate * momentum


def update(norm, rate, output, input_grad, masters, moments, grads, steps=8):
    count = len(masters)

    def block(value):
        if value.shape[0] == 1:
            return pl.BlockSpec(value.shape, lambda i: (0, 0))
        return pl.BlockSpec((value.shape[0] // steps, value.shape[1]), lambda i: (i, 0))

    ins = [v for triple in zip(masters, moments, grads) for v in triple]
    outs = [v for master in masters for v in (master, master)]
    values = pl.pallas_call(
        functools.partial(update_body, count),
        grid=(steps,),
        in_specs=[
            pl.BlockSpec(norm.shape, lambda i: (0, 0)),
            pl.BlockSpec(memory_space=pltpu.SMEM),
            block(output),
            block(input_grad),
        ]
        + [block(v) for v in ins],
        out_specs=[block(v) for v in (*outs, output, input_grad)],
        out_shape=[jax.ShapeDtypeStruct(v.shape, F32) for v in outs]
        + [
            jax.ShapeDtypeStruct(output.shape, BF),
            jax.ShapeDtypeStruct(input_grad.shape, F32),
        ],
        compiler_params=pltpu.CompilerParams(vmem_limit_bytes=VMEM),
        name="update",
    )(norm, rate.reshape(1), output, input_grad, *ins)
    *values, output, input_grad = values
    return values[0::2], values[1::2], output, input_grad


def after(*values):
    return lax.optimization_barrier(values)


def build(dps, shards):
    total = dps * shards
    axes = ("dp", "shard")
    zgroups = [[i for i in range(dps) if i % 2 == p] for p in (0, 1)]

    def swap(values, dx, ds):
        pairs = [
            (i, ((i // shards) ^ dx) * shards + ((i % shards) ^ ds)) for i in range(total)
        ]
        return lax.ppermute(values, axes, pairs)

    def gather(piece):
        return lax.all_gather(piece, "dp", axis=0, tiled=True, axis_index_groups=zgroups)

    def scatter(whole):
        return lax.psum_scatter(
            whole, "dp", scatter_dimension=0, tiled=True, axis_index_groups=zgroups
        )


    def on_device(
        tokens,
        block_ids,
        cotangent,
        gain_first,
        w_query,
        w_key,
        w_value,
        w_output,
        gain_second,
        w_gate,
        w_up,
        w_down,
        moment_first,
        moment_query,
        moment_key,
        moment_value,
        moment_output,
        moment_second,
        moment_gate,
        moment_up,
        moment_down,
        step,
        rate,
    ):
        length = block_ids.shape[1]
        width = tokens.shape[1]
        group = H // KV
        dp = lax.axis_index("dp")
        me = lax.axis_index("shard")
        x = lax.rem(dp, 2)
        quarter = length // shards
        rows = w_query.shape[0]

        def half(values, which):
            size = values.shape[1] // 2
            return lax.dynamic_slice_in_dim(values, which * size, size, axis=1)

        def ordered(mine, theirs, axis=0):
            first = jnp.where(x == 0, mine, theirs)
            second = jnp.where(x == 0, theirs, mine)
            return jnp.concatenate([first, second], axis=axis)

        def natural(parts):
            stacked = jnp.stack(parts)
            return jnp.concatenate(
                [
                    lax.dynamic_index_in_dim(stacked, me ^ q, axis=0, keepdims=False)
                    for q in range(shards)
                ],
                axis=0,
            )

        def cut(values, ds):
            return lax.dynamic_slice_in_dim(values, (me ^ ds) * quarter, quarter, axis=0)

        def halves(own, other):
            return [
                jnp.stack([cut(own, dc), cut(own, dc + 2), cut(other, dc), cut(other, dc + 2)])
                for dc in (0, 1)
            ]

        def streams(mine, theirs):
            return [
                natural([mine[k], theirs[k], mine[k + 1], theirs[k + 1]]) for k in (0, 2)
            ]

        def flat(values):
            return values.reshape(-1, values.shape[-1])

        qc = group * HD
        cols = qc + 2 * HD
        gains = jnp.stack([gain_first, gain_second]).astype(BF)
        gains = jnp.pad(gains, ((0, 14), (0, cols + qc - rows)))
        piece = opening(w_query, w_key, w_value, w_output, gains)
        groups = dps // 2

        blocks_x = swap(block_ids, 1, 0)
        low_g = w_gate.astype(BF)
        low_u = w_up.astype(BF)
        low_d = w_down.astype(BF).T
        units = low_g.shape[1] // 2
        sizes = (units * 5 // 8, units * 3 // 8)
        offsets = (0, sizes[0])

        def ffn_part(which, j):
            return jnp.concatenate(
                [
                    lax.dynamic_slice_in_dim(low, which * units + offsets[j], sizes[j], axis=1)
                    for low in (low_g, low_u, low_d)
                ],
                axis=1,
            )

        both, first_part = entry(
            after(tokens, piece[:16, :128])[0], ffn_part(x, 0), ffn_part(1 - x, 0)
        )
        ffn_weights = [gather(first_part)]
        packed = gather(piece)
        packed = packed.reshape(groups, 2 * rows + 32, cols + qc)
        out_weight = packed[:, : 2 * rows, cols:].reshape(width, qc)
        tails = packed[:, 2 * rows :].reshape(groups, 2, 16, cols + qc)
        gain_one = tails[:, :, 0, :rows].reshape(1, width).astype(F32)
        gain_two = tails[:, :, 1, :rows].reshape(1, width).astype(F32)

        cosine, sine = rope_tables(length, group)

        normed, query, key, value, cot_near = qkv(
            both, gain_one, packed, cosine, sine, cotangent, group
        )
        blocks = jnp.concatenate([block_ids, blocks_x], axis=0)
        block_rows = blocks[:, None, :]
        block_cols = blocks.reshape(2 * length, 1)
        mixed, lse, cot_far, core_near, core_far, second_x = attend(
            query, key, value, block_rows, block_cols, cot_near, ffn_part(1 - x, 1), length
        )
        ffn_weights.append(gather(ordered(ffn_part(x, 1), second_x)))
        late, _ = after(cotangent, mixed[:16, :128])
        cot_own = [cut(late, ds) for ds in range(shards)]
        cot_mine = jnp.concatenate([cot_own[0], cot_own[2], cot_near, cot_far], axis=0)
        cot_theirs = jnp.concatenate([cot_own[1], cot_own[3], core_near, core_far], axis=0)
        mixed_own, mixed_other = mixed[:length], mixed[length:]
        mixed_mine, mixed_theirs = halves(mixed_own, mixed_other)

        def project(values, weight):
            partial = jnp.einsum("atk,dk->atd", values, weight, preferred_element_type=F32)
            return partial.astype(BF)

        tokens_own = cut(tokens, 0)
        mine, theirs, hidden = mid_stage(
            project(mixed_mine, out_weight),
            project(mixed_theirs, out_weight),
            tokens_own,
            gain_two,
        )
        two_mine, two_theirs = flat(mine), flat(theirs)

        shape = (4, quarter, width)
        acts_mine = []
        acts_theirs = []
        part_mine = part_theirs = None
        first_grads = None
        for j in range(CHUNKS):
            last = j == CHUNKS - 1
            weight = ffn_weights[j]
            theirs_in = two_theirs
            if first_grads is not None:
                theirs_in, first_grads = after(two_theirs, first_grads)
            act_theirs, gu_theirs, part_theirs = up_back(
                theirs_in, cot_theirs, weight, part_theirs, last
            )
            mine_in = two_mine
            if last:
                mine_in, part_theirs = after(two_mine, part_theirs)
            act_mine, gu_mine, part_mine = up_back(mine_in, cot_mine, weight, part_mine, last)
            acts_mine.append(act_mine)
            acts_theirs.append(act_theirs)

            if not last:
                first_grads = ffn_grads(
                    (two_mine, two_theirs),
                    (cot_mine, cot_theirs),
                    (gu_mine, gu_theirs),
                    (act_mine, act_theirs),
                )
        mine, theirs, grad_hidden, gain_grad_two, last_grads, out_mine, out_theirs = back_stage(
            part_mine.reshape(shape),
            part_theirs.reshape(shape),
            hidden,
            cut(cotangent, 0),
            gain_two,
            (two_mine, two_theirs, cot_mine, cot_theirs, gu_mine, gu_theirs),
            (acts_mine, acts_theirs),
            ffn_weights,
        )
        gh_mine = mine.reshape(shape)
        gh_theirs = theirs.reshape(shape)
        first_piece = scatter(first_grads)
        last_piece = scatter(last_grads)
        grad_mixed_mine = project(gh_mine, out_weight.T)
        grad_mixed_theirs = project(gh_theirs, out_weight.T)
        grad_mixed = streams(grad_mixed_mine, grad_mixed_theirs)
        grad_q, grad_kv, output = attend_back(
            query,
            key,
            value,
            block_rows,
            block_cols,
            lse,
            jnp.concatenate(grad_mixed, axis=0),
            cosine,
            sine,
            length,
            out_mine.reshape(shape),
            out_theirs.reshape(shape),
            hidden,
        )
        grad_qkv = jnp.concatenate([grad_q, grad_kv], axis=1)
        gq_mine, gq_theirs = halves(grad_qkv[:length], grad_qkv[length:])
        d_attn, even_in, odd_in, first_theirs = attn_grads(
            normed,
            grad_qkv,
            (flat(gh_mine), flat(gh_theirs)),
            (flat(mixed_mine), flat(mixed_theirs)),
            (flat(gq_mine), flat(gq_theirs)),
            packed,
            first_piece,
        )
        grad_attn = scatter(d_attn)
        input_grad, gain_grads, last_theirs = end_stage(
            even_in.reshape(shape),
            odd_in.reshape(shape),
            tokens_own,
            grad_hidden,
            gain_one,
            gain_grad_two,
            last_piece,
            dps,
            shards,
        )
        pairs = [(first_piece, first_theirs), (last_piece, last_theirs)]
        gain_rows = gain_grads.reshape(2, dps, rows).transpose(1, 0, 2)
        own_q, own_k, own_v, own_o, own_g, own_u, own_d, norm, own_first, own_second = finish(
            grad_attn, gain_rows, pairs, dps, shards, 2
        )
        global_norm = norm[0, 0]
        owned = (own_first, own_q, own_k, own_v, own_o, own_second, own_g, own_u, own_d)
        rate_now = rate * jnp.minimum(1.0, (step.astype(F32) + 1.0) / WARMUP)
        masters = (gain_first, w_query, w_key, w_value, w_output, gain_second, w_gate, w_up, w_down)
        moments = (
            moment_first,
            moment_query,
            moment_key,
            moment_value,
            moment_output,
            moment_second,
            moment_gate,
            moment_up,
            moment_down,
        )
        lists = [
            [v.reshape(1, -1) if v.ndim == 1 else v for v in values]
            for values in (masters, moments, owned)
        ]
        *parts, output, input_grad = update(norm, rate_now, output, input_grad, *lists)
        momenta, updated = (
            [v.reshape(-1) if v.shape[0] == 1 else v for v in values] for values in parts
        )
        return (output, input_grad, global_norm, *momenta, *updated)

    return on_device


def solution(mesh):
    rows, both, back = P("dp"), P("dp", "shard"), P("shard", "dp")
    tokens = P("dp", None)
    params = (rows, both, both, both, back, rows, both, both, back)
    in_specs = (tokens, tokens, tokens, *params, *params, P(), P())
    out_specs = (tokens, tokens, P(), *params, *params)
    return jax.shard_map(
        build(mesh.shape["dp"], mesh.shape["shard"]),
        mesh=mesh,
        in_specs=in_specs,
        out_specs=out_specs,
        check_vma=False,
    )
```
